32 devices in a mesh: section: 4 (over x, core), bulk: 8 (over z, y).
Axes of the slice: x: 2, y: 2, z: 4, core: 2. Of those that a mesh axis runs over, the one named last changes fastest.
Arguments:
- activations: bfloat16 [4, 4, 2048, 256], P('section', None, 'bulk'), may hold values from -6 to 6
- weights: bfloat16 [4, 3, 256, 256], P('section'), may hold values from -0.109375 to 0.109375
- film_gain: float32 [4, 36, 256], P('section'), may hold values from 0.25 to 1.75
- film_shift: float32 [4, 36, 256], P('section'), may hold values from -3 to 3
- doa_bins: int32 [4], replicated, may hold values from 0 to 35
- cotangent: bfloat16 [4, 2048, 256], P(None, 'bulk'), may hold values from -6 to 6
Outputs:
- d_inputs: bfloat16 [4, 4, 2048, 256], P('section', None, 'bulk')
- d_weights: float32 [4, 3, 256, 256], P('section')
- d_gain: float32 [4, 36, 256], P('section')
- d_shift: float32 [4, 36, 256], P('section')
The draws below stay inside these ranges and needn't reach their ends.
All inputs are finite; a program needn't handle non-finite values.
Results may differ from the reference program's by a relative error of at most 0.014.
Values may be sent and summed in bfloat16 or wider, within the bound.
No kernel may reach another device: no remote copies, remote signals or barrier semaphores. Data moves between devices by JAX's collectives and lax.ppermute only.
A program may use at most 64 MiB of HBM per device.

```python
import jax
import jax.numpy as jnp

C = 256
BINS = 36
MB = 4
PIX = 2048
SECTIONS = 4


def with_ends(values, rng, smallest, largest):
    longest = values.shape.index(max(values.shape))
    spots = []
    for shift in (0, 1):
        where = [jax.random.randint(jax.random.fold_in(rng, axis), (), 0, length) for axis, length in enumerate(values.shape)]
        where[longest] = (where[longest] + shift) % values.shape[longest]
        spots.append(tuple(where))
    return values.at[spots[0]].set(smallest).at[spots[1]].set(largest)


def block_scale(rng, dims, cuts, low, top_value):
    def one(axis_at, blocks):
        draws = jax.random.uniform(jax.random.fold_in(jax.random.fold_in(rng, 6), axis_at), (blocks,), jnp.float32, low / len(cuts), top_value / len(cuts))
        return jnp.repeat(jnp.exp(draws), dims[axis_at] // blocks).reshape((-1,) + (1,) * (len(dims) - axis_at - 1))

    gain = one(*cuts[0])
    for cut in cuts[1:]:
        gain = gain * one(*cut)
    return gain


def normal_values(key, dims, deviation, bound, cuts=(), held_as=jnp.bfloat16):
    loudness = block_scale(key, dims, cuts, -0.22, 0.18) if cuts else 1.0
    entries = jax.random.normal(key, dims, jnp.float32) * deviation * loudness
    return jnp.minimum(jnp.maximum(entries, -bound), bound).astype(held_as)


def setup_inputs(seed: int = 0) -> dict:
    arg_keys = jax.random.split(jax.random.key(seed), 7)
    return {
        "activations": normal_values(arg_keys[0], (SECTIONS, MB, PIX, C), 1.0, 6.0, ((0, 4), (2, 8))),
        "weights": normal_values(arg_keys[1], (SECTIONS, 3, C, C), (12 * C) ** -0.5, 0.109375, ((0, 4),)),
        "film_gain": jnp.clip(1.0 + 0.15 * jax.random.normal(arg_keys[2], (SECTIONS, BINS, C), jnp.float32), 0.25, 1.75),
        "film_shift": normal_values(arg_keys[3], (SECTIONS, BINS, C), 0.5, 3.0, ((0, 4),), jnp.float32),
        "doa_bins": with_ends(jax.random.randint(arg_keys[4], (MB,), 0, BINS), jax.random.fold_in(arg_keys[4], 1), 0, BINS - 1).astype(jnp.int32),
        "cotangent": normal_values(arg_keys[5], (MB, PIX, C), 1.0, 6.0, ((1, 8),)),
    }


def reference(activations, weights, film_gain, film_shift, doa_bins, cotangent):
    section_total = activations.shape[0]
    micro_count = activations.shape[1]
    channels = activations.shape[3]
    bins_count = film_gain.shape[1]
    grads = [cotangent[batch_no] for batch_no in range(micro_count)]
    section_inputs = [None] * section_total
    section_weights = [None] * section_total
    section_gains = [None] * section_total
    section_shifts = [None] * section_total
    for section_no in range(section_total - 1, -1, -1):
        w_set = weights[section_no]
        grad_w = jnp.zeros((3, channels, channels), jnp.float32)
        grad_gain = jnp.zeros((bins_count, channels), jnp.float32)
        grad_shift = jnp.zeros((bins_count, channels), jnp.float32)
        for batch_no in range(micro_count):
            act_now = activations[section_no, batch_no]
            before = jnp.roll(act_now, 1, 0)
            after = jnp.roll(act_now, -1, 0)
            pre_film = jnp.dot(before, w_set[0], preferred_element_type=jnp.float32)
            pre_film = pre_film + jnp.dot(act_now, w_set[1], preferred_element_type=jnp.float32)
            pre_film = pre_film + jnp.dot(after, w_set[2], preferred_element_type=jnp.float32)
            bin_id = doa_bins[batch_no]
            gain_row = film_gain[section_no, bin_id]
            shift_row = film_shift[section_no, bin_id]
            filmed = pre_film * gain_row + shift_row
            sigmoid_v = jax.nn.sigmoid(filmed)
            top_grad = grads[batch_no].astype(jnp.float32)
            grad_film = top_grad * sigmoid_v * (1.0 + filmed * (1.0 - sigmoid_v))
            grad_pre = (grad_film * gain_row).astype(jnp.bfloat16)
            back_prev = jnp.dot(grad_pre, w_set[0].T, preferred_element_type=jnp.float32)
            back_mid = jnp.dot(grad_pre, w_set[1].T, preferred_element_type=jnp.float32)
            back_next = jnp.dot(grad_pre, w_set[2].T, preferred_element_type=jnp.float32)
            grad_input = top_grad + jnp.roll(back_prev, -1, 0) + back_mid + jnp.roll(back_next, 1, 0)
            grads[batch_no] = grad_input.astype(jnp.bfloat16)
            grad_w = grad_w + jnp.stack([
                jnp.dot(before.T, grad_pre, preferred_element_type=jnp.float32),
                jnp.dot(act_now.T, grad_pre, preferred_element_type=jnp.float32),
                jnp.dot(after.T, grad_pre, preferred_element_type=jnp.float32)])
            grad_gain = grad_gain.at[bin_id].add(jnp.sum(grad_film * pre_film, 0))
            grad_shift = grad_shift.at[bin_id].add(jnp.sum(grad_film, 0))
        section_inputs[section_no] = jnp.stack(grads)
        section_weights[section_no] = grad_w
        section_gains[section_no] = grad_gain
        section_shifts[section_no] = grad_shift
    return (jnp.stack(section_inputs), jnp.stack(section_weights), jnp.stack(section_gains), jnp.stack(section_shifts))
```

```python
import functools

import jax
import jax.numpy as jnp
from jax import lax
from jax.experimental import pallas as pl
from jax.experimental.pallas import tpu as pltpu
from jax.sharding import PartitionSpec as P


F32 = jnp.float32
BF16 = jnp.bfloat16


def cost(flops, moved, trans=0):
    return pl.CostEstimate(flops=flops, bytes_accessed=moved, transcendentals=trans)


def shifted(value, amount):
    rows = value.shape[0]
    return pltpu.roll(value, amount % rows, 0)


def forward_kernel(
    bins, x_ref, cot_ref, low_ref, high_ref, w_ref, gain_ref, shift_ref, slope_ref, pre_ref, g_ref
):
    bin_id = bins[pl.program_id(0)]
    pad = low_ref.shape[2]
    rows = x_ref.shape[1]
    x_all = jnp.concatenate([low_ref[0, 0], x_ref[0], high_ref[0, 0]], axis=0)
    g_ref[0, :pad] = low_ref[1, 0]
    g_ref[0, pad : pad + rows] = cot_ref[0]
    g_ref[0, pad + rows :] = high_ref[1, 0]
    wide = x_all.astype(F32)
    pre = jnp.dot(shifted(wide, 1).astype(BF16), w_ref[0], preferred_element_type=F32)
    pre = pre + jnp.dot(x_all, w_ref[1], preferred_element_type=F32)
    pre = pre + jnp.dot(shifted(wide, -1).astype(BF16), w_ref[2], preferred_element_type=F32)
    filmed = pre * gain_ref[pl.ds(bin_id, 1), :] + shift_ref[pl.ds(bin_id, 1), :]
    sig = 0.5 * jnp.tanh(0.5 * filmed) + 0.5
    slope_ref[0] = sig * (1.0 + filmed * (1.0 - sig))
    pre_ref[0] = pre[pad : pad + rows]


def times_trans(left, right):
    return lax.dot_general(left, right, (((1,), (1,)), ((), ())), preferred_element_type=F32)


def trans_times(left, right):
    return lax.dot_general(left, right, (((0,), (0,)), ((), ())), preferred_element_type=F32)


def backward(g, slope, gain_row, w_ref):
    grad_film = g * slope
    grad_pre = (grad_film * gain_row).astype(BF16)
    wide = grad_pre.astype(F32)
    later = shifted(wide, -1).astype(BF16)
    earlier = shifted(wide, 1).astype(BF16)
    d_in = g + times_trans(later, w_ref[0]) + times_trans(grad_pre, w_ref[1])
    d_in = d_in + times_trans(earlier, w_ref[2])
    return grad_film, later, grad_pre, earlier, d_in.astype(BF16)


def relay_kernel(bins, active, g_ref, slope_ref, w_ref, gain_ref, d_ref):
    @pl.when(active[0] == 1)
    def _():
        gain_row = gain_ref[pl.ds(bins[pl.program_id(0)], 1), :]
        d_ref[0] = backward(g_ref[0].astype(F32), slope_ref[0], gain_row, w_ref)[-1]


def split_rows(rows):
    high = rows.astype(BF16)
    low = (rows - high.astype(F32)).astype(BF16)
    return jnp.concatenate([high.astype(F32), low.astype(F32)], axis=0).astype(BF16)


def joined_rows(pair):
    wide = pair.astype(F32)
    half = wide.shape[0] // 2
    return wide[:half] + wide[half:]


def last_kernel(sources, outer, *refs):
    bins, place = refs[:2]
    g_refs = refs[2 : 2 + sources]
    slope_ref, pre_ref, x_ref, w_ref, gain_ref = refs[2 + sources : 7 + sources]
    d_ref, own_ref = refs[7 + sources : 9 + sources]
    send_refs = refs[9 + sources : 9 + sources + outer - 1]
    g_now, total, sums = refs[9 + sources + outer - 1 :]
    step = pl.program_id(0)
    micro = pl.num_programs(0)
    rows, channels = x_ref.shape[1:]
    pad = (slope_ref.shape[1] - rows) // 2
    for index in range(sources):

        @pl.when(place[0] == index)
        def _(index=index):
            g_now[...] = g_refs[index][0]

    @pl.when(step == 0)
    def _():
        total[...] = jnp.zeros_like(total)

    gain_row = gain_ref[pl.ds(bins[step], 1), :]
    parts = backward(g_now[...].astype(F32), slope_ref[0], gain_row, w_ref)
    grad_film, d_in = parts[0], parts[4]
    inner = slice(pad, pad + rows)
    d_ref[0] = d_in[inner]
    x_now = x_ref[0]
    for tap in range(3):
        total[pl.ds(tap * channels, channels), :] += trans_times(x_now, parts[1 + tap][inner])
    film_main = grad_film[inner]
    half = sums.shape[0] // 2
    sums[pl.ds(step, 1), :] = jnp.sum(film_main * pre_ref[0], axis=0, keepdims=True)
    sums[pl.ds(half + step, 1), :] = jnp.sum(film_main, axis=0, keepdims=True)

    @pl.when(step == micro - 1)
    def _():
        chunk = own_ref.shape[0]
        own_ref[...] = total[pl.ds(place[1] * chunk, chunk), :]
        rows_out = split_rows(sums[...])
        for k in range(1, outer):
            start = pl.multiple_of((place[1] ^ k) * chunk, chunk)
            send_refs[k - 1][:chunk] = total[pl.ds(start, chunk), :].astype(BF16)
            send_refs[k - 1][chunk:] = rows_out


def gather_kernel(outer, place, own_ref, mine_ref, *refs):
    got_refs = refs[: outer - 1]
    out_ref, held = refs[outer - 1 :]
    chunk = own_ref.shape[0]
    acc = own_ref[...]
    for k in range(1, outer):
        acc = acc + got_refs[k - 1][:chunk].astype(F32)
    out_ref[:chunk] = acc.astype(BF16)
    held[place[1]] = joined_rows(mine_ref[chunk:])
    for k in range(1, outer):
        held[place[1] ^ k] = joined_rows(got_refs[k - 1][chunk:])
    rows = held[0]
    for index in range(1, outer):
        rows = rows + held[index]
    out_ref[chunk:] = split_rows(rows)


def pair_kernel(micro, bins, a_ref, b_ref, out_ref, gain_ref, shift_ref):
    chunk = out_ref.shape[0]
    out_ref[...] = (a_ref[:chunk].astype(F32) + b_ref[:chunk].astype(F32)).astype(BF16)
    rows = joined_rows(a_ref[chunk:]) + joined_rows(b_ref[chunk:])
    half = rows.shape[0] // 2
    gain_ref[...] = jnp.zeros_like(gain_ref)
    shift_ref[...] = jnp.zeros_like(shift_ref)
    for index in range(micro):
        where = pl.ds(bins[index], 1)
        gain_ref[where, :] += rows[index : index + 1]
        shift_ref[where, :] += rows[half + index : half + index + 1]


def spread_kernel(outer, place, *refs):
    out_ref = refs[outer]
    chunk = refs[0].shape[0]
    for k in range(outer):
        start = pl.multiple_of((place[1] ^ k) * chunk, chunk)
        out_ref[pl.ds(start, chunk), :] = refs[k][...].astype(F32)


def whole(shape):
    zeros = (0,) * len(shape)
    return pl.BlockSpec(shape, lambda *_: zeros)


def per_micro(shape):
    zeros = (0,) * len(shape)
    return pl.BlockSpec((1, *shape), lambda m, *_: (m, *zeros))


def shape_of(shape, dtype):
    return jax.ShapeDtypeStruct(shape, dtype)


def shards(activations, weights, film_gain, film_shift, doa_bins, cotangent):
    sections = lax.axis_size("section")
    section_id = lax.axis_index("section")
    bulk_count = lax.axis_size("bulk")
    outer = bulk_count // 2
    x = activations[0]
    w_set = weights[0]
    gain_table = film_gain[0]
    shift_table = film_shift[0]
    micro, rows, channels = x.shape
    bins_count = gain_table.shape[0]
    pad = 16 * -(-(sections + 1) // 16)
    wide = rows + 2 * pad
    place = jnp.stack(
        [sections - 1 - section_id, lax.axis_index("bulk") // 2]
    ).astype(jnp.int32)

    ring = [(i, (i + 1) % bulk_count) for i in range(bulk_count)]
    back = [(target, source) for source, target in ring]
    both = jnp.stack([x, cotangent])
    low = lax.ppermute(both[:, :, rows - pad :], "bulk", ring)
    high = lax.ppermute(both[:, :, :pad], "bulk", back)

    side = pl.BlockSpec((2, 1, pad, channels), lambda m, *_: (0, m, 0, 0))
    w_spec = whole((3, channels, channels))
    table = whole((bins_count, channels))
    matmul = 2 * 3 * micro * wide * channels * channels
    slope, pre, g_top = pl.pallas_call(
        forward_kernel,
        grid_spec=pltpu.PrefetchScalarGridSpec(
            num_scalar_prefetch=1,
            grid=(micro,),
            in_specs=[per_micro((rows, channels))] * 2 + [side] * 2 + [w_spec, table, table],
            out_specs=[
                per_micro((wide, channels)),
                per_micro((rows, channels)),
                per_micro((wide, channels)),
            ],
        ),
        out_shape=[
            shape_of((micro, wide, channels), F32),
            shape_of((micro, rows, channels), F32),
            shape_of((micro, wide, channels), BF16),
        ],
        cost_estimate=cost(matmul, 12 * micro * wide * channels, micro * wide * channels),
        name="forward",
    )(doa_bins, x, cotangent, low, high, w_set, gain_table, shift_table)

    sources = [g_top]
    for hop in range(sections - 1):
        upper = sections - 1 - hop
        active = (section_id == upper).astype(jnp.int32)[None]
        d_wide = pl.pallas_call(
            relay_kernel,
            grid_spec=pltpu.PrefetchScalarGridSpec(
                num_scalar_prefetch=2,
                grid=(micro,),
                in_specs=[per_micro((wide, channels))] * 2 + [w_spec, table],
                out_specs=per_micro((wide, channels)),
            ),
            out_shape=shape_of((micro, wide, channels), BF16),
            cost_estimate=cost(matmul, 8 * micro * wide * channels),
            name="relay",
        )(doa_bins, active, sources[hop], slope, w_set, gain_table)
        if upper % 2 and sections % 2 == 0:
            pairs = [(i, i ^ 1) for i in range(sections)]
        else:
            pairs = [(upper, upper - 1)]
        sources.append(lax.ppermute(d_wide, "section", pairs))

    chunk = 3 * channels // outer
    extra = 4 * micro
    message = shape_of((chunk + extra, channels), BF16)

    def source_spec(index):
        return pl.BlockSpec(
            (1, wide, channels),
            lambda m, _, place: (jnp.where(place[0] == index, m, 0), 0, 0),
        )

    made = pl.pallas_call(
        functools.partial(last_kernel, sections, outer),
        grid_spec=pltpu.PrefetchScalarGridSpec(
            num_scalar_prefetch=2,
            grid=(micro,),
            in_specs=[source_spec(index) for index in range(sections)]
            + [
                per_micro((wide, channels)),
                per_micro((rows, channels)),
                per_micro((rows, channels)),
                w_spec,
                table,
            ],
            out_specs=[per_micro((rows, channels)), whole((chunk, channels))]
            + [whole(message.shape)] * (outer - 1),
            scratch_shapes=[
                pltpu.VMEM((wide, channels), BF16),
                pltpu.VMEM((3 * channels, channels), F32),
                pltpu.VMEM((2 * micro, channels), F32),
            ],
        ),
        out_shape=[shape_of((micro, rows, channels), BF16), shape_of((chunk, channels), F32)]
        + [message] * (outer - 1),
        cost_estimate=cost(2 * matmul, 12 * micro * wide * channels),
        name="last",
    )(doa_bins, place, *sources, slope, pre, x, w_set, gain_table)
    d_local, own = made[:2]
    sends = made[2:]

    def across(value, k):
        pairs = [(i, i ^ (2 * k)) for i in range(bulk_count)]
        return lax.ppermute(value, "bulk", pairs)

    got = [across(sends[k - 1], k) for k in range(1, outer)]
    small = pltpu.VMEM((outer, 2 * micro, channels), F32)
    partial_sum = pl.pallas_call(
        functools.partial(gather_kernel, outer),
        grid_spec=pltpu.PrefetchScalarGridSpec(
            num_scalar_prefetch=1,
            grid=(1,),
            in_specs=[whole((chunk, channels))] + [whole(message.shape)] * outer,
            out_specs=whole(message.shape),
            scratch_shapes=[small],
        ),
        out_shape=message,
        cost_estimate=cost(1, 1),
        name="gathered",
    )(place, own, sends[0], *got)
    other = lax.ppermute(partial_sum, "bulk", [(i, i ^ 1) for i in range(bulk_count)])
    done, d_gain, d_shift = pl.pallas_call(
        functools.partial(pair_kernel, micro),
        grid_spec=pltpu.PrefetchScalarGridSpec(
            num_scalar_prefetch=1,
            grid=(1,),
            in_specs=[whole(message.shape)] * 2,
            out_specs=[whole((chunk, channels)), table, table],
        ),
        out_shape=[
            shape_of((chunk, channels), BF16),
            shape_of((bins_count, channels), F32),
            shape_of((bins_count, channels), F32),
        ],
        cost_estimate=cost(1, 1),
        name="paired",
    )(doa_bins, partial_sum, other)
    spread = [done] + [across(done, k) for k in range(1, outer)]
    d_weights = pl.pallas_call(
        functools.partial(spread_kernel, outer),
        grid_spec=pltpu.PrefetchScalarGridSpec(
            num_scalar_prefetch=1,
            grid=(1,),
            in_specs=[whole((chunk, channels))] * outer,
            out_specs=whole((3 * channels, channels)),
        ),
        out_shape=shape_of((3 * channels, channels), F32),
        cost_estimate=cost(1, 1),
        name="spread",
    )(place, *spread)
    d_weights = d_weights.reshape(3, channels, channels)
    return (d_local[None], d_weights[None], d_gain[None], d_shift[None])


def solution(mesh):
    return jax.shard_map(
        shards,
        mesh=mesh,
        in_specs=(
            P("section", None, "bulk", None),
            P("section", None, None, None),
            P("section", None, None),
            P("section", None, None),
            P(),
            P(None, "bulk", None),
        ),
        out_specs=(
            P("section", None, "bulk", None),
            P("section", None, None, None),
            P("section", None, None),
            P("section", None, None),
        ),
        check_vma=False,
    )
```

```python
import functools

import jax
import jax.numpy as jnp
from jax import lax
from jax.experimental import pallas as pl
from jax.experimental.pallas import tpu as pltpu
from jax.sharding import PartitionSpec as P


F32 = jnp.float32
BF16 = jnp.bfloat16


def cost(flops, moved, trans=0):
    return pl.CostEstimate(flops=flops, bytes_accessed=moved, transcendentals=trans)


def shifted(value, amount):
    rows = value.shape[0]
    return pltpu.roll(value, amount % rows, 0)


def forward_kernel(
    bins, x_ref, cot_ref, low_ref, high_ref, w_ref, gain_ref, shift_ref, slope_ref, pre_ref, g_ref
):
    micro, rows = x_ref.shape[:2]
    pad = low_ref.shape[2]
    for m in range(micro):
        x_all = jnp.concatenate([low_ref[0, m], x_ref[m], high_ref[0, m]], axis=0)
        g_ref[m, :pad] = low_ref[1, m]
        g_ref[m, pad : pad + rows] = cot_ref[m]
        g_ref[m, pad + rows :] = high_ref[1, m]
        wide = x_all.astype(F32)
        pre = jnp.dot(shifted(wide, 1).astype(BF16), w_ref[0], preferred_element_type=F32)
        pre = pre + jnp.dot(x_all, w_ref[1], preferred_element_type=F32)
        pre = pre + jnp.dot(shifted(wide, -1).astype(BF16), w_ref[2], preferred_element_type=F32)
        filmed = pre * gain_ref[bins[m]] + shift_ref[bins[m]]
        sig = 0.5 * jnp.tanh(0.5 * filmed) + 0.5
        slope_ref[m] = sig * (1.0 + filmed * (1.0 - sig))
        pre_ref[m] = pre[pad : pad + rows]


def times_trans(left, right):
    return lax.dot_general(left, right, (((1,), (1,)), ((), ())), preferred_element_type=F32)


def trans_times(left, right):
    return lax.dot_general(left, right, (((0,), (0,)), ((), ())), preferred_element_type=F32)


def backward(g, slope, gain_row, w_ref):
    grad_film = g * slope
    grad_pre = (grad_film * gain_row).astype(BF16)
    wide = grad_pre.astype(F32)
    later = shifted(wide, -1).astype(BF16)
    earlier = shifted(wide, 1).astype(BF16)
    d_in = g + times_trans(later, w_ref[0]) + times_trans(grad_pre, w_ref[1])
    d_in = d_in + times_trans(earlier, w_ref[2])
    return grad_film, later, grad_pre, earlier, d_in.astype(BF16)


def relay_kernel(upper, bins, g_ref, slope_ref, w_ref, gain_ref, d_ref):
    @pl.when(lax.axis_index("section") == upper)
    def _():
        for m in range(g_ref.shape[0]):
            g = g_ref[m].astype(F32)
            d_ref[m] = backward(g, slope_ref[m], gain_ref[bins[m]], w_ref)[-1]


def split_rows(rows):
    high = rows.astype(BF16).astype(F32)
    low = (rows - high).astype(BF16).astype(F32)
    return jnp.concatenate([high, low], axis=0).astype(BF16)


def joined_rows(pair):
    wide = pair.astype(F32)
    half = wide.shape[0] // 2
    return wide[:half] + wide[half:]


def last_kernel(sections, outer, *refs):
    bins = refs[0]
    g_refs = refs[1 : 1 + sections]
    slope_ref, pre_ref, x_ref, w_ref, gain_ref = refs[1 + sections : 6 + sections]
    d_ref, own_ref = refs[6 + sections : 8 + sections]
    send_refs = refs[8 + sections : 7 + sections + outer]
    g_now, total, sums = refs[7 + sections + outer :]
    micro, rows, channels = x_ref.shape
    pad = (slope_ref.shape[1] - rows) // 2
    inner = slice(pad, pad + rows)
    section_id = lax.axis_index("section")
    mine = lax.axis_index("bulk") // 2
    for index in range(sections):

        @pl.when(section_id == sections - 1 - index)
        def _(index=index):
            g_now[...] = g_refs[index][...]

    for m in range(micro):
        g = g_now[m].astype(F32)
        parts = backward(g, slope_ref[m], gain_ref[bins[m]], w_ref)
        d_ref[m] = parts[4][inner]
        for tap in range(3):
            where = slice(tap * channels, (tap + 1) * channels)
            term = trans_times(x_ref[m], parts[1 + tap][inner])
            total[where] = term if m == 0 else total[where] + term
        film_main = parts[0][inner]
        sums[m : m + 1] = jnp.sum(film_main * pre_ref[m], axis=0, keepdims=True)
        sums[micro + m : micro + m + 1] = jnp.sum(film_main, axis=0, keepdims=True)
    chunk = own_ref.shape[0]
    own_ref[...] = total[pl.ds(pl.multiple_of(mine * chunk, chunk), chunk), :]
    rows_out = split_rows(sums[...])
    for k in range(1, outer):
        start = pl.multiple_of((mine ^ k) * chunk, chunk)
        send_refs[k - 1][:chunk] = total[pl.ds(start, chunk), :].astype(BF16)
        send_refs[k - 1][chunk:] = rows_out


def gather_kernel(outer, own_ref, mine_ref, *refs):
    got_refs = refs[: outer - 1]
    out_ref, held = refs[outer - 1 :]
    mine = lax.axis_index("bulk") // 2
    chunk = own_ref.shape[0]
    acc = own_ref[...]
    for k in range(1, outer):
        acc = acc + got_refs[k - 1][:chunk].astype(F32)
    out_ref[:chunk] = acc.astype(BF16)
    held[mine] = joined_rows(mine_ref[chunk:])
    for k in range(1, outer):
        held[mine ^ k] = joined_rows(got_refs[k - 1][chunk:])
    rows = held[0]
    for index in range(1, outer):
        rows = rows + held[index]
    out_ref[chunk:] = split_rows(rows)


def pair_kernel(a_ref, b_ref, out_ref):
    chunk = out_ref.shape[0]
    out_ref[...] = (a_ref[:chunk].astype(F32) + b_ref[:chunk].astype(F32)).astype(BF16)


def spread_kernel(micro, outer, bins, a_ref, b_ref, *refs):
    out_ref, gain_ref, shift_ref = refs[outer:]
    chunk = refs[0].shape[0]
    mine = lax.axis_index("bulk") // 2
    for k in range(outer):
        start = pl.multiple_of((mine ^ k) * chunk, chunk)
        out_ref[pl.ds(start, chunk), :] = refs[k][...].astype(F32)
    rows = joined_rows(a_ref[chunk:]) + joined_rows(b_ref[chunk:])
    gain_ref[...] = jnp.zeros_like(gain_ref)
    shift_ref[...] = jnp.zeros_like(shift_ref)
    for m in range(micro):
        gain_ref[bins[m]] += rows[m : m + 1]
        shift_ref[bins[m]] += rows[micro + m : micro + m + 1]


def shape_of(shape, dtype):
    return jax.ShapeDtypeStruct(shape, dtype)


def call(kernel, name, outs, args, scalars=(), scratch=(), flops=1, limit=4):
    vmem = pl.BlockSpec(memory_space=pltpu.VMEM)
    smem = pl.BlockSpec(memory_space=pltpu.SMEM)
    several = isinstance(outs, (list, tuple))
    return pl.pallas_call(
        kernel,
        in_specs=[smem] * len(scalars) + [vmem] * len(args),
        out_specs=[vmem] * len(outs) if several else vmem,
        out_shape=outs,
        scratch_shapes=scratch,
        compiler_params=pltpu.CompilerParams(vmem_limit_bytes=limit << 20),
        cost_estimate=cost(flops, 1 << 20),
        name=name,
    )(*scalars, *args)


def shards(activations, weights, film_gain, film_shift, doa_bins, cotangent):
    sections = lax.axis_size("section")
    bulk_count = lax.axis_size("bulk")
    outer = bulk_count // 2
    x = activations[0]
    w_set = weights[0]
    micro, rows, channels = x.shape
    bins_count = film_gain.shape[1]
    gain_table = film_gain.reshape(bins_count, 1, channels)
    shift_table = film_shift.reshape(bins_count, 1, channels)
    pad = 16 * -(-(sections + 1) // 16)
    wide = rows + 2 * pad

    ring = [(i, (i + 1) % bulk_count) for i in range(bulk_count)]
    back = [(target, source) for source, target in ring]
    low = lax.ppermute(
        jnp.stack([x[:, rows - pad :], cotangent[:, rows - pad :]]), "bulk", ring
    )
    high = lax.ppermute(jnp.stack([x[:, :pad], cotangent[:, :pad]]), "bulk", back)

    matmul = 2 * 3 * micro * wide * channels * channels
    wide_shape = (micro, wide, channels)
    slope, pre, g_top = call(
        forward_kernel,
        "forward",
        [shape_of(wide_shape, F32), shape_of(x.shape, F32), shape_of(wide_shape, BF16)],
        [x, cotangent, low, high, w_set, gain_table, shift_table],
        scalars=[doa_bins],
        flops=matmul,
        limit=12,
    )

    sources = [g_top]
    for hop in range(sections - 1):
        upper = sections - 1 - hop
        d_wide = call(
            functools.partial(relay_kernel, upper),
            "relay",
            shape_of(wide_shape, BF16),
            [sources[hop], slope, w_set, gain_table],
            scalars=[doa_bins],
            flops=matmul,
            limit=8,
        )
        if upper % 2 and sections % 2 == 0:
            pairs = [(i, i ^ 1) for i in range(sections)]
        else:
            pairs = [(upper, upper - 1)]
        sources.append(lax.ppermute(d_wide, "section", pairs))

    chunk = 3 * channels // outer
    message = shape_of((chunk + 4 * micro, channels), BF16)
    made = call(
        functools.partial(last_kernel, sections, outer),
        "last",
        [shape_of(x.shape, BF16), shape_of((chunk, channels), F32)] + [message] * (outer - 1),
        [*sources, slope, pre, x, w_set, gain_table],
        scalars=[doa_bins],
        scratch=[
            pltpu.VMEM(wide_shape, BF16),
            pltpu.VMEM((3 * channels, channels), F32),
            pltpu.VMEM((2 * micro, channels), F32),
        ],
        flops=2 * matmul,
        limit=16,
    )
    d_local, own = made[:2]
    sends = made[2:]

    def across(value, k):
        pairs = [(i, i ^ (2 * k)) for i in range(bulk_count)]
        return lax.ppermute(value, "bulk", pairs)

    got = [across(sends[k - 1], k) for k in range(1, outer)]
    partial_sum = call(
        functools.partial(gather_kernel, outer),
        "gathered",
        message,
        [own, sends[0], *got],
        scratch=[pltpu.VMEM((outer, 2 * micro, channels), F32)],
    )
    other = lax.ppermute(partial_sum, "bulk", [(i, i ^ 1) for i in range(bulk_count)])
    done = call(pair_kernel, "paired", shape_of((chunk, channels), BF16), [partial_sum, other])
    spread = [done] + [across(done, k) for k in range(1, outer)]
    table = shape_of((bins_count, 1, channels), F32)
    d_weights, d_gain, d_shift = call(
        functools.partial(spread_kernel, micro, outer),
        "spread",
        [shape_of((3 * channels, channels), F32), table, table],
        [partial_sum, other, *spread],
        scalars=[doa_bins],
    )
    return (
        d_local[None],
        d_weights.reshape(1, 3, channels, channels),
        d_gain.reshape(1, bins_count, channels),
        d_shift.reshape(1, bins_count, channels),
    )


def solution(mesh):
    return jax.shard_map(
        shards,
        mesh=mesh,
        in_specs=(
            P("section", None, "bulk", None),
            P("section", None, None, None),
            P("section", None, None),
            P("section", None, None),
            P(),
            P(None, "bulk", None),
        ),
        out_specs=(
            P("section", None, "bulk", None),
            P("section", None, None, None),
            P("section", None, None),
            P("section", None, None),
        ),
        check_vma=False,
    )
```

```python
import functools

import jax
import jax.numpy as jnp
from jax import lax
from jax.experimental import pallas as pl
from jax.experimental.pallas import tpu as pltpu
from jax.sharding import PartitionSpec as P


F32 = jnp.float32
BF16 = jnp.bfloat16


def cost(flops, moved, trans=0):
    return pl.CostEstimate(flops=flops, bytes_accessed=moved, transcendentals=trans)


def shifted(value, amount):
    rows = value.shape[0]
    return pltpu.roll(value, amount % rows, 0)


def copies(pairs, sems):
    started = []
    for index, (source, target) in enumerate(pairs):
        copy = pltpu.make_async_copy(source, target, sems.at[index])
        copy.start()
        started.append(copy)
    return started


def edge_kernel(x_ref, cot_ref, near_ref, far_ref, sems):
    rows = x_ref.shape[1]
    pad = near_ref.shape[2]
    odd = lax.axis_index("bulk") % 2
    last = rows - pad
    near = pl.multiple_of((1 - odd) * last, pad)
    far = pl.multiple_of(odd * last, pad)
    pairs = []
    for index, ref in enumerate((x_ref, cot_ref)):
        pairs.append((ref.at[:, pl.ds(near, pad), :], near_ref.at[index]))
        pairs.append((ref.at[:, pl.ds(far, pad), :], far_ref.at[index]))
    for copy in copies(pairs, sems):
        copy.wait()


def slopes(filmed):
    sig = 0.5 * jnp.tanh(0.5 * filmed) + 0.5
    return sig * (1.0 + filmed * (1.0 - sig))


def taps(value, w_ref):
    wide = value.astype(F32)
    pre = jnp.dot(shifted(wide, 1).astype(BF16), w_ref[0], preferred_element_type=F32)
    pre = pre + jnp.dot(value, w_ref[1], preferred_element_type=F32)
    return pre + jnp.dot(shifted(wide, -1).astype(BF16), w_ref[2], preferred_element_type=F32)


def forward_kernel(bins, x_in, cot_in, w_in, gain_in, shift_in, *refs):
    x_ref, cot_ref, w_ref, gain_ref, shift_ref, slope_ref, pre_ref, sems = refs
    micro = x_ref.shape[0]
    pairs = [(w_in, w_ref), (x_in, x_ref)]
    for m in range(micro):
        pairs.append((gain_in.at[bins[m]], gain_ref.at[m]))
        pairs.append((shift_in.at[bins[m]], shift_ref.at[m]))
    started = copies(pairs + [(cot_in, cot_ref)], sems)
    for copy in started[:-1]:
        copy.wait()
    for m in range(micro):
        pre = taps(x_ref[m], w_ref)
        slope_ref[m] = slopes(pre * gain_ref[m] + shift_ref[m])
        pre_ref[m] = pre
    started[-1].wait()


def rim_kernel(near_ref, far_ref, x_ref, w_ref, gain_ref, shift_ref, *refs):
    slope_ref, pre_ref, g_ref, halo = refs
    micro, rows = x_ref.shape[:2]
    pad = near_ref.shape[2]
    odd = lax.axis_index("bulk") % 2

    @pl.when(odd == 1)
    def _():
        halo[0] = near_ref[...]
        halo[1] = far_ref[...]

    @pl.when(odd == 0)
    def _():
        halo[0] = far_ref[...]
        halo[1] = near_ref[...]

    parts = []
    for m in range(micro):
        parts += [halo[0, 0, m], x_ref[m, :pad], x_ref[m, rows - pad :], halo[1, 0, m]]
        g_ref[m, 0] = halo[0, 1, m]
        g_ref[m, 1] = halo[1, 1, m]
    pre = taps(jnp.concatenate(parts, axis=0), w_ref)
    for m in range(micro):
        for side in range(2):
            start = (2 * m + side) * 2 * pad
            here = pre[start : start + 2 * pad]
            pre_ref[m, side] = here
            slope_ref[m, side] = slopes(here * gain_ref[m] + shift_ref[m])


def with_rim(main, rim, m):
    pad = rim.shape[2] // 2
    rows = main.shape[1]
    parts = [rim[m, 0, : pad + 8], main[m, 8 : rows - 8], rim[m, 1, pad - 8 :]]
    return jnp.concatenate(parts, axis=0)


def times_trans(left, right):
    return lax.dot_general(left, right, (((1,), (1,)), ((), ())), preferred_element_type=F32)


def trans_times(left, right):
    return lax.dot_general(left, right, (((0,), (0,)), ((), ())), preferred_element_type=F32)


def backward(g, slope, gain_row, w_ref):
    grad_film = g * slope
    grad_pre = (grad_film * gain_row).astype(BF16)
    wide = grad_pre.astype(F32)
    later = shifted(wide, -1).astype(BF16)
    earlier = shifted(wide, 1).astype(BF16)
    d_in = g + times_trans(later, w_ref[0]) + times_trans(grad_pre, w_ref[1])
    d_in = d_in + times_trans(earlier, w_ref[2])
    return grad_film, later, grad_pre, earlier, d_in.astype(BF16)


def top_gradient(cot_ref, rim_ref, m):
    return jnp.concatenate([rim_ref[m, 0], cot_ref[m], rim_ref[m, 1]], axis=0)


def relay_kernel(upper, slope_ref, slope_rim, w_ref, gain_ref, *refs):
    g_refs, d_ref = refs[:-1], refs[-1]

    @pl.when(lax.axis_index("section") == upper)
    def _():
        for m in range(slope_ref.shape[0]):
            g = top_gradient(*g_refs, m) if len(g_refs) == 2 else g_refs[0][m]
            slope = with_rim(slope_ref, slope_rim, m)
            d_ref[m] = backward(g.astype(F32), slope, gain_ref[m], w_ref)[-1]


def split_rows(rows):
    high = rows.astype(BF16).astype(F32)
    low = (rows - high).astype(BF16).astype(F32)
    return jnp.concatenate([high, low], axis=0).astype(BF16)


def joined_rows(pair):
    wide = pair.astype(F32)
    half = wide.shape[0] // 2
    return wide[:half] + wide[half:]


def last_kernel(hops, outer, *refs):
    slope_ref, slope_rim, pre_ref, pre_rim, x_ref, w_ref, gain_ref = refs[:7]
    cot_ref, g_rim = refs[7:9]
    got_refs = refs[9 : 9 + hops]
    d_ref, own_ref = refs[9 + hops : 11 + hops]
    send_refs = refs[11 + hops : 10 + hops + outer]
    g_now, total, sums = refs[10 + hops + outer :]
    micro, rows, channels = x_ref.shape
    pad = g_rim.shape[2]
    inner = slice(pad, pad + rows)
    section_id = lax.axis_index("section")
    mine = lax.axis_index("bulk") // 2

    @pl.when(section_id == hops)
    def _():
        for m in range(micro):
            g_now[m] = top_gradient(cot_ref, g_rim, m)

    for index in range(hops):

        @pl.when(section_id == hops - 1 - index)
        def _(index=index):
            g_now[...] = got_refs[index][...]

    for m in range(micro):
        g = g_now[m].astype(F32)
        slope = with_rim(slope_ref, slope_rim, m)
        parts = backward(g, slope, gain_ref[m], w_ref)
        d_ref[m] = parts[4][inner]
        for tap in range(3):
            where = slice(tap * channels, (tap + 1) * channels)
            term = trans_times(x_ref[m], parts[1 + tap][inner])
            total[where] = term if m == 0 else total[where] + term
        film_main = parts[0][inner]
        pre = with_rim(pre_ref, pre_rim, m)[inner]
        sums[m : m + 1] = jnp.sum(film_main * pre, axis=0, keepdims=True)
        sums[micro + m : micro + m + 1] = jnp.sum(film_main, axis=0, keepdims=True)
    chunk = own_ref.shape[0]
    own_ref[...] = total[pl.ds(pl.multiple_of(mine * chunk, chunk), chunk), :]
    rows_out = split_rows(sums[...])
    for k in range(1, outer):
        start = pl.multiple_of((mine ^ k) * chunk, chunk)
        send_refs[k - 1][:chunk] = total[pl.ds(start, chunk), :].astype(BF16)
        send_refs[k - 1][chunk:] = rows_out


def gather_kernel(outer, own_ref, mine_ref, *refs):
    got_refs = refs[: outer - 1]
    out_ref, held = refs[outer - 1 :]
    mine = lax.axis_index("bulk") // 2
    chunk = own_ref.shape[0]
    acc = own_ref[...]
    for k in range(1, outer):
        acc = acc + got_refs[k - 1][:chunk].astype(F32)
    out_ref[:chunk] = acc.astype(BF16)
    held[mine] = joined_rows(mine_ref[chunk:])
    for k in range(1, outer):
        held[mine ^ k] = joined_rows(got_refs[k - 1][chunk:])
    rows = held[0]
    for index in range(1, outer):
        rows = rows + held[index]
    out_ref[chunk:] = split_rows(rows)


def pair_kernel(a_ref, b_ref, out_ref):
    chunk = out_ref.shape[0]
    out_ref[...] = (a_ref[:chunk].astype(F32) + b_ref[:chunk].astype(F32)).astype(BF16)


def spread_kernel(micro, outer, bins, a_ref, b_ref, *refs):
    out_ref, gain_ref, shift_ref = refs[outer:]
    chunk = refs[0].shape[0]
    mine = lax.axis_index("bulk") // 2
    for k in range(outer):
        start = pl.multiple_of((mine ^ k) * chunk, chunk)
        out_ref[pl.ds(start, chunk), :] = refs[k][...].astype(F32)
    rows = joined_rows(a_ref[chunk:]) + joined_rows(b_ref[chunk:])
    gain_ref[...] = jnp.zeros_like(gain_ref)
    shift_ref[...] = jnp.zeros_like(shift_ref)
    for m in range(micro):
        gain_ref[bins[m]] += rows[m : m + 1]
        shift_ref[bins[m]] += rows[micro + m : micro + m + 1]


def shape_of(shape, dtype):
    return jax.ShapeDtypeStruct(shape, dtype)


def call(kernel, name, outs, args, scalars=(), remote=(), scratch=(), flops=1, limit=4):
    vmem = pl.BlockSpec(memory_space=pltpu.VMEM)
    smem = pl.BlockSpec(memory_space=pltpu.SMEM)
    kept = pl.BlockSpec(memory_space=pltpu.HBM)
    several = isinstance(outs, (list, tuple))
    return pl.pallas_call(
        kernel,
        in_specs=[smem] * len(scalars) + [kept] * len(remote) + [vmem] * len(args),
        out_specs=[vmem] * len(outs) if several else vmem,
        out_shape=outs,
        scratch_shapes=scratch,
        compiler_params=pltpu.CompilerParams(vmem_limit_bytes=limit << 20),
        cost_estimate=cost(flops, 1 << 20),
        name=name,
    )(*scalars, *[pltpu.with_memory_space_constraint(v, pltpu.HBM) for v in remote], *args)


def shards(activations, weights, film_gain, film_shift, doa_bins, cotangent):
    sections = lax.axis_size("section")
    bulk_count = lax.axis_size("bulk")
    outer = bulk_count // 2
    x = activations[0]
    w_set = weights[0]
    micro, rows, channels = x.shape
    bins_count = film_gain.shape[1]
    gain_table = film_gain.reshape(bins_count, 1, channels)
    shift_table = film_shift.reshape(bins_count, 1, channels)
    pad = 16 * -(-(sections + 1) // 16)
    wide = rows + 2 * pad

    edges = shape_of((2, micro, pad, channels), BF16)
    near, far = call(
        edge_kernel,
        "edges",
        [edges, edges],
        [],
        remote=[x, cotangent],
        scratch=[pltpu.SemaphoreType.DMA((4,))],
    )
    opposite = [(i, (i + 1 if i % 2 else i - 1) % bulk_count) for i in range(bulk_count)]
    far = lax.ppermute(far, "bulk", opposite)
    near = lax.ppermute(near, "bulk", [(i, i ^ 1) for i in range(bulk_count)])

    matmul = 2 * 3 * micro * wide * channels * channels
    wide_shape = (micro, wide, channels)
    rim_shape = (micro, 2, 2 * pad, channels)
    picked = shape_of((micro, 1, channels), F32)
    x, cot, w_set, gain_rows, shift_rows, slope, pre = call(
        forward_kernel,
        "forward",
        [shape_of(v.shape, v.dtype) for v in (x, cotangent, w_set)]
        + [picked, picked, shape_of(x.shape, F32), shape_of(x.shape, F32)],
        [],
        scalars=[doa_bins],
        remote=[x, cotangent, w_set, gain_table, shift_table],
        scratch=[pltpu.SemaphoreType.DMA((3 + 2 * micro,))],
        flops=matmul,
        limit=12,
    )
    slope_rim, pre_rim, g_rim = call(
        rim_kernel,
        "rim",
        [
            shape_of(rim_shape, F32),
            shape_of(rim_shape, F32),
            shape_of((micro, 2, pad, channels), BF16),
        ],
        [near, far, x, w_set, gain_rows, shift_rows],
        scratch=[pltpu.VMEM((2, 2, micro, pad, channels), BF16)],
        flops=matmul // 4,
        limit=8,
    )

    sources = []
    for hop in range(sections - 1):
        upper = sections - 1 - hop
        d_wide = call(
            functools.partial(relay_kernel, upper),
            "relay",
            shape_of(wide_shape, BF16),
            [slope, slope_rim, w_set, gain_rows] + (sources[-1:] if hop else [cot, g_rim]),
            flops=matmul,
            limit=8,
        )
        if upper % 2 and sections % 2 == 0:
            pairs = [(i, i ^ 1) for i in range(sections)]
        else:
            pairs = [(upper, upper - 1)]
        sources.append(lax.ppermute(d_wide, "section", pairs))

    chunk = 3 * channels // outer
    message = shape_of((chunk + 4 * micro, channels), BF16)
    made = call(
        functools.partial(last_kernel, sections - 1, outer),
        "last",
        [shape_of(x.shape, BF16), shape_of((chunk, channels), F32)] + [message] * (outer - 1),
        [slope, slope_rim, pre, pre_rim, x, w_set, gain_rows, cot, g_rim, *sources],
        scratch=[
            pltpu.VMEM(wide_shape, BF16),
            pltpu.VMEM((3 * channels, channels), F32),
            pltpu.VMEM((2 * micro, channels), F32),
        ],
        flops=2 * matmul,
        limit=16,
    )
    d_local, own = made[:2]
    sends = made[2:]

    def across(value, k):
        pairs = [(i, i ^ (2 * k)) for i in range(bulk_count)]
        return lax.ppermute(value, "bulk", pairs)

    got = [across(sends[k - 1], k) for k in range(1, outer)]
    partial_sum = call(
        functools.partial(gather_kernel, outer),
        "gathered",
        message,
        [own, sends[0], *got],
        scratch=[pltpu.VMEM((outer, 2 * micro, channels), F32)],
    )
    other = lax.ppermute(partial_sum, "bulk", [(i, i ^ 1) for i in range(bulk_count)])
    done = call(pair_kernel, "paired", shape_of((chunk, channels), BF16), [partial_sum, other])
    spread = [done] + [across(done, k) for k in range(1, outer)]
    table = shape_of((bins_count, 1, channels), F32)
    d_weights, d_gain, d_shift = call(
        functools.partial(spread_kernel, micro, outer),
        "spread",
        [shape_of((3 * channels, channels), F32), table, table],
        [partial_sum, other, *spread],
        scalars=[doa_bins],
    )
    return (
        d_local[None],
        d_weights.reshape(1, 3, channels, channels),
        d_gain.reshape(1, bins_count, channels),
        d_shift.reshape(1, bins_count, channels),
    )


def solution(mesh):
    return jax.shard_map(
        shards,
        mesh=mesh,
        in_specs=(
            P("section", None, "bulk", None),
            P("section", None, None, None),
            P("section", None, None),
            P("section", None, None),
            P(),
            P(None, "bulk", None),
        ),
        out_specs=(
            P("section", None, "bulk", None),
            P("section", None, None, None),
            P("section", None, None),
            P("section", None, None),
        ),
        check_vma=False,
    )
```

```python
import functools

import jax
import jax.numpy as jnp
from jax import lax
from jax.experimental import pallas as pl
from jax.experimental.pallas import tpu as pltpu
from jax.sharding import PartitionSpec as P


F32 = jnp.float32
BF16 = jnp.bfloat16
PARTS = 2


def cost(flops, moved, trans=0):
    return pl.CostEstimate(flops=flops, bytes_accessed=moved, transcendentals=trans)


def shifted(value, amount):
    rows = value.shape[0]
    return pltpu.roll(value, amount % rows, 0)


def copies(pairs, sems):
    started = []
    for index, (source, target) in enumerate(pairs):
        copy = pltpu.make_async_copy(source, target, sems.at[index])
        copy.start()
        started.append(copy)
    return started


def edge_kernel(x_ref, cot_ref, near_ref, far_ref, sems):
    rows = x_ref.shape[1]
    pad = near_ref.shape[2]
    odd = lax.axis_index("bulk") % 2
    last = rows - pad
    near = pl.multiple_of((1 - odd) * last, pad)
    far = pl.multiple_of(odd * last, pad)
    pairs = []
    for index, ref in enumerate((x_ref, cot_ref)):
        pairs.append((ref.at[:, pl.ds(near, pad), :], near_ref.at[index]))
        pairs.append((ref.at[:, pl.ds(far, pad), :], far_ref.at[index]))
    for copy in copies(pairs, sems):
        copy.wait()


def slopes(filmed):
    sig = 0.5 * jnp.tanh(0.5 * filmed) + 0.5
    return sig * (1.0 + filmed * (1.0 - sig))


def taps(value, w_ref):
    wide = value.astype(F32)
    pre = jnp.dot(shifted(wide, 1).astype(BF16), w_ref[0], preferred_element_type=F32)
    pre = pre + jnp.dot(value, w_ref[1], preferred_element_type=F32)
    return pre + jnp.dot(shifted(wide, -1).astype(BF16), w_ref[2], preferred_element_type=F32)


def forward_kernel(bins, x_in, cot_in, w_in, gain_in, shift_in, *refs):
    x_ref, cot_ref, w_ref, gain_ref, shift_ref, slope_ref, pre_ref, sems = refs
    micro = x_ref.shape[0]
    pairs = [(w_in, w_ref), (x_in, x_ref)]
    for m in range(micro):
        pairs.append((gain_in.at[bins[m]], gain_ref.at[m]))
        pairs.append((shift_in.at[bins[m]], shift_ref.at[m]))
    started = copies(pairs + [(cot_in, cot_ref)], sems)
    for copy in started[:-1]:
        copy.wait()
    for m in range(micro):
        pre = taps(x_ref[m], w_ref)
        slope_ref[m] = slopes(pre * gain_ref[m] + shift_ref[m])
        pre_ref[m] = pre
    started[-1].wait()


def rim_kernel(near_ref, far_ref, x_ref, w_ref, gain_ref, shift_ref, *refs):
    slope_ref, pre_ref, g_ref, halo = refs
    micro, rows = x_ref.shape[:2]
    pad = near_ref.shape[2]
    odd = lax.axis_index("bulk") % 2

    @pl.when(odd == 1)
    def _():
        halo[0] = near_ref[...]
        halo[1] = far_ref[...]

    @pl.when(odd == 0)
    def _():
        halo[0] = far_ref[...]
        halo[1] = near_ref[...]

    parts = []
    for m in range(micro):
        parts += [halo[0, 0, m], x_ref[m, :pad], x_ref[m, rows - pad :], halo[1, 0, m]]
        g_ref[m, 0] = halo[0, 1, m]
        g_ref[m, 1] = halo[1, 1, m]
    pre = taps(jnp.concatenate(parts, axis=0), w_ref)
    for m in range(micro):
        for side in range(2):
            start = (2 * m + side) * 2 * pad
            here = pre[start : start + 2 * pad]
            pre_ref[m, side] = here
            slope_ref[m, side] = slopes(here * gain_ref[m] + shift_ref[m])


def with_rim(main, rim, m):
    pad = rim.shape[2] // 2
    rows = main.shape[1]
    parts = [rim[m, 0, : pad + 8], main[m, 8 : rows - 8], rim[m, 1, pad - 8 :]]
    return jnp.concatenate(parts, axis=0)


def times_trans(left, right):
    return lax.dot_general(left, right, (((1,), (1,)), ((), ())), preferred_element_type=F32)


def trans_times(left, right):
    return lax.dot_general(left, right, (((0,), (0,)), ((), ())), preferred_element_type=F32)


def backward(g, slope, gain_row, w_ref):
    grad_film = g * slope
    grad_pre = (grad_film * gain_row).astype(BF16)
    wide = grad_pre.astype(F32)
    later = shifted(wide, -1).astype(BF16)
    earlier = shifted(wide, 1).astype(BF16)
    d_in = g + times_trans(later, w_ref[0]) + times_trans(grad_pre, w_ref[1])
    d_in = d_in + times_trans(earlier, w_ref[2])
    return grad_film, later, grad_pre, earlier, d_in.astype(BF16)


def top_gradient(cot_ref, rim_ref, m):
    return jnp.concatenate([rim_ref[m, 0], cot_ref[m], rim_ref[m, 1]], axis=0)


def relay_kernel(upper, slope_ref, slope_rim, w_ref, gain_ref, *refs):
    g_refs, d_ref = refs[:-1], refs[-1]

    @pl.when(lax.axis_index("section") == upper)
    def _():
        for m in range(slope_ref.shape[0]):
            g = top_gradient(*g_refs, m) if len(g_refs) == 2 else g_refs[0][m]
            slope = with_rim(slope_ref, slope_rim, m)
            d_ref[m] = backward(g.astype(F32), slope, gain_ref[m], w_ref)[-1]


def split_rows(rows):
    high = rows.astype(BF16).astype(F32)
    low = (rows - high).astype(BF16).astype(F32)
    return jnp.concatenate([high, low], axis=0).astype(BF16)


def joined_rows(pair):
    wide = pair.astype(F32)
    half = wide.shape[0] // 2
    return wide[:half] + wide[half:]


def last_kernel(hops, outer, *refs):
    slope_ref, slope_rim, pre_ref, pre_rim, x_ref, w_ref, gain_ref = refs[:7]
    cot_ref, g_rim = refs[7:9]
    got_refs = refs[9 : 9 + hops]
    d_ref = refs[9 + hops]
    own_refs = refs[10 + hops : 10 + hops + PARTS]
    send_refs = refs[10 + hops + PARTS : -3]
    g_now, total, sums = refs[-3:]
    micro, rows, channels = x_ref.shape
    pad = g_rim.shape[2]
    inner = slice(pad, pad + rows)
    section_id = lax.axis_index("section")
    mine = lax.axis_index("bulk") // 2

    @pl.when(section_id == hops)
    def _():
        for m in range(micro):
            g_now[m] = top_gradient(cot_ref, g_rim, m)

    for index in range(hops):

        @pl.when(section_id == hops - 1 - index)
        def _(index=index):
            g_now[...] = got_refs[index][...]

    for m in range(micro):
        g = g_now[m].astype(F32)
        slope = with_rim(slope_ref, slope_rim, m)
        parts = backward(g, slope, gain_ref[m], w_ref)
        d_ref[m] = parts[4][inner]
        for tap in range(3):
            where = slice(tap * channels, (tap + 1) * channels)
            term = trans_times(x_ref[m], parts[1 + tap][inner])
            total[where] = term if m == 0 else total[where] + term
        film_main = parts[0][inner]
        pre = with_rim(pre_ref, pre_rim, m)[inner]
        sums[m : m + 1] = jnp.sum(film_main * pre, axis=0, keepdims=True)
        sums[micro + m : micro + m + 1] = jnp.sum(film_main, axis=0, keepdims=True)
    rows_out = split_rows(sums[...])
    extra = rows_out.shape[0]
    chunk = own_refs[0].shape[0]
    parts_count = len(own_refs)
    for part in range(parts_count):
        for k in range(outer):
            start = pl.multiple_of(((mine ^ k) * parts_count + part) * chunk, 8)
            term = total[pl.ds(start, chunk), :]
            if k == 0:
                own_refs[part][...] = term
            else:
                ref = send_refs[part * (outer - 1) + k - 1]
                ref[ref.shape[0] - chunk :] = term.astype(BF16)
                if part == 0:
                    ref[:extra] = rows_out


def gather_kernel(outer, own_ref, mine_ref, *refs):
    got_refs = refs[: outer - 1]
    out_ref, held = refs[outer - 1 :]
    mine = lax.axis_index("bulk") // 2
    chunk = own_ref.shape[0]
    extra = out_ref.shape[0] - chunk
    acc = own_ref[...]
    for k in range(1, outer):
        acc = acc + got_refs[k - 1][extra:].astype(F32)
    out_ref[extra:] = acc.astype(BF16)
    if extra:
        held[mine] = joined_rows(mine_ref[:extra])
        for k in range(1, outer):
            held[mine ^ k] = joined_rows(got_refs[k - 1][:extra])
        rows = held[0]
        for index in range(1, outer):
            rows = rows + held[index]
        out_ref[:extra] = split_rows(rows)


def pair_kernel(a_ref, b_ref, *refs):
    out_ref = refs[-1]
    extra = a_ref.shape[0] - out_ref.shape[0]
    out_ref[...] = (a_ref[extra:].astype(F32) + b_ref[extra:].astype(F32)).astype(BF16)


def spread_kernel(micro, outer, bins, a_ref, b_ref, *refs):
    chunk_refs = refs[:-3]
    out_ref, gain_ref, shift_ref = refs[-3:]
    chunk = chunk_refs[0].shape[0]
    parts_count = len(chunk_refs) // outer
    mine = lax.axis_index("bulk") // 2
    for part in range(parts_count):
        for k in range(outer):
            start = pl.multiple_of(((mine ^ k) * parts_count + part) * chunk, 8)
            out_ref[pl.ds(start, chunk), :] = chunk_refs[part * outer + k][...].astype(F32)
    extra = 4 * micro
    rows = joined_rows(a_ref[:extra]) + joined_rows(b_ref[:extra])
    gain_ref[...] = jnp.zeros_like(gain_ref)
    shift_ref[...] = jnp.zeros_like(shift_ref)
    for m in range(micro):
        gain_ref[bins[m]] += rows[m : m + 1]
        shift_ref[bins[m]] += rows[micro + m : micro + m + 1]


def shape_of(shape, dtype):
    return jax.ShapeDtypeStruct(shape, dtype)


def call(kernel, outs, args, scalars=(), remote=(), scratch=(), flops=1, limit=4):
    vmem = pl.BlockSpec(memory_space=pltpu.VMEM)
    smem = pl.BlockSpec(memory_space=pltpu.SMEM)
    kept = pl.BlockSpec(memory_space=pltpu.HBM)
    several = isinstance(outs, (list, tuple))
    return pl.pallas_call(
        kernel,
        in_specs=[smem] * len(scalars) + [kept] * len(remote) + [vmem] * len(args),
        out_specs=[vmem] * len(outs) if several else vmem,
        out_shape=outs,
        scratch_shapes=scratch,
        compiler_params=pltpu.CompilerParams(vmem_limit_bytes=limit << 20),
        cost_estimate=cost(flops, 1 << 20),
    )(*scalars, *[pltpu.with_memory_space_constraint(v, pltpu.HBM) for v in remote], *args)


def step(activations, weights, film_gain, film_shift, doa_bins, cotangent):
    sections = lax.axis_size("section")
    bulk_count = lax.axis_size("bulk")
    outer = bulk_count // 2
    x = activations[0]
    w_set = weights[0]
    micro, rows, channels = x.shape
    bins_count = film_gain.shape[1]
    gain_table = film_gain.reshape(bins_count, 1, channels)
    shift_table = film_shift.reshape(bins_count, 1, channels)
    pad = 16 * -(-(sections + 1) // 16)
    wide = rows + 2 * pad

    edges = shape_of((2, micro, pad, channels), BF16)
    near, far = call(
        edge_kernel,
        [edges, edges],
        [],
        remote=[x, cotangent],
        scratch=[pltpu.SemaphoreType.DMA((4,))],
    )
    opposite = [(i, (i + 1 if i % 2 else i - 1) % bulk_count) for i in range(bulk_count)]
    far = lax.ppermute(far, "bulk", opposite)
    near = lax.ppermute(near, "bulk", [(i, i ^ 1) for i in range(bulk_count)])

    matmul = 2 * 3 * micro * wide * channels * channels
    wide_shape = (micro, wide, channels)
    rim_shape = (micro, 2, 2 * pad, channels)
    picked = shape_of((micro, 1, channels), F32)
    x, cot, w_set, gain_rows, shift_rows, slope, pre = call(
        forward_kernel,
        [shape_of(v.shape, v.dtype) for v in (x, cotangent, w_set)]
        + [picked, picked, shape_of(x.shape, F32), shape_of(x.shape, F32)],
        [],
        scalars=[doa_bins],
        remote=[x, cotangent, w_set, gain_table, shift_table],
        scratch=[pltpu.SemaphoreType.DMA((3 + 2 * micro,))],
        flops=matmul,
        limit=12,
    )
    slope_rim, pre_rim, g_rim = call(
        rim_kernel,
        [
            shape_of(rim_shape, F32),
            shape_of(rim_shape, F32),
            shape_of((micro, 2, pad, channels), BF16),
        ],
        [near, far, x, w_set, gain_rows, shift_rows],
        scratch=[pltpu.VMEM((2, 2, micro, pad, channels), BF16)],
        flops=matmul // 4,
        limit=8,
    )

    sources = []
    for hop in range(sections - 1):
        upper = sections - 1 - hop
        d_wide = call(
            functools.partial(relay_kernel, upper),
            shape_of(wide_shape, BF16),
            [slope, slope_rim, w_set, gain_rows] + (sources[-1:] if hop else [cot, g_rim]),
            flops=matmul,
            limit=8,
        )
        if upper % 2 and sections % 2 == 0:
            pairs = [(i, i ^ 1) for i in range(sections)]
        else:
            pairs = [(upper, upper - 1)]
        sources.append(lax.ppermute(d_wide, "section", pairs))

    chunk = 3 * channels // outer // PARTS
    extra = 4 * micro
    messages = [shape_of((chunk + (0 if part else extra), channels), BF16) for part in range(PARTS)]
    made = call(
        functools.partial(last_kernel, sections - 1, outer),
        [shape_of(x.shape, BF16)]
        + [shape_of((chunk, channels), F32)] * PARTS
        + [messages[part] for part in range(PARTS) for _ in range(outer - 1)],
        [slope, slope_rim, pre, pre_rim, x, w_set, gain_rows, cot, g_rim, *sources],
        scratch=[
            pltpu.VMEM(wide_shape, BF16),
            pltpu.VMEM((3 * channels, channels), F32),
            pltpu.VMEM((2 * micro, channels), F32),
        ],
        flops=2 * matmul,
        limit=16,
    )
    d_local = made[0]
    owns = made[1 : 1 + PARTS]

    def across(value, k):
        pairs = [(i, i ^ (2 * k)) for i in range(bulk_count)]
        return lax.ppermute(value, "bulk", pairs)

    swap = [(i, i ^ 1) for i in range(bulk_count)]
    order = [k for k in range(2, outer)] + [1]
    scattered = []
    for part in range(PARTS):
        sends = made[1 + PARTS + part * (outer - 1) :][: outer - 1]
        got = {k: across(sends[k - 1], k) for k in order}
        scattered.append((sends[0], got))
    summed = []
    for part in range(PARTS):
        first, got = scattered[part]
        partial_sum = call(
            functools.partial(gather_kernel, outer),
            messages[part],
            [owns[part], first] + [got[k] for k in range(1, outer)],
            scratch=[pltpu.VMEM((outer, 2 * micro, channels), F32)],
        )
        summed.append((partial_sum, lax.ppermute(partial_sum, "bulk", swap)))
    spread = []
    for part in range(PARTS):
        done = call(
            pair_kernel, shape_of((chunk, channels), BF16), list(summed[part]) + spread[-outer:][:1]
        )
        got = {k: across(done, k) for k in order}
        spread += [done] + [got[k] for k in range(1, outer)]
    table = shape_of((bins_count, 1, channels), F32)
    d_weights, d_gain, d_shift = call(
        functools.partial(spread_kernel, micro, outer),
        [shape_of((3 * channels, channels), F32), table, table],
        [*summed[0], *spread],
        scalars=[doa_bins],
    )
    return (
        d_local[None],
        d_weights.reshape(1, 3, channels, channels),
        d_gain.reshape(1, bins_count, channels),
        d_shift.reshape(1, bins_count, channels),
    )


def solution(mesh):
    return jax.shard_map(
        step,
        mesh=mesh,
        in_specs=(
            P("section", None, "bulk", None),
            P("section", None, None, None),
            P("section", None, None),
            P("section", None, None),
            P(),
            P(None, "bulk", None),
        ),
        out_specs=(
            P("section", None, "bulk", None),
            P("section", None, None, None),
            P("section", None, None),
            P("section", None, None),
        ),
        check_vma=False,
    )
```

```python
import functools

import jax
import jax.numpy as jnp
from jax import lax
from jax.experimental import pallas as pl
from jax.experimental.pallas import tpu as pltpu
from jax.sharding import PartitionSpec as P


F32 = jnp.float32
BF16 = jnp.bfloat16
PARTS = 2


def cost(flops, moved, trans=0):
    return pl.CostEstimate(flops=flops, bytes_accessed=moved, transcendentals=trans)


def shifted(value, amount):
    rows = value.shape[0]
    return pltpu.roll(value, amount % rows, 0)


def copies(pairs, sems):
    started = []
    for index, (source, target) in enumerate(pairs):
        copy = pltpu.make_async_copy(source, target, sems.at[index])
        copy.start()
        started.append(copy)
    return started


def edge_kernel(x_ref, cot_ref, near_ref, far_ref, sems):
    rows = x_ref.shape[1]
    pad = near_ref.shape[2]
    odd = lax.axis_index("bulk") % 2
    last = rows - pad
    near = pl.multiple_of((1 - odd) * last, pad)
    far = pl.multiple_of(odd * last, pad)
    pairs = []
    for index, ref in enumerate((x_ref, cot_ref)):
        pairs.append((ref.at[:, pl.ds(near, pad), :], near_ref.at[index]))
        pairs.append((ref.at[:, pl.ds(far, pad), :], far_ref.at[index]))
    for copy in copies(pairs, sems):
        copy.wait()


def slopes(filmed):
    sig = 0.5 * jnp.tanh(0.5 * filmed) + 0.5
    return sig * (1.0 + filmed * (1.0 - sig))


def taps(value, w_ref):
    wide = value.astype(F32)
    pre = jnp.dot(shifted(wide, 1).astype(BF16), w_ref[0], preferred_element_type=F32)
    pre = pre + jnp.dot(value, w_ref[1], preferred_element_type=F32)
    return pre + jnp.dot(shifted(wide, -1).astype(BF16), w_ref[2], preferred_element_type=F32)


def turn(half, micro, place):
    start = half if place == 0 else 1 - half
    return [start * (micro // 2) + j for j in range(micro // 2)]


def forward_kernel(bins, x_in, cot_in, w_in, gain_in, shift_in, *refs):
    x_ref, cot_ref, w_ref, gain_ref, shift_ref, keep_ref, send_ref, pre_ref, sems = refs
    micro = x_ref.shape[0]
    half = lax.axis_index("section") % 2
    pairs = [(w_in, w_ref), (x_in, x_ref)]
    for m in range(micro):
        pairs.append((gain_in.at[bins[m]], gain_ref.at[m]))
        pairs.append((shift_in.at[bins[m]], shift_ref.at[m]))
    mine = cot_in.at[pl.ds(half * (micro // 2), micro // 2)]
    started = copies(pairs + [(mine, cot_ref)], sems)
    for copy in started[:-1]:
        copy.wait()
    for place, out in enumerate((keep_ref, send_ref)):
        for j, m in enumerate(turn(half, micro, place)):
            pre = taps(x_ref[m], w_ref)
            out[j] = slopes(pre * gain_ref[m] + shift_ref[m]) * gain_ref[m]
            pre_ref[m] = pre
    started[-1].wait()


def rim_kernel(near_ref, far_ref, x_ref, w_ref, gain_ref, shift_ref, *refs):
    keep_ref, send_ref, pre_ref, g_ref, halo = refs
    micro, rows = x_ref.shape[:2]
    pad = near_ref.shape[2]
    odd = lax.axis_index("bulk") % 2
    half = lax.axis_index("section") % 2

    @pl.when(odd == 1)
    def _():
        halo[0] = near_ref[...]
        halo[1] = far_ref[...]

    @pl.when(odd == 0)
    def _():
        halo[0] = far_ref[...]
        halo[1] = near_ref[...]

    parts = []
    order = turn(half, micro, 0) + turn(half, micro, 1)
    for m in order:
        parts += [halo[0, 0, m], x_ref[m, :pad], x_ref[m, rows - pad :], halo[1, 0, m]]
    for j, m in enumerate(turn(half, micro, 0)):
        g_ref[j, 0] = halo[0, 1, m]
        g_ref[j, 1] = halo[1, 1, m]
    pre = taps(jnp.concatenate(parts, axis=0), w_ref)
    for index, m in enumerate(order):
        out = (keep_ref, send_ref)[index // (micro // 2)]
        for side in range(2):
            start = (2 * index + side) * 2 * pad
            here = pre[start : start + 2 * pad]
            pre_ref[m, side] = here
            filmed = here * gain_ref[m] + shift_ref[m]
            out[index % (micro // 2), side] = slopes(filmed) * gain_ref[m]


def with_rim(main, rim, m):
    pad = rim.shape[2] // 2
    rows = main.shape[1]
    parts = [rim[m, 0, : pad + 8], main[m, 8 : rows - 8], rim[m, 1, pad - 8 :]]
    return jnp.concatenate(parts, axis=0)


def times_trans(left, right):
    return lax.dot_general(left, right, (((1,), (1,)), ((), ())), preferred_element_type=F32)


def trans_times(left, right):
    return lax.dot_general(left, right, (((0,), (0,)), ((), ())), preferred_element_type=F32)


def both_sides(grad_pre):
    wide = grad_pre.astype(F32)
    return shifted(wide, -1).astype(BF16), shifted(wide, 1).astype(BF16)


def backward(g, slope, w_ref):
    grad_pre = (g * slope).astype(BF16)
    later, earlier = both_sides(grad_pre)
    d_in = g + times_trans(later, w_ref[0]) + times_trans(grad_pre, w_ref[1])
    d_in = d_in + times_trans(earlier, w_ref[2])
    return grad_pre, d_in.astype(BF16)


def top_gradient(cot_ref, rim_ref, m):
    return jnp.concatenate([rim_ref[m, 0], cot_ref[m], rim_ref[m, 1]], axis=0)


def factors(refs, j):
    main, rim, w_ref = refs
    return with_rim(main, rim, j), w_ref


def relay_kernel(pair, *refs):
    own, other, g_refs, d_ref = refs[:3], refs[3:6], refs[6:-1], refs[-1]
    section_id = lax.axis_index("section")
    for half in range(2):
        upper, lower = (own, other) if half else (other, own)

        @pl.when(section_id == 2 * pair + half)
        def _(upper=upper, lower=lower):
            for j in range(d_ref.shape[0]):
                g = top_gradient(*g_refs, j) if len(g_refs) == 2 else g_refs[0][j]
                middle = backward(g.astype(F32), *factors(upper, j))[1]
                d_ref[j] = backward(middle.astype(F32), *factors(lower, j))[1]


def chain_kernel(hops, *refs):
    own, other, top_refs = refs[:3], refs[3:6], refs[6:8]
    got_refs = refs[8 : 8 + hops]
    grad_ref, d_ref, send_ref, g_now = refs[8 + hops :]
    rows, wide = d_ref.shape[1], grad_ref.shape[1]
    pad = (wide - rows) // 2
    inner = slice(pad, pad + rows)
    section_id = lax.axis_index("section")

    @pl.when(section_id // 2 == hops)
    def _():
        for j in range(d_ref.shape[0]):
            g_now[j] = top_gradient(*top_refs, j)

    for index in range(hops):

        @pl.when(section_id // 2 == hops - 1 - index)
        def _(index=index):
            g_now[...] = got_refs[index][...]

    for half in range(2):
        upper, lower = (own, other) if half else (other, own)

        @pl.when(section_id % 2 == half)
        def _(upper=upper, lower=lower, half=half):
            for j in range(d_ref.shape[0]):
                first = backward(g_now[j].astype(F32), *factors(upper, j))
                second = backward(first[1].astype(F32), *factors(lower, j))
                mine, away = (first, second) if half else (second, first)
                grad_ref[j] = mine[0]
                d_ref[j] = mine[1][inner]
                send_ref[j, :wide] = away[0]
                send_ref[j, wide:] = away[1][inner]


def split_rows(rows):
    high = rows.astype(BF16).astype(F32)
    low = (rows - high).astype(BF16).astype(F32)
    return jnp.concatenate([high, low], axis=0).astype(BF16)


def joined_rows(pair):
    wide = pair.astype(F32)
    half = wide.shape[0] // 2
    return wide[:half] + wide[half:]


def last_kernel(outer, *refs):
    x_ref, pre_ref, pre_rim, gain_ref, grad_ref, d_mine, got_ref, d_ref = refs[:8]
    own_refs = refs[8 : 8 + PARTS]
    send_refs = refs[8 + PARTS : -2]
    total, sums = refs[-2:]
    micro, rows, channels = x_ref.shape
    wide = grad_ref.shape[1]
    pad = (wide - rows) // 2
    inner = slice(pad, pad + rows)
    mine = lax.axis_index("bulk") // 2
    half = lax.axis_index("section") % 2
    for place, source in enumerate((grad_ref, got_ref)):
        for j, m in enumerate(turn(half, micro, place)):
            grad_pre = source[j, :wide]
            later, earlier = both_sides(grad_pre)
            d_ref[m] = got_ref[j, wide:] if place else d_mine[j]
            for tap, side in enumerate((later, grad_pre, earlier)):
                where = slice(tap * channels, (tap + 1) * channels)
                term = trans_times(x_ref[m], side[inner])
                total[where] = total[where] + term if place or j else term
            film = grad_pre[inner].astype(F32)
            pre = with_rim(pre_ref, pre_rim, m)[inner]
            scale = 1.0 / gain_ref[m]
            sums[pl.ds(m, 1)] = scale * jnp.sum(film * pre, axis=0, keepdims=True)
            sums[pl.ds(micro + m, 1)] = scale * jnp.sum(film, axis=0, keepdims=True)
    rows_out = split_rows(sums[...])
    extra = rows_out.shape[0]
    chunk = own_refs[0].shape[0]
    parts_count = len(own_refs)
    for part in range(parts_count):
        for k in range(outer):
            start = pl.multiple_of(((mine ^ k) * parts_count + part) * chunk, 8)
            term = total[pl.ds(start, chunk), :]
            if k == 0:
                own_refs[part][...] = term
            else:
                ref = send_refs[part * (outer - 1) + k - 1]
                ref[ref.shape[0] - chunk :] = term.astype(BF16)
                if part == 0:
                    ref[:extra] = rows_out


def gather_kernel(outer, own_ref, mine_ref, *refs):
    got_refs = refs[: outer - 1]
    out_ref, held = refs[outer - 1 :]
    mine = lax.axis_index("bulk") // 2
    chunk = own_ref.shape[0]
    extra = out_ref.shape[0] - chunk
    acc = own_ref[...]
    for k in range(1, outer):
        acc = acc + got_refs[k - 1][extra:].astype(F32)
    out_ref[extra:] = acc.astype(BF16)
    if extra:
        held[mine] = joined_rows(mine_ref[:extra])
        for k in range(1, outer):
            held[mine ^ k] = joined_rows(got_refs[k - 1][:extra])
        rows = held[0]
        for index in range(1, outer):
            rows = rows + held[index]
        out_ref[:extra] = split_rows(rows)


def pair_kernel(a_ref, b_ref, *refs):
    out_ref = refs[-1]
    extra = a_ref.shape[0] - out_ref.shape[0]
    out_ref[...] = (a_ref[extra:].astype(F32) + b_ref[extra:].astype(F32)).astype(BF16)


def spread_kernel(micro, outer, bins, a_ref, b_ref, *refs):
    chunk_refs = refs[:-3]
    out_ref, gain_ref, shift_ref = refs[-3:]
    chunk = chunk_refs[0].shape[0]
    parts_count = len(chunk_refs) // outer
    mine = lax.axis_index("bulk") // 2
    for part in range(parts_count):
        for k in range(outer):
            start = pl.multiple_of(((mine ^ k) * parts_count + part) * chunk, 8)
            out_ref[pl.ds(start, chunk), :] = chunk_refs[part * outer + k][...].astype(F32)
    extra = 4 * micro
    rows = joined_rows(a_ref[:extra]) + joined_rows(b_ref[:extra])
    gain_ref[...] = jnp.zeros_like(gain_ref)
    shift_ref[...] = jnp.zeros_like(shift_ref)
    for m in range(micro):
        gain_ref[bins[m]] += rows[m : m + 1]
        shift_ref[bins[m]] += rows[micro + m : micro + m + 1]


def shape_of(shape, dtype):
    return jax.ShapeDtypeStruct(shape, dtype)


def call(kernel, outs, args, scalars=(), remote=(), scratch=(), flops=1, limit=4):
    vmem = pl.BlockSpec(memory_space=pltpu.VMEM)
    smem = pl.BlockSpec(memory_space=pltpu.SMEM)
    kept = pl.BlockSpec(memory_space=pltpu.HBM)
    several = isinstance(outs, (list, tuple))
    return pl.pallas_call(
        kernel,
        in_specs=[smem] * len(scalars) + [kept] * len(remote) + [vmem] * len(args),
        out_specs=[vmem] * len(outs) if several else vmem,
        out_shape=outs,
        scratch_shapes=scratch,
        compiler_params=pltpu.CompilerParams(vmem_limit_bytes=limit << 20),
        cost_estimate=cost(flops, 1 << 20),
    )(*scalars, *[pltpu.with_memory_space_constraint(v, pltpu.HBM) for v in remote], *args)


def step(activations, weights, film_gain, film_shift, doa_bins, cotangent):
    sections = lax.axis_size("section")
    bulk_count = lax.axis_size("bulk")
    outer = bulk_count // 2
    x = activations[0]
    w_set = weights[0]
    micro, rows, channels = x.shape
    bins_count = film_gain.shape[1]
    gain_table = film_gain.reshape(bins_count, 1, channels)
    shift_table = film_shift.reshape(bins_count, 1, channels)
    pad = 16 * -(-(sections + 1) // 16)
    wide = rows + 2 * pad

    edges = shape_of((2, micro, pad, channels), BF16)
    near, far = call(
        edge_kernel,
        [edges, edges],
        [],
        remote=[x, cotangent],
        scratch=[pltpu.SemaphoreType.DMA((4,))],
    )
    opposite = [(i, (i + 1 if i % 2 else i - 1) % bulk_count) for i in range(bulk_count)]
    far = lax.ppermute(far, "bulk", opposite)
    near = lax.ppermute(near, "bulk", [(i, i ^ 1) for i in range(bulk_count)])

    matmul = 2 * 3 * micro * wide * channels * channels
    picked = shape_of((micro, 1, channels), F32)
    count = micro // 2
    half_main = shape_of((count, rows, channels), F32)
    x, cot, w_set, gain_rows, shift_rows, keep, send, pre = call(
        forward_kernel,
        [shape_of(x.shape, BF16), shape_of((count, rows, channels), BF16)]
        + [shape_of(w_set.shape, BF16), picked, picked]
        + [half_main, half_main, shape_of(x.shape, F32)],
        [],
        scalars=[doa_bins],
        remote=[x, cotangent, w_set, gain_table, shift_table],
        scratch=[pltpu.SemaphoreType.DMA((3 + 2 * micro,))],
        flops=matmul,
        limit=12,
    )

    def to_other(value):
        return lax.ppermute(value, "section", [(i, i ^ 1) for i in range(sections)])

    other_w = to_other(w_set)
    other = to_other(send)
    half_rim = shape_of((count, 2, 2 * pad, channels), F32)
    keep_rim, send_rim, pre_rim, g_rim = call(
        rim_kernel,
        [half_rim, half_rim]
        + [
            shape_of((micro, 2, 2 * pad, channels), F32),
            shape_of((count, 2, pad, channels), BF16),
        ],
        [near, far, x, w_set, gain_rows, shift_rows],
        scratch=[pltpu.VMEM((2, 2, micro, pad, channels), BF16)],
        flops=matmul // 4,
        limit=8,
    )
    other_rim = to_other(send_rim)
    tables = [keep, keep_rim, w_set, other, other_rim, other_w]

    sources = []
    half_wide = shape_of((count, wide, channels), BF16)
    hops = sections // 2 - 1
    for hop in range(hops):
        pair = hops - hop
        d_wide = call(
            functools.partial(relay_kernel, pair),
            half_wide,
            tables + (sources[-1:] if hop else [cot, g_rim]),
            flops=matmul,
            limit=8,
        )
        down = [(2 * pair + c, 2 * pair - 2 + c) for c in range(2)]
        pairs = down + [(target, source) for source, target in down]
        sources.append(lax.ppermute(d_wide, "section", pairs))
    grad_own, d_own, away = call(
        functools.partial(chain_kernel, hops),
        [
            half_wide,
            shape_of((count, rows, channels), BF16),
            shape_of((count, wide + rows, channels), BF16),
        ],
        tables + [cot, g_rim] + sources,
        scratch=[pltpu.VMEM(half_wide.shape, BF16)],
        flops=matmul,
        limit=12,
    )
    got_away = to_other(away)

    chunk = 3 * channels // outer // PARTS
    extra = 4 * micro
    messages = [shape_of((chunk + (0 if part else extra), channels), BF16) for part in range(PARTS)]
    made = call(
        functools.partial(last_kernel, outer),
        [shape_of(x.shape, BF16)]
        + [shape_of((chunk, channels), F32)] * PARTS
        + [messages[part] for part in range(PARTS) for _ in range(outer - 1)],
        [x, pre, pre_rim, gain_rows, grad_own, d_own, got_away],
        scratch=[
            pltpu.VMEM((3 * channels, channels), F32),
            pltpu.VMEM((2 * micro, channels), F32),
        ],
        flops=matmul,
        limit=16,
    )
    d_local = made[0]
    owns = made[1 : 1 + PARTS]

    def across(value, k):
        pairs = [(i, i ^ (2 * k)) for i in range(bulk_count)]
        return lax.ppermute(value, "bulk", pairs)

    swap = [(i, i ^ 1) for i in range(bulk_count)]
    order = [k for k in range(2, outer)] + [1]
    scattered = []
    for part in range(PARTS):
        sends = made[1 + PARTS + part * (outer - 1) :][: outer - 1]
        got = {k: across(sends[k - 1], k) for k in order}
        scattered.append((sends[0], got))
    summed = []
    for part in range(PARTS):
        first, got = scattered[part]
        partial_sum = call(
            functools.partial(gather_kernel, outer),
            messages[part],
            [owns[part], first] + [got[k] for k in range(1, outer)],
            scratch=[pltpu.VMEM((outer, 2 * micro, channels), F32)],
        )
        summed.append((partial_sum, lax.ppermute(partial_sum, "bulk", swap)))
    spread = []
    for part in range(PARTS):
        done = call(
            pair_kernel,
            shape_of((chunk, channels), BF16),
            list(summed[part]) + spread[-outer:][:1],
        )
        got = {k: across(done, k) for k in order}
        spread += [done] + [got[k] for k in range(1, outer)]
    table = shape_of((bins_count, 1, channels), F32)
    d_weights, d_gain, d_shift = call(
        functools.partial(spread_kernel, micro, outer),
        [shape_of((3 * channels, channels), F32), table, table],
        [*summed[0], *spread],
        scalars=[doa_bins],
    )
    return (
        d_local[None],
        d_weights.reshape(1, 3, channels, channels),
        d_gain.reshape(1, bins_count, channels),
        d_shift.reshape(1, bins_count, channels),
    )


def solution(mesh):
    return jax.shard_map(
        step,
        mesh=mesh,
        in_specs=(
            P("section", None, "bulk", None),
            P("section", None, None, None),
            P("section", None, None),
            P("section", None, None),
            P(),
            P(None, "bulk", None),
        ),
        out_specs=(
            P("section", None, "bulk", None),
            P("section", None, None, None),
            P("section", None, None),
            P("section", None, None),
        ),
        check_vma=False,
    )
```

```python
import functools

import jax
import jax.numpy as jnp
from jax import lax
from jax.experimental import pallas as pl
from jax.experimental.pallas import tpu as pltpu
from jax.sharding import PartitionSpec as P


F32 = jnp.float32
BF16 = jnp.bfloat16
PARTS = 2


def cost(flops, moved, trans=0):
    return pl.CostEstimate(flops=flops, bytes_accessed=moved, transcendentals=trans)


def shifted(value, amount):
    rows = value.shape[0]
    return pltpu.roll(value, amount % rows, 0)


def copies(pairs, sems):
    started = []
    for index, (source, target) in enumerate(pairs):
        copy = pltpu.make_async_copy(source, target, sems.at[index])
        copy.start()
        started.append(copy)
    return started


def edge_kernel(x_ref, cot_ref, near_ref, far_ref, sems):
    rows = x_ref.shape[1]
    pad = near_ref.shape[2]
    odd = lax.axis_index("bulk") % 2
    last = rows - pad
    near = pl.multiple_of((1 - odd) * last, pad)
    far = pl.multiple_of(odd * last, pad)
    pairs = []
    for index, ref in enumerate((x_ref, cot_ref)):
        pairs.append((ref.at[:, pl.ds(near, pad), :], near_ref.at[index]))
        pairs.append((ref.at[:, pl.ds(far, pad), :], far_ref.at[index]))
    for copy in copies(pairs, sems):
        copy.wait()


def slopes(filmed):
    sig = 0.5 * jnp.tanh(0.5 * filmed) + 0.5
    return sig * (1.0 + filmed * (1.0 - sig))


def taps(value, w_ref):
    wide = value.astype(F32)
    pre = jnp.dot(shifted(wide, 1).astype(BF16), w_ref[0], preferred_element_type=F32)
    pre = pre + jnp.dot(value, w_ref[1], preferred_element_type=F32)
    return pre + jnp.dot(shifted(wide, -1).astype(BF16), w_ref[2], preferred_element_type=F32)


def turn(half, micro, place):
    start = half if place == 0 else 1 - half
    return [start * (micro // 2) + j for j in range(micro // 2)]


def forward_kernel(bins_in, x_in, cot_in, w_in, gain_in, shift_in, *refs):
    x_ref, cot_ref, w_ref, gain_ref, shift_ref, keep_ref, send_ref, pre_ref = refs[:8]
    bins, gains, shifts, sems = refs[8:]
    micro = x_ref.shape[0]
    half = lax.axis_index("section") % 2
    order = turn(half, micro, 1) + turn(half, micro, 0)
    pairs = [(bins_in, bins), (gain_in, gains), (shift_in, shifts), (w_in, w_ref)]
    pairs += [(x_in.at[m], x_ref.at[m]) for m in order]
    mine = cot_in.at[pl.ds(half * (micro // 2), micro // 2)]
    started = copies(pairs + [(mine, cot_ref)], sems)
    for copy in started[:4]:
        copy.wait()
    for m in range(micro):
        gain_ref[m] = gains[bins[m]]
        shift_ref[m] = shifts[bins[m]]
    for index, m in enumerate(order):
        started[4 + index].wait()
        out = (send_ref, keep_ref)[index // (micro // 2)]
        pre = taps(x_ref[m], w_ref)
        out[index % (micro // 2)] = slopes(pre * gain_ref[m] + shift_ref[m]) * gain_ref[m]
        pre_ref[m] = pre
    started[-1].wait()


def rim_kernel(near_ref, far_ref, x_ref, w_ref, gain_ref, shift_ref, *refs):
    keep_ref, send_ref, pre_ref, g_ref, halo = refs
    micro, rows = x_ref.shape[:2]
    pad = near_ref.shape[2]
    odd = lax.axis_index("bulk") % 2
    half = lax.axis_index("section") % 2

    @pl.when(odd == 1)
    def _():
        halo[0] = near_ref[...]
        halo[1] = far_ref[...]

    @pl.when(odd == 0)
    def _():
        halo[0] = far_ref[...]
        halo[1] = near_ref[...]

    parts = []
    order = turn(half, micro, 0) + turn(half, micro, 1)
    for m in order:
        parts += [halo[0, 0, m], x_ref[m, :pad], x_ref[m, rows - pad :], halo[1, 0, m]]
    for j, m in enumerate(turn(half, micro, 0)):
        g_ref[j, 0] = halo[0, 1, m]
        g_ref[j, 1] = halo[1, 1, m]
    pre = taps(jnp.concatenate(parts, axis=0), w_ref)
    for index, m in enumerate(order):
        out = (keep_ref, send_ref)[index // (micro // 2)]
        for side in range(2):
            start = (2 * index + side) * 2 * pad
            here = pre[start : start + 2 * pad]
            pre_ref[m, side] = here
            filmed = here * gain_ref[m] + shift_ref[m]
            out[index % (micro // 2), side] = slopes(filmed) * gain_ref[m]


def with_rim(main, rim, m):
    pad = rim.shape[2] // 2
    rows = main.shape[1]
    parts = [rim[m, 0, : pad + 8], main[m, 8 : rows - 8], rim[m, 1, pad - 8 :]]
    return jnp.concatenate(parts, axis=0)


def times_trans(left, right):
    return lax.dot_general(left, right, (((1,), (1,)), ((), ())), preferred_element_type=F32)


def trans_times(left, right):
    return lax.dot_general(left, right, (((0,), (0,)), ((), ())), preferred_element_type=F32)


def both_sides(grad_pre):
    wide = grad_pre.astype(F32)
    return shifted(wide, -1).astype(BF16), shifted(wide, 1).astype(BF16)


def backward(g, slope, w_ref):
    grad_pre = (g * slope).astype(BF16)
    later, earlier = both_sides(grad_pre)
    d_in = g + times_trans(later, w_ref[0]) + times_trans(grad_pre, w_ref[1])
    d_in = d_in + times_trans(earlier, w_ref[2])
    return grad_pre, d_in.astype(BF16), d_in


def top_gradient(cot_ref, rim_ref, m):
    return jnp.concatenate([rim_ref[m, 0], cot_ref[m], rim_ref[m, 1]], axis=0)


def factors(refs, j):
    main, rim, w_ref = refs
    return with_rim(main, rim, j), w_ref


def by_half(pair, own, other, run):
    section_id = lax.axis_index("section")
    for half in range(2):
        upper, lower = (own, other) if half else (other, own)
        here = section_id % 2 == half if pair is None else section_id == 2 * pair + half

        @pl.when(here)
        def _(upper=upper, lower=lower, half=half):
            run(upper, lower, half)


def inner_kernel(pair, *refs):
    own, other, cot_ref, d_ref = refs[:2], refs[2:4], refs[4], refs[5]
    rows = cot_ref.shape[1]
    cut = (rows - d_ref.shape[1]) // 2

    def run(upper, lower, half):
        for j in range(d_ref.shape[0]):
            g = cot_ref[j].astype(F32)
            middle = backward(g, upper[0][j], upper[1])[1].astype(F32)
            d_ref[j] = backward(middle, lower[0][j], lower[1])[2][cut : rows - cut].astype(BF16)

    by_half(pair, own, other, run)


def outer_kernel(pair, *refs):
    own, other, cot_ref, rim_ref, d_ref = refs[:2], refs[2:4], refs[4], refs[5], refs[6]
    count, rows = cot_ref.shape[:2]
    pad = rim_ref.shape[2]
    cut = d_ref.shape[2] // 2

    def stacked(ref):
        return jnp.concatenate([ref[j, side] for j in range(count) for side in range(2)], axis=0)

    def run(upper, lower, half):
        parts = []
        for j in range(count):
            parts += [rim_ref[j, 0], cot_ref[j, :pad], cot_ref[j, rows - pad :], rim_ref[j, 1]]
        g = jnp.concatenate(parts, axis=0).astype(F32)
        middle = backward(g, stacked(upper[0]), upper[1])[1].astype(F32)
        d_in = backward(middle, stacked(lower[0]), lower[1])[2]
        for j in range(count):
            for side in range(2):
                start = (2 * j + side) * 2 * pad + pad - cut
                d_ref[j, side] = d_in[start : start + 2 * cut].astype(BF16)

    by_half(pair, own, other, run)


def arrived(inner_ref, outer_ref, j, wide):
    rest = wide - inner_ref.shape[1] - 2 * outer_ref.shape[2]
    fill = jnp.zeros((rest // 2, inner_ref.shape[2]), F32)
    parts = [outer_ref[j, 0], inner_ref[j], outer_ref[j, 1]]
    return jnp.concatenate([fill] + [part.astype(F32) for part in parts] + [fill], axis=0)


def relay_kernel(pair, *refs):
    own, other, got_refs = refs[:3], refs[3:6], refs[6:8]
    inner_ref, outer_ref = refs[8:]
    cut = outer_ref.shape[2] // 2
    size = inner_ref.shape[1]
    wide = own[0].shape[1] + own[1].shape[2]

    def run(upper, lower, half):
        for j in range(inner_ref.shape[0]):
            g = arrived(*got_refs, j, wide)
            middle = backward(g, *factors(upper, j))[1].astype(F32)
            d_in = backward(middle, *factors(lower, j))[2]
            start = (wide - size) // 2
            inner_ref[j] = d_in[start : start + size].astype(BF16)
            outer_ref[j, 0] = d_in[start - 2 * cut : start].astype(BF16)
            outer_ref[j, 1] = d_in[start + size : start + size + 2 * cut].astype(BF16)

    by_half(pair, own, other, run)


def chain_kernel(hops, *refs):
    own, other, top_refs = refs[:3], refs[3:6], refs[6:8]
    got_refs = refs[8 : 8 + 2 * hops]
    grad_ref, d_ref, send_ref, g_now = refs[8 + 2 * hops :]
    rows, wide = d_ref.shape[1], grad_ref.shape[1]
    pad = (wide - rows) // 2
    inner = slice(pad, pad + rows)
    section_id = lax.axis_index("section")

    @pl.when(section_id // 2 == hops)
    def _():
        for j in range(d_ref.shape[0]):
            g_now[j] = top_gradient(*top_refs, j).astype(F32)

    for index in range(hops):

        @pl.when(section_id // 2 == hops - 1 - index)
        def _(index=index):
            for j in range(d_ref.shape[0]):
                g_now[j] = arrived(*got_refs[2 * index : 2 * index + 2], j, wide)

    def run(upper, lower, half):
        for j in range(d_ref.shape[0]):
            first = backward(g_now[j], *factors(upper, j))
            second = backward(first[1].astype(F32), *factors(lower, j))
            mine, away = (first, second) if half else (second, first)
            grad_ref[j] = mine[0]
            d_ref[j] = mine[1][inner]
            send_ref[j, :wide] = away[0]
            send_ref[j, wide:] = away[1][inner]

    by_half(None, own, other, run)


def split_rows(rows):
    high = rows.astype(BF16).astype(F32)
    low = (rows - high).astype(BF16).astype(F32)
    return jnp.concatenate([high, low], axis=0).astype(BF16)


def joined_rows(pair):
    wide = pair.astype(F32)
    half = wide.shape[0] // 2
    return wide[:half] + wide[half:]


def last_kernel(outer, *refs):
    x_ref, pre_ref, pre_rim, gain_ref, grad_ref, d_mine, got_ref, d_ref = refs[:8]
    own_refs = refs[8 : 8 + PARTS]
    send_refs = refs[8 + PARTS : -2]
    total, sums = refs[-2:]
    micro, rows, channels = x_ref.shape
    wide = grad_ref.shape[1]
    pad = (wide - rows) // 2
    inner = slice(pad, pad + rows)
    mine = lax.axis_index("bulk") // 2
    half = lax.axis_index("section") % 2
    for place, source in enumerate((grad_ref, got_ref)):
        for j, m in enumerate(turn(half, micro, place)):
            grad_pre = source[j, :wide]
            later, earlier = both_sides(grad_pre)
            d_ref[m] = got_ref[j, wide:] if place else d_mine[j]
            for tap, side in enumerate((later, grad_pre, earlier)):
                where = slice(tap * channels, (tap + 1) * channels)
                term = trans_times(x_ref[m], side[inner])
                total[where] = total[where] + term if place or j else term
            film = grad_pre[inner].astype(F32)
            pre = with_rim(pre_ref, pre_rim, m)[inner]
            scale = 1.0 / gain_ref[m]
            sums[pl.ds(m, 1)] = scale * jnp.sum(film * pre, axis=0, keepdims=True)
            sums[pl.ds(micro + m, 1)] = scale * jnp.sum(film, axis=0, keepdims=True)
    rows_out = split_rows(sums[...])
    extra = rows_out.shape[0]
    chunk = own_refs[0].shape[0]
    parts_count = len(own_refs)
    for part in range(parts_count):
        for k in range(outer):
            start = pl.multiple_of(((mine ^ k) * parts_count + part) * chunk, 8)
            term = total[pl.ds(start, chunk), :]
            if k == 0:
                own_refs[part][...] = term
            else:
                ref = send_refs[part * (outer - 1) + k - 1]
                ref[ref.shape[0] - chunk :] = term.astype(BF16)
                if part == 0:
                    ref[:extra] = rows_out


def gather_kernel(outer, own_ref, mine_ref, *refs):
    got_refs = refs[: outer - 1]
    out_ref, held = refs[outer - 1 :]
    mine = lax.axis_index("bulk") // 2
    chunk = own_ref.shape[0]
    extra = out_ref.shape[0] - chunk
    acc = own_ref[...]
    for k in range(1, outer):
        acc = acc + got_refs[k - 1][extra:].astype(F32)
    out_ref[extra:] = acc.astype(BF16)
    if extra:
        held[mine] = joined_rows(mine_ref[:extra])
        for k in range(1, outer):
            held[mine ^ k] = joined_rows(got_refs[k - 1][:extra])
        rows = held[0]
        for index in range(1, outer):
            rows = rows + held[index]
        out_ref[:extra] = split_rows(rows)


def pair_kernel(a_ref, b_ref, *refs):
    out_ref = refs[-1]
    extra = a_ref.shape[0] - out_ref.shape[0]
    out_ref[...] = (a_ref[extra:].astype(F32) + b_ref[extra:].astype(F32)).astype(BF16)


def spread_kernel(micro, outer, bins, a_ref, b_ref, *refs):
    chunk_refs = refs[:-3]
    out_ref, gain_ref, shift_ref = refs[-3:]
    chunk = chunk_refs[0].shape[0]
    parts_count = len(chunk_refs) // outer
    mine = lax.axis_index("bulk") // 2
    for part in range(parts_count):
        for k in range(outer):
            start = pl.multiple_of(((mine ^ k) * parts_count + part) * chunk, 8)
            out_ref[pl.ds(start, chunk), :] = chunk_refs[part * outer + k][...].astype(F32)
    extra = 4 * micro
    rows = joined_rows(a_ref[:extra]) + joined_rows(b_ref[:extra])
    gain_ref[...] = jnp.zeros_like(gain_ref)
    shift_ref[...] = jnp.zeros_like(shift_ref)
    for m in range(micro):
        gain_ref[bins[m]] += rows[m : m + 1]
        shift_ref[bins[m]] += rows[micro + m : micro + m + 1]


def shape_of(shape, dtype):
    return jax.ShapeDtypeStruct(shape, dtype)


def call(kernel, outs, args, scalars=(), remote=(), scratch=(), flops=1, limit=4):
    vmem = pl.BlockSpec(memory_space=pltpu.VMEM)
    smem = pl.BlockSpec(memory_space=pltpu.SMEM)
    kept = pl.BlockSpec(memory_space=pltpu.HBM)
    several = isinstance(outs, (list, tuple))
    return pl.pallas_call(
        kernel,
        in_specs=[smem] * len(scalars) + [kept] * len(remote) + [vmem] * len(args),
        out_specs=[vmem] * len(outs) if several else vmem,
        out_shape=outs,
        scratch_shapes=scratch,
        compiler_params=pltpu.CompilerParams(vmem_limit_bytes=limit << 20),
        cost_estimate=cost(flops, 1 << 20),
    )(*scalars, *[pltpu.with_memory_space_constraint(v, pltpu.HBM) for v in remote], *args)


def step(activations, weights, film_gain, film_shift, doa_bins, cotangent):
    sections = lax.axis_size("section")
    bulk_count = lax.axis_size("bulk")
    outer = bulk_count // 2
    x = activations[0]
    w_set = weights[0]
    micro, rows, channels = x.shape
    bins_count = film_gain.shape[1]
    gain_table = film_gain.reshape(bins_count, 1, channels)
    shift_table = film_shift.reshape(bins_count, 1, channels)
    pad = 16 * -(-(sections + 1) // 16)
    wide = rows + 2 * pad

    edges = shape_of((2, micro, pad, channels), BF16)
    near, far = call(
        edge_kernel,
        [edges, edges],
        [],
        remote=[x, cotangent],
        scratch=[pltpu.SemaphoreType.DMA((4,))],
    )
    opposite = [(i, (i + 1 if i % 2 else i - 1) % bulk_count) for i in range(bulk_count)]
    far = lax.ppermute(far, "bulk", opposite)
    near = lax.ppermute(near, "bulk", [(i, i ^ 1) for i in range(bulk_count)])

    matmul = 2 * 3 * micro * wide * channels * channels
    picked = shape_of((micro, 1, channels), F32)
    count = micro // 2
    half_main = shape_of((count, rows, channels), F32)
    x, cot, w_set, gain_rows, shift_rows, keep, send, pre = call(
        forward_kernel,
        [shape_of(x.shape, BF16), shape_of((count, rows, channels), BF16)]
        + [shape_of(w_set.shape, BF16), picked, picked]
        + [half_main, half_main, shape_of(x.shape, F32)],
        [],
        remote=[doa_bins, x, cotangent, w_set, gain_table, shift_table],
        scratch=[
            pltpu.SMEM(doa_bins.shape, jnp.int32),
            pltpu.VMEM(gain_table.shape, F32),
            pltpu.VMEM(shift_table.shape, F32),
            pltpu.SemaphoreType.DMA((5 + micro,)),
        ],
        flops=matmul,
        limit=12,
    )

    def to_other(value):
        return lax.ppermute(value, "section", [(i, i ^ 1) for i in range(sections)])

    other_w = to_other(w_set)
    other = to_other(send)
    half_rim = shape_of((count, 2, 2 * pad, channels), F32)
    keep_rim, send_rim, pre_rim, g_rim = call(
        rim_kernel,
        [half_rim, half_rim]
        + [shape_of((micro, 2, 2 * pad, channels), F32), shape_of((count, 2, pad, channels), BF16)],
        [near, far, x, w_set, gain_rows, shift_rows],
        scratch=[pltpu.VMEM((2, 2, micro, pad, channels), BF16)],
        flops=matmul // 4,
        limit=8,
    )
    other_rim = to_other(send_rim)
    tables = [keep, keep_rim, w_set, other, other_rim, other_w]

    half_wide = shape_of((count, wide, channels), BF16)
    hops = sections // 2 - 1
    cut = 8 * -(-sections // 8)
    inner_shape = shape_of((count, rows - 2 * cut, channels), BF16)
    outer_shape = shape_of((count, 2, 2 * cut, channels), BF16)

    def down(value, pair):
        pairs = [(2 * pair + c, 2 * pair - 2 + c) for c in range(2)]
        return lax.ppermute(value, "section", pairs + [(low, high) for high, low in pairs])

    sources = []
    for hop in range(hops):
        pair = hops - hop
        if hop:
            inner, outer_rows = call(
                functools.partial(relay_kernel, pair),
                [inner_shape, outer_shape],
                tables + sources[-2:],
                flops=matmul,
                limit=8,
            )
            sources += [down(inner, pair), down(outer_rows, pair)]
            continue
        inner = call(
            functools.partial(inner_kernel, pair),
            inner_shape,
            [keep, w_set, other, other_w, cot],
            flops=matmul,
            limit=8,
        )
        inner = down(inner, pair)
        outer_rows = call(
            functools.partial(outer_kernel, pair),
            outer_shape,
            [keep_rim, w_set, other_rim, other_w, cot, g_rim],
            flops=matmul // 2,
            limit=8,
        )
        outer_rows = down(outer_rows, pair)
        sources += [inner, outer_rows]
    grad_own, d_own, away = call(
        functools.partial(chain_kernel, hops),
        [
            half_wide,
            shape_of((count, rows, channels), BF16),
            shape_of((count, wide + rows, channels), BF16),
        ],
        tables + [cot, g_rim] + sources,
        scratch=[pltpu.VMEM(half_wide.shape, F32)],
        flops=matmul,
        limit=12,
    )
    got_away = to_other(away)

    chunk = 3 * channels // outer // PARTS
    extra = 4 * micro
    messages = [shape_of((chunk + (0 if part else extra), channels), BF16) for part in range(PARTS)]
    made = call(
        functools.partial(last_kernel, outer),
        [shape_of(x.shape, BF16)]
        + [shape_of((chunk, channels), F32)] * PARTS
        + [messages[part] for part in range(PARTS) for _ in range(outer - 1)],
        [x, pre, pre_rim, gain_rows, grad_own, d_own, got_away],
        scratch=[
            pltpu.VMEM((3 * channels, channels), F32),
            pltpu.VMEM((2 * micro, channels), F32),
        ],
        flops=matmul,
        limit=16,
    )
    d_local = made[0]
    owns = made[1 : 1 + PARTS]

    def across(value, k):
        pairs = [(i, i ^ (2 * k)) for i in range(bulk_count)]
        return lax.ppermute(value, "bulk", pairs)

    swap = [(i, i ^ 1) for i in range(bulk_count)]
    order = [k for k in range(2, outer)] + [1]
    scattered = []
    for part in range(PARTS):
        sends = made[1 + PARTS + part * (outer - 1) :][: outer - 1]
        got = {k: across(sends[k - 1], k) for k in order}
        scattered.append((sends[0], got))
    summed = []
    for part in range(PARTS):
        first, got = scattered[part]
        partial_sum = call(
            functools.partial(gather_kernel, outer),
            messages[part],
            [owns[part], first] + [got[k] for k in range(1, outer)],
            scratch=[pltpu.VMEM((outer, 2 * micro, channels), F32)],
        )
        summed.append((partial_sum, lax.ppermute(partial_sum, "bulk", swap)))
    spread = []
    for part in range(PARTS):
        done = call(
            pair_kernel, shape_of((chunk, channels), BF16), list(summed[part]) + spread[-outer:][:1]
        )
        got = {k: across(done, k) for k in order}
        spread += [done] + [got[k] for k in range(1, outer)]
    table = shape_of((bins_count, 1, channels), F32)
    d_weights, d_gain, d_shift = call(
        functools.partial(spread_kernel, micro, outer),
        [shape_of((3 * channels, channels), F32), table, table],
        [*summed[0], *spread],
        scalars=[doa_bins],
    )
    return (
        d_local[None],
        d_weights.reshape(1, 3, channels, channels),
        d_gain.reshape(1, bins_count, channels),
        d_shift.reshape(1, bins_count, channels),
    )


def solution(mesh):
    return jax.shard_map(
        step,
        mesh=mesh,
        in_specs=(
            P("section", None, "bulk", None),
            P("section", None, None, None),
            P("section", None, None),
            P("section", None, None),
            P(),
            P(None, "bulk", None),
        ),
        out_specs=(
            P("section", None, "bulk", None),
            P("section", None, None, None),
            P("section", None, None),
            P("section", None, None),
        ),
        check_vma=False,
    )
```

```python
import functools

import jax
import jax.numpy as jnp
from jax import lax
from jax.experimental import pallas as pl
from jax.experimental.pallas import tpu as pltpu
from jax.sharding import PartitionSpec as P


F32 = jnp.float32
BF16 = jnp.bfloat16
PARTS = 2


def cost(flops, moved, trans=0):
    return pl.CostEstimate(flops=flops, bytes_accessed=moved, transcendentals=trans)


def shifted(value, amount):
    rows = value.shape[0]
    return pltpu.roll(value, amount % rows, 0)


def copies(pairs, sems):
    started = []
    for index, (source, target) in enumerate(pairs):
        copy = pltpu.make_async_copy(source, target, sems.at[index])
        copy.start()
        started.append(copy)
    return started


def load_kernel(bins_in, x_in, cot_in, w_in, gain_in, shift_in, *refs):
    near_ref, far_ref, x_ref, cot_ref, w_ref, gain_ref, shift_ref = refs[:7]
    bins, gains, shifts, sems = refs[7:]
    micro, rows = x_ref.shape[:2]
    count = micro // 2
    pad = near_ref.shape[1]
    odd = lax.axis_index("bulk") % 2
    mine = cot_in.at[pl.ds(lax.axis_index("section") % 2 * count, count)]
    pairs = [(x_in, x_ref), (mine, cot_ref), (bins_in, bins), (gain_in, gains)]
    started = copies(pairs + [(shift_in, shifts), (w_in, w_ref)], sems)
    for copy in started[:2]:
        copy.wait()
    near = pl.multiple_of((1 - odd) * (rows - pad), pad)
    far = pl.multiple_of(odd * (rows - pad), pad)
    for out, start in ((near_ref, near), (far_ref, far)):
        out[:micro] = x_ref[:, pl.ds(start, pad), :]
        out[micro:] = cot_ref[:, pl.ds(start, pad), :]
    for copy in started[2:]:
        copy.wait()
    for m in range(micro):
        gain_ref[m] = gains[bins[m]]
        shift_ref[m] = shifts[bins[m]]


def slopes(filmed):
    sig = 0.5 * jnp.tanh(0.5 * filmed) + 0.5
    return sig * (1.0 + filmed * (1.0 - sig))


def taps(value, w_ref):
    wide = value.astype(F32)
    pre = jnp.dot(shifted(wide, 1).astype(BF16), w_ref[0], preferred_element_type=F32)
    pre = pre + jnp.dot(value, w_ref[1], preferred_element_type=F32)
    return pre + jnp.dot(shifted(wide, -1).astype(BF16), w_ref[2], preferred_element_type=F32)


def turn(half, micro, place):
    start = half if place == 0 else 1 - half
    return [start * (micro // 2) + j for j in range(micro // 2)]


def forward_kernel(x_ref, w_ref, gain_ref, shift_ref, send_ref, keep_ref, pre_ref):
    micro = x_ref.shape[0]
    half = lax.axis_index("section") % 2
    for place, out in ((1, send_ref), (0, keep_ref)):
        for j, m in enumerate(turn(half, micro, place)):
            pre = taps(x_ref[m], w_ref)
            out[j] = slopes(pre * gain_ref[m] + shift_ref[m]) * gain_ref[m]
            pre_ref[m] = pre


def rim_kernel(near_ref, far_ref, x_ref, w_ref, gain_ref, shift_ref, *refs):
    keep_ref, send_ref, pre_ref, g_ref, halo = refs
    micro, rows = x_ref.shape[:2]
    pad = near_ref.shape[1]
    odd = lax.axis_index("bulk") % 2
    half = lax.axis_index("section") % 2

    @pl.when(odd == 1)
    def _():
        halo[0] = near_ref[...]
        halo[1] = far_ref[...]

    @pl.when(odd == 0)
    def _():
        halo[0] = far_ref[...]
        halo[1] = near_ref[...]

    parts = []
    order = turn(half, micro, 0) + turn(half, micro, 1)
    for m in order:
        parts += [halo[0, m], x_ref[m, :pad], x_ref[m, rows - pad :], halo[1, m]]
    for j in range(micro // 2):
        g_ref[j, 0] = halo[0, micro + j]
        g_ref[j, 1] = halo[1, micro + j]
    pre = taps(jnp.concatenate(parts, axis=0), w_ref)
    for index, m in enumerate(order):
        out = (keep_ref, send_ref)[index // (micro // 2)]
        for side in range(2):
            start = (2 * index + side) * 2 * pad
            here = pre[start : start + 2 * pad]
            pre_ref[m, side] = here
            filmed = here * gain_ref[m] + shift_ref[m]
            out[index % (micro // 2), side] = slopes(filmed) * gain_ref[m]


def with_rim(main, rim, m):
    pad = rim.shape[2] // 2
    rows = main.shape[1]
    parts = [rim[m, 0, : pad + 8], main[m, 8 : rows - 8], rim[m, 1, pad - 8 :]]
    return jnp.concatenate(parts, axis=0)


def times_trans(left, right):
    return lax.dot_general(left, right, (((1,), (1,)), ((), ())), preferred_element_type=F32)


def trans_times(left, right):
    return lax.dot_general(left, right, (((0,), (0,)), ((), ())), preferred_element_type=F32)


def both_sides(grad_pre):
    wide = grad_pre.astype(F32)
    return shifted(wide, -1).astype(BF16), shifted(wide, 1).astype(BF16)


def backward(g, slope, w_ref):
    grad_pre = (g * slope).astype(BF16)
    later, earlier = both_sides(grad_pre)
    d_in = g + times_trans(later, w_ref[0]) + times_trans(grad_pre, w_ref[1])
    d_in = d_in + times_trans(earlier, w_ref[2])
    return grad_pre, d_in.astype(BF16), d_in


def top_gradient(cot_ref, rim_ref, m):
    return jnp.concatenate([rim_ref[m, 0], cot_ref[m], rim_ref[m, 1]], axis=0)


def factors(refs, j):
    main, rim, w_ref = refs
    return with_rim(main, rim, j), w_ref


def by_half(pair, own, other, run):
    section_id = lax.axis_index("section")
    for half in range(2):
        upper, lower = (own, other) if half else (other, own)
        here = section_id % 2 == half if pair is None else section_id == 2 * pair + half

        @pl.when(here)
        def _(upper=upper, lower=lower, half=half):
            run(upper, lower, half)


def inner_kernel(pair, *refs):
    own, other, cot_ref, d_ref = refs[:2], refs[2:4], refs[4], refs[5]
    rows = cot_ref.shape[1]
    cut = (rows - d_ref.shape[1]) // 2

    def run(upper, lower, half):
        for j in range(d_ref.shape[0]):
            g = cot_ref[j].astype(F32)
            middle = backward(g, upper[0][j], upper[1])[1].astype(F32)
            d_ref[j] = backward(middle, lower[0][j], lower[1])[2][cut : rows - cut].astype(BF16)

    by_half(pair, own, other, run)


def outer_kernel(pair, *refs):
    own, other, cot_ref, rim_ref, d_ref = refs[:2], refs[2:4], refs[4], refs[5], refs[6]
    count, rows = cot_ref.shape[:2]
    pad = rim_ref.shape[2]
    cut = d_ref.shape[2] // 2

    def stacked(ref):
        return jnp.concatenate([ref[j, side] for j in range(count) for side in range(2)], axis=0)

    def run(upper, lower, half):
        parts = []
        for j in range(count):
            parts += [rim_ref[j, 0], cot_ref[j, :pad], cot_ref[j, rows - pad :], rim_ref[j, 1]]
        g = jnp.concatenate(parts, axis=0).astype(F32)
        middle = backward(g, stacked(upper[0]), upper[1])[1].astype(F32)
        d_in = backward(middle, stacked(lower[0]), lower[1])[2]
        for j in range(count):
            for side in range(2):
                start = (2 * j + side) * 2 * pad + pad - cut
                d_ref[j, side] = d_in[start : start + 2 * cut].astype(BF16)

    by_half(pair, own, other, run)


def arrived(inner_ref, outer_ref, j, wide):
    rest = wide - inner_ref.shape[1] - 2 * outer_ref.shape[2]
    fill = jnp.zeros((rest // 2, inner_ref.shape[2]), F32)
    parts = [outer_ref[j, 0], inner_ref[j], outer_ref[j, 1]]
    return jnp.concatenate([fill] + [part.astype(F32) for part in parts] + [fill], axis=0)


def relay_kernel(pair, *refs):
    own, other, got_refs = refs[:3], refs[3:6], refs[6:8]
    inner_ref, outer_ref = refs[8:]
    cut = outer_ref.shape[2] // 2
    size = inner_ref.shape[1]
    wide = own[0].shape[1] + own[1].shape[2]

    def run(upper, lower, half):
        for j in range(inner_ref.shape[0]):
            g = arrived(*got_refs, j, wide)
            middle = backward(g, *factors(upper, j))[1].astype(F32)
            d_in = backward(middle, *factors(lower, j))[2]
            start = (wide - size) // 2
            inner_ref[j] = d_in[start : start + size].astype(BF16)
            outer_ref[j, 0] = d_in[start - 2 * cut : start].astype(BF16)
            outer_ref[j, 1] = d_in[start + size : start + size + 2 * cut].astype(BF16)

    by_half(pair, own, other, run)


def chain_kernel(hops, *refs):
    own, other, top_refs = refs[:3], refs[3:6], refs[6:8]
    got_refs = refs[8 : 8 + 2 * hops]
    grad_ref, d_ref, send_ref, g_now = refs[8 + 2 * hops :]
    rows, wide = d_ref.shape[1], grad_ref.shape[1]
    pad = (wide - rows) // 2
    inner = slice(pad, pad + rows)
    section_id = lax.axis_index("section")

    @pl.when(section_id // 2 == hops)
    def _():
        for j in range(d_ref.shape[0]):
            g_now[j] = top_gradient(*top_refs, j).astype(F32)

    for index in range(hops):

        @pl.when(section_id // 2 == hops - 1 - index)
        def _(index=index):
            for j in range(d_ref.shape[0]):
                g_now[j] = arrived(*got_refs[2 * index : 2 * index + 2], j, wide)

    def run(upper, lower, half):
        for j in range(d_ref.shape[0]):
            first = backward(g_now[j], *factors(upper, j))
            second = backward(first[1].astype(F32), *factors(lower, j))
            mine, away = (first, second) if half else (second, first)
            grad_ref[j] = mine[0]
            d_ref[j] = mine[1][inner]
            send_ref[j, :wide] = away[0]
            send_ref[j, wide:] = away[1][inner]

    by_half(None, own, other, run)


def split_rows(rows):
    high = rows.astype(BF16).astype(F32)
    low = (rows - high).astype(BF16).astype(F32)
    return jnp.concatenate([high, low], axis=0).astype(BF16)


def joined_rows(pair):
    wide = pair.astype(F32)
    half = wide.shape[0] // 2
    return wide[:half] + wide[half:]


def last_kernel(outer, *refs):
    x_ref, pre_ref, pre_rim, gain_ref, grad_ref, d_mine, got_ref, d_ref = refs[:8]
    own_refs = refs[8 : 8 + PARTS]
    send_refs = refs[8 + PARTS : -2]
    total, sums = refs[-2:]
    micro, rows, channels = x_ref.shape
    wide = grad_ref.shape[1]
    pad = (wide - rows) // 2
    inner = slice(pad, pad + rows)
    mine = lax.axis_index("bulk") // 2
    half = lax.axis_index("section") % 2
    for place, source in enumerate((grad_ref, got_ref)):
        for j, m in enumerate(turn(half, micro, place)):
            grad_pre = source[j, :wide]
            later, earlier = both_sides(grad_pre)
            d_ref[m] = got_ref[j, wide:] if place else d_mine[j]
            for tap, side in enumerate((later, grad_pre, earlier)):
                where = slice(tap * channels, (tap + 1) * channels)
                term = trans_times(x_ref[m], side[inner])
                total[where] = total[where] + term if place or j else term
            film = grad_pre[inner].astype(F32)
            pre = with_rim(pre_ref, pre_rim, m)[inner]
            scale = 1.0 / gain_ref[m]
            sums[pl.ds(m, 1)] = scale * jnp.sum(film * pre, axis=0, keepdims=True)
            sums[pl.ds(micro + m, 1)] = scale * jnp.sum(film, axis=0, keepdims=True)
    rows_out = split_rows(sums[...])
    extra = rows_out.shape[0]
    chunk = own_refs[0].shape[0]
    parts_count = len(own_refs)
    for part in range(parts_count):
        for k in range(outer):
            start = pl.multiple_of(((mine ^ k) * parts_count + part) * chunk, 8)
            term = total[pl.ds(start, chunk), :]
            if k == 0:
                own_refs[part][...] = term
            else:
                ref = send_refs[part * (outer - 1) + k - 1]
                ref[ref.shape[0] - chunk :] = term.astype(BF16)
                if part == 0:
                    ref[:extra] = rows_out


def gather_kernel(outer, own_ref, mine_ref, *refs):
    got_refs = refs[: outer - 1]
    out_ref, held = refs[outer - 1 :]
    mine = lax.axis_index("bulk") // 2
    chunk = own_ref.shape[0]
    extra = out_ref.shape[0] - chunk
    acc = own_ref[...]
    for k in range(1, outer):
        acc = acc + got_refs[k - 1][extra:].astype(F32)
    out_ref[extra:] = acc.astype(BF16)
    if extra:
        held[mine] = joined_rows(mine_ref[:extra])
        for k in range(1, outer):
            held[mine ^ k] = joined_rows(got_refs[k - 1][:extra])
        rows = held[0]
        for index in range(1, outer):
            rows = rows + held[index]
        out_ref[:extra] = split_rows(rows)


def pair_kernel(a_ref, b_ref, *refs):
    out_ref = refs[-1]
    extra = a_ref.shape[0] - out_ref.shape[0]
    out_ref[...] = (a_ref[extra:].astype(F32) + b_ref[extra:].astype(F32)).astype(BF16)


def spread_kernel(micro, outer, bins, a_ref, b_ref, *refs):
    chunk_refs = refs[:-3]
    out_ref, gain_ref, shift_ref = refs[-3:]
    chunk = chunk_refs[0].shape[0]
    parts_count = len(chunk_refs) // outer
    mine = lax.axis_index("bulk") // 2
    for part in range(parts_count):
        for k in range(outer):
            start = pl.multiple_of(((mine ^ k) * parts_count + part) * chunk, 8)
            out_ref[pl.ds(start, chunk), :] = chunk_refs[part * outer + k][...].astype(F32)
    extra = 4 * micro
    rows = joined_rows(a_ref[:extra]) + joined_rows(b_ref[:extra])
    gain_ref[...] = jnp.zeros_like(gain_ref)
    shift_ref[...] = jnp.zeros_like(shift_ref)
    for m in range(micro):
        gain_ref[bins[m]] += rows[m : m + 1]
        shift_ref[bins[m]] += rows[micro + m : micro + m + 1]


def shape_of(shape, dtype):
    return jax.ShapeDtypeStruct(shape, dtype)


def call(kernel, outs, args, scalars=(), remote=(), scratch=(), flops=1, limit=4):
    vmem = pl.BlockSpec(memory_space=pltpu.VMEM)
    smem = pl.BlockSpec(memory_space=pltpu.SMEM)
    kept = pl.BlockSpec(memory_space=pltpu.HBM)
    several = isinstance(outs, (list, tuple))
    return pl.pallas_call(
        kernel,
        in_specs=[smem] * len(scalars) + [kept] * len(remote) + [vmem] * len(args),
        out_specs=[vmem] * len(outs) if several else vmem,
        out_shape=outs,
        scratch_shapes=scratch,
        compiler_params=pltpu.CompilerParams(vmem_limit_bytes=limit << 20),
        cost_estimate=cost(flops, 1 << 20),
    )(*scalars, *[pltpu.with_memory_space_constraint(v, pltpu.HBM) for v in remote], *args)


def step(activations, weights, film_gain, film_shift, doa_bins, cotangent):
    sections = lax.axis_size("section")
    bulk_count = lax.axis_size("bulk")
    outer = bulk_count // 2
    x = activations[0]
    w_set = weights[0]
    micro, rows, channels = x.shape
    bins_count = film_gain.shape[1]
    gain_table = film_gain.reshape(bins_count, 1, channels)
    shift_table = film_shift.reshape(bins_count, 1, channels)
    pad = 16 * -(-(sections + 1) // 16)
    wide = rows + 2 * pad

    count = micro // 2
    edges = shape_of((micro + count, pad, channels), BF16)
    picked = shape_of((micro, 1, channels), F32)
    near, far, x, cot, w_set, gain_rows, shift_rows = call(
        load_kernel,
        [edges, edges, shape_of(x.shape, BF16), shape_of((count, rows, channels), BF16)]
        + [shape_of(w_set.shape, BF16), picked, picked],
        [],
        remote=[doa_bins, x, cotangent, w_set, gain_table, shift_table],
        scratch=[
            pltpu.SMEM(doa_bins.shape, jnp.int32),
            pltpu.VMEM(gain_table.shape, F32),
            pltpu.VMEM(shift_table.shape, F32),
            pltpu.SemaphoreType.DMA((6,)),
        ],
        limit=8,
    )
    opposite = [(i, (i + 1 if i % 2 else i - 1) % bulk_count) for i in range(bulk_count)]
    far = lax.ppermute(far, "bulk", opposite)
    near = lax.ppermute(near, "bulk", [(i, i ^ 1) for i in range(bulk_count)])

    matmul = 2 * 3 * micro * wide * channels * channels
    picked = shape_of((micro, 1, channels), F32)
    count = micro // 2
    half_main = shape_of((count, rows, channels), F32)
    half_main = shape_of((count, rows, channels), F32)
    send, keep, pre = call(
        forward_kernel,
        [half_main, half_main, shape_of(x.shape, F32)],
        [x, w_set, gain_rows, shift_rows],
        flops=matmul,
        limit=8,
    )

    def to_other(value):
        return lax.ppermute(value, "section", [(i, i ^ 1) for i in range(sections)])

    other_w = to_other(w_set)
    other = to_other(send)
    half_rim = shape_of((count, 2, 2 * pad, channels), F32)
    keep_rim, send_rim, pre_rim, g_rim = call(
        rim_kernel,
        [half_rim, half_rim]
        + [shape_of((micro, 2, 2 * pad, channels), F32), shape_of((count, 2, pad, channels), BF16)],
        [near, far, x, w_set, gain_rows, shift_rows],
        scratch=[pltpu.VMEM((2, *edges.shape), BF16)],
        flops=matmul // 4,
        limit=8,
    )
    other_rim = to_other(send_rim)
    tables = [keep, keep_rim, w_set, other, other_rim, other_w]

    half_wide = shape_of((count, wide, channels), BF16)
    hops = sections // 2 - 1
    cut = 8 * -(-sections // 8)
    inner_shape = shape_of((count, rows - 2 * cut, channels), BF16)
    outer_shape = shape_of((count, 2, 2 * cut, channels), BF16)

    def down(value, pair):
        pairs = [(2 * pair + c, 2 * pair - 2 + c) for c in range(2)]
        return lax.ppermute(value, "section", pairs + [(low, high) for high, low in pairs])

    sources = []
    for hop in range(hops):
        pair = hops - hop
        if hop:
            inner, outer_rows = call(
                functools.partial(relay_kernel, pair),
                [inner_shape, outer_shape],
                tables + sources[-2:],
                flops=matmul,
                limit=8,
            )
            sources += [down(inner, pair), down(outer_rows, pair)]
            continue
        inner = call(
            functools.partial(inner_kernel, pair),
            inner_shape,
            [keep, w_set, other, other_w, cot],
            flops=matmul,
            limit=8,
        )
        inner = down(inner, pair)
        outer_rows = call(
            functools.partial(outer_kernel, pair),
            outer_shape,
            [keep_rim, w_set, other_rim, other_w, cot, g_rim],
            flops=matmul // 2,
            limit=8,
        )
        outer_rows = down(outer_rows, pair)
        sources += [inner, outer_rows]
    grad_own, d_own, away = call(
        functools.partial(chain_kernel, hops),
        [
            half_wide,
            shape_of((count, rows, channels), BF16),
            shape_of((count, wide + rows, channels), BF16),
        ],
        tables + [cot, g_rim] + sources,
        scratch=[pltpu.VMEM(half_wide.shape, F32)],
        flops=matmul,
        limit=12,
    )
    got_away = to_other(away)

    chunk = 3 * channels // outer // PARTS
    extra = 4 * micro
    messages = [shape_of((chunk + (0 if part else extra), channels), BF16) for part in range(PARTS)]
    made = call(
        functools.partial(last_kernel, outer),
        [shape_of(x.shape, BF16)]
        + [shape_of((chunk, channels), F32)] * PARTS
        + [messages[part] for part in range(PARTS) for _ in range(outer - 1)],
        [x, pre, pre_rim, gain_rows, grad_own, d_own, got_away],
        scratch=[
            pltpu.VMEM((3 * channels, channels), F32),
            pltpu.VMEM((2 * micro, channels), F32),
        ],
        flops=matmul,
        limit=16,
    )
    d_local = made[0]
    owns = made[1 : 1 + PARTS]

    def across(value, k):
        pairs = [(i, i ^ (2 * k)) for i in range(bulk_count)]
        return lax.ppermute(value, "bulk", pairs)

    swap = [(i, i ^ 1) for i in range(bulk_count)]
    order = [k for k in range(2, outer)] + [1]
    scattered = []
    for part in range(PARTS):
        sends = made[1 + PARTS + part * (outer - 1) :][: outer - 1]
        got = {k: across(sends[k - 1], k) for k in order}
        scattered.append((sends[0], got))
    summed = []
    for part in range(PARTS):
        first, got = scattered[part]
        partial_sum = call(
            functools.partial(gather_kernel, outer),
            messages[part],
            [owns[part], first] + [got[k] for k in range(1, outer)],
            scratch=[pltpu.VMEM((outer, 2 * micro, channels), F32)],
        )
        summed.append((partial_sum, lax.ppermute(partial_sum, "bulk", swap)))
    spread = []
    for part in range(PARTS):
        done = call(
            pair_kernel, shape_of((chunk, channels), BF16), list(summed[part]) + spread[-outer:][:1]
        )
        got = {k: across(done, k) for k in order}
        spread += [done] + [got[k] for k in range(1, outer)]
    table = shape_of((bins_count, 1, channels), F32)
    d_weights, d_gain, d_shift = call(
        functools.partial(spread_kernel, micro, outer),
        [shape_of((3 * channels, channels), F32), table, table],
        [*summed[0], *spread],
        scalars=[doa_bins],
    )
    return (
        d_local[None],
        d_weights.reshape(1, 3, channels, channels),
        d_gain.reshape(1, bins_count, channels),
        d_shift.reshape(1, bins_count, channels),
    )


def solution(mesh):
    return jax.shard_map(
        step,
        mesh=mesh,
        in_specs=(
            P("section", None, "bulk", None),
            P("section", None, None, None),
            P("section", None, None),
            P("section", None, None),
            P(),
            P(None, "bulk", None),
        ),
        out_specs=(
            P("section", None, "bulk", None),
            P("section", None, None, None),
            P("section", None, None),
            P("section", None, None),
        ),
        check_vma=False,
    )
```

```python
import functools

import jax
import jax.numpy as jnp
from jax import lax
from jax.experimental import pallas as pl
from jax.experimental.pallas import tpu as pltpu
from jax.sharding import PartitionSpec as P


F32 = jnp.float32
BF16 = jnp.bfloat16
PARTS = 2


def cost(flops, moved, trans=0):
    return pl.CostEstimate(flops=flops, bytes_accessed=moved, transcendentals=trans)


def shifted(value, amount):
    rows = value.shape[0]
    return pltpu.roll(value, amount % rows, 0)


def copies(pairs, sems):
    started = []
    for index, (source, target) in enumerate(pairs):
        copy = pltpu.make_async_copy(source, target, sems.at[index])
        copy.start()
        started.append(copy)
    return started


def load_kernel(bins_in, x_in, cot_in, w_in, gain_in, shift_in, *refs):
    near_ref, far_ref, x_ref, cot_ref, w_ref, gain_ref, shift_ref = refs[:7]
    bins, gains, shifts, sems = refs[7:]
    micro, rows = x_ref.shape[:2]
    count = micro // 2
    pad = near_ref.shape[1]
    odd = lax.axis_index("bulk") % 2
    mine = cot_in.at[pl.ds(lax.axis_index("section") % 2 * count, count)]
    pairs = [(x_in, x_ref), (mine, cot_ref), (bins_in, bins), (gain_in, gains)]
    started = copies(pairs + [(shift_in, shifts), (w_in, w_ref)], sems)
    for copy in started[:2]:
        copy.wait()
    near = pl.multiple_of((1 - odd) * (rows - pad), pad)
    far = pl.multiple_of(odd * (rows - pad), pad)
    for out, start in ((near_ref, near), (far_ref, far)):
        out[:micro] = x_ref[:, pl.ds(start, pad), :]
        out[micro:] = cot_ref[:, pl.ds(start, pad), :]
    for copy in started[2:]:
        copy.wait()
    for m in range(micro):
        gain_ref[m] = gains[bins[m]]
        shift_ref[m] = shifts[bins[m]]


def slopes(filmed):
    sig = 0.5 * jnp.tanh(0.5 * filmed) + 0.5
    return sig * (1.0 + filmed * (1.0 - sig))


def taps(value, w_ref):
    wide = value.astype(F32)
    pre = jnp.dot(shifted(wide, 1).astype(BF16), w_ref[0], preferred_element_type=F32)
    pre = pre + jnp.dot(value, w_ref[1], preferred_element_type=F32)
    return pre + jnp.dot(shifted(wide, -1).astype(BF16), w_ref[2], preferred_element_type=F32)


def turn(half, micro, place):
    start = half if place == 0 else 1 - half
    return [start * (micro // 2) + j for j in range(micro // 2)]


def forward_kernel(x_ref, w_ref, gain_ref, shift_ref, send_ref, keep_ref, pre_ref):
    micro = x_ref.shape[0]
    half = lax.axis_index("section") % 2
    for place, out in ((1, send_ref), (0, keep_ref)):
        for j, m in enumerate(turn(half, micro, place)):
            pre = taps(x_ref[m], w_ref)
            out[j] = slopes(pre * gain_ref[m] + shift_ref[m]) * gain_ref[m]
            pre_ref[m] = pre


def rim_kernel(near_ref, far_ref, x_ref, w_ref, gain_ref, shift_ref, *refs):
    keep_ref, send_ref, pre_ref, g_ref, halo = refs
    micro, rows = x_ref.shape[:2]
    pad = near_ref.shape[1]
    odd = lax.axis_index("bulk") % 2
    half = lax.axis_index("section") % 2

    @pl.when(odd == 1)
    def _():
        halo[0] = near_ref[...]
        halo[1] = far_ref[...]

    @pl.when(odd == 0)
    def _():
        halo[0] = far_ref[...]
        halo[1] = near_ref[...]

    parts = []
    order = turn(half, micro, 0) + turn(half, micro, 1)
    for m in order:
        parts += [halo[0, m], x_ref[m, :pad], x_ref[m, rows - pad :], halo[1, m]]
    for j in range(micro // 2):
        g_ref[j, 0] = halo[0, micro + j]
        g_ref[j, 1] = halo[1, micro + j]
    pre = taps(jnp.concatenate(parts, axis=0), w_ref)
    for index, m in enumerate(order):
        out = (keep_ref, send_ref)[index // (micro // 2)]
        for side in range(2):
            start = (2 * index + side) * 2 * pad
            here = pre[start : start + 2 * pad]
            pre_ref[m, side] = here
            filmed = here * gain_ref[m] + shift_ref[m]
            out[index % (micro // 2), side] = slopes(filmed) * gain_ref[m]


def with_rim(main, rim, m):
    pad = rim.shape[2] // 2
    rows = main.shape[1]
    parts = [rim[m, 0, : pad + 8], main[m, 8 : rows - 8], rim[m, 1, pad - 8 :]]
    return jnp.concatenate(parts, axis=0)


def times_trans(left, right):
    return lax.dot_general(left, right, (((1,), (1,)), ((), ())), preferred_element_type=F32)


def trans_times(left, right):
    return lax.dot_general(left, right, (((0,), (0,)), ((), ())), preferred_element_type=F32)


def both_sides(grad_pre):
    wide = grad_pre.astype(F32)
    return shifted(wide, -1).astype(BF16), shifted(wide, 1).astype(BF16)


def backward(g, slope, w_ref):
    grad_pre = (g * slope).astype(BF16)
    later, earlier = both_sides(grad_pre)
    d_in = g + times_trans(later, w_ref[0]) + times_trans(grad_pre, w_ref[1])
    d_in = d_in + times_trans(earlier, w_ref[2])
    return grad_pre, d_in.astype(BF16), d_in


def top_gradient(cot_ref, rim_ref, m):
    return jnp.concatenate([rim_ref[m, 0], cot_ref[m], rim_ref[m, 1]], axis=0)


def factors(refs, j):
    main, rim, w_ref = refs
    return with_rim(main, rim, j), w_ref


def by_half(pair, own, other, run):
    section_id = lax.axis_index("section")
    for half in range(2):
        upper, lower = (own, other) if half else (other, own)
        here = section_id % 2 == half if pair is None else section_id == 2 * pair + half

        @pl.when(here)
        def _(upper=upper, lower=lower, half=half):
            run(upper, lower, half)


def inner_kernel(pair, *refs):
    own, other, cot_ref, d_ref = refs[:2], refs[2:4], refs[4], refs[5]
    rows = cot_ref.shape[1]
    cut = (rows - d_ref.shape[1]) // 2

    def run(upper, lower, half):
        for j in range(d_ref.shape[0]):
            g = cot_ref[j].astype(F32)
            middle = backward(g, upper[0][j], upper[1])[1].astype(F32)
            d_ref[j] = backward(middle, lower[0][j], lower[1])[2][cut : rows - cut].astype(BF16)

    by_half(pair, own, other, run)


def outer_kernel(pair, *refs):
    own, other, cot_ref, rim_ref, d_ref = refs[:2], refs[2:4], refs[4], refs[5], refs[6]
    count, rows = cot_ref.shape[:2]
    pad = rim_ref.shape[2]
    cut = d_ref.shape[2] // 2

    def stacked(ref):
        return jnp.concatenate([ref[j, side] for j in range(count) for side in range(2)], axis=0)

    def run(upper, lower, half):
        parts = []
        for j in range(count):
            parts += [rim_ref[j, 0], cot_ref[j, :pad], cot_ref[j, rows - pad :], rim_ref[j, 1]]
        g = jnp.concatenate(parts, axis=0).astype(F32)
        middle = backward(g, stacked(upper[0]), upper[1])[1].astype(F32)
        d_in = backward(middle, stacked(lower[0]), lower[1])[2]
        for j in range(count):
            for side in range(2):
                start = (2 * j + side) * 2 * pad + pad - cut
                d_ref[j, side] = d_in[start : start + 2 * cut].astype(BF16)

    by_half(pair, own, other, run)


def arrived(inner_ref, outer_ref, j, wide):
    rest = wide - inner_ref.shape[1] - 2 * outer_ref.shape[2]
    fill = jnp.zeros((rest // 2, inner_ref.shape[2]), F32)
    parts = [outer_ref[j, 0], inner_ref[j], outer_ref[j, 1]]
    return jnp.concatenate([fill] + [part.astype(F32) for part in parts] + [fill], axis=0)


def relay_kernel(pair, *refs):
    own, other, got_refs = refs[:3], refs[3:6], refs[6:8]
    inner_ref, outer_ref = refs[8:]
    cut = outer_ref.shape[2] // 2
    size = inner_ref.shape[1]
    wide = own[0].shape[1] + own[1].shape[2]

    def run(upper, lower, half):
        for j in range(inner_ref.shape[0]):
            g = arrived(*got_refs, j, wide)
            middle = backward(g, *factors(upper, j))[1].astype(F32)
            d_in = backward(middle, *factors(lower, j))[2]
            start = (wide - size) // 2
            inner_ref[j] = d_in[start : start + size].astype(BF16)
            outer_ref[j, 0] = d_in[start - 2 * cut : start].astype(BF16)
            outer_ref[j, 1] = d_in[start + size : start + size + 2 * cut].astype(BF16)

    by_half(pair, own, other, run)


def chain_kernel(hops, *refs):
    own, other, top_refs = refs[:3], refs[3:6], refs[6:8]
    got_refs = refs[8 : 8 + 2 * hops]
    grad_ref, d_ref, send_ref, g_now = refs[8 + 2 * hops :]
    rows, wide = d_ref.shape[1], grad_ref.shape[1]
    pad = (wide - rows) // 2
    inner = slice(pad, pad + rows)
    section_id = lax.axis_index("section")

    @pl.when(section_id // 2 == hops)
    def _():
        for j in range(d_ref.shape[0]):
            g_now[j] = top_gradient(*top_refs, j).astype(F32)

    for index in range(hops):

        @pl.when(section_id // 2 == hops - 1 - index)
        def _(index=index):
            for j in range(d_ref.shape[0]):
                g_now[j] = arrived(*got_refs[2 * index : 2 * index + 2], j, wide)

    def run(upper, lower, half):
        for j in range(d_ref.shape[0]):
            first = backward(g_now[j], *factors(upper, j))
            second = backward(first[1].astype(F32), *factors(lower, j))
            mine, away = (first, second) if half else (second, first)
            grad_ref[j] = mine[0]
            d_ref[j] = mine[1][inner]
            send_ref[j, :wide] = away[0]
            send_ref[j, wide:] = away[1][inner]

    by_half(None, own, other, run)


def split_rows(rows):
    high = rows.astype(BF16).astype(F32)
    low = (rows - high).astype(BF16).astype(F32)
    return jnp.concatenate([high, low], axis=0).astype(BF16)


def joined_rows(pair):
    wide = pair.astype(F32)
    half = wide.shape[0] // 2
    return wide[:half] + wide[half:]


def add_terms(place, source, wide, x_ref, pre_ref, pre_rim, gain_ref, total, sums):
    micro, rows, channels = x_ref.shape
    pad = (wide - rows) // 2
    inner = slice(pad, pad + rows)
    half = lax.axis_index("section") % 2
    for j, m in enumerate(turn(half, micro, place)):
        grad_pre = source[j, :wide]
        later, earlier = both_sides(grad_pre)
        for tap, side in enumerate((later, grad_pre, earlier)):
            where = slice(tap * channels, (tap + 1) * channels)
            term = trans_times(x_ref[m], side[inner])
            total[where] = total[where] + term if place or j else term
        film = grad_pre[inner].astype(F32)
        pre = with_rim(pre_ref, pre_rim, m)[inner]
        scale = 1.0 / gain_ref[m]
        sums[pl.ds(m, 1)] = scale * jnp.sum(film * pre, axis=0, keepdims=True)
        sums[pl.ds(micro + m, 1)] = scale * jnp.sum(film, axis=0, keepdims=True)


def own_kernel(x_ref, pre_ref, pre_rim, gain_ref, grad_ref, total, sums):
    sums[...] = jnp.zeros_like(sums)
    wide = grad_ref.shape[1]
    add_terms(0, grad_ref, wide, x_ref, pre_ref, pre_rim, gain_ref, total, sums)


def last_kernel(outer, *refs):
    x_ref, pre_ref, pre_rim, gain_ref, total_in, sums_in, d_mine, got_ref, d_ref = refs[:9]
    own_refs = refs[9 : 9 + PARTS]
    send_refs = refs[9 + PARTS : -2]
    total, sums = refs[-2:]
    micro, rows, _ = x_ref.shape
    wide = got_ref.shape[1] - rows
    mine = lax.axis_index("bulk") // 2
    half = lax.axis_index("section") % 2
    total[...] = total_in[...]
    sums[...] = sums_in[...]
    add_terms(1, got_ref, wide, x_ref, pre_ref, pre_rim, gain_ref, total, sums)
    for j, m in enumerate(turn(half, micro, 0)):
        d_ref[m] = d_mine[j]
    for j, m in enumerate(turn(half, micro, 1)):
        d_ref[m] = got_ref[j, wide:]
    rows_out = split_rows(sums[...])
    extra = rows_out.shape[0]
    chunk = own_refs[0].shape[0]
    parts_count = len(own_refs)
    for part in range(parts_count):
        for k in range(outer):
            start = pl.multiple_of(((mine ^ k) * parts_count + part) * chunk, 8)
            term = total[pl.ds(start, chunk), :]
            if k == 0:
                own_refs[part][...] = term
            else:
                ref = send_refs[part * (outer - 1) + k - 1]
                ref[ref.shape[0] - chunk :] = term.astype(BF16)
                if part == 0:
                    ref[:extra] = rows_out


def gather_kernel(outer, own_ref, mine_ref, *refs):
    got_refs = refs[: outer - 1]
    out_ref, held = refs[outer - 1 :]
    mine = lax.axis_index("bulk") // 2
    chunk = own_ref.shape[0]
    extra = out_ref.shape[0] - chunk
    acc = own_ref[...]
    for k in range(1, outer):
        acc = acc + got_refs[k - 1][extra:].astype(F32)
    out_ref[extra:] = acc.astype(BF16)
    if extra:
        held[mine] = joined_rows(mine_ref[:extra])
        for k in range(1, outer):
            held[mine ^ k] = joined_rows(got_refs[k - 1][:extra])
        rows = held[0]
        for index in range(1, outer):
            rows = rows + held[index]
        out_ref[:extra] = split_rows(rows)


def pair_kernel(a_ref, b_ref, *refs):
    out_ref = refs[-1]
    extra = a_ref.shape[0] - out_ref.shape[0]
    out_ref[...] = (a_ref[extra:].astype(F32) + b_ref[extra:].astype(F32)).astype(BF16)


def bins_kernel(micro, bins, a_ref, b_ref, gain_ref, shift_ref):
    extra = 4 * micro
    rows = joined_rows(a_ref[:extra]) + joined_rows(b_ref[:extra])
    gain_ref[...] = jnp.zeros_like(gain_ref)
    shift_ref[...] = jnp.zeros_like(shift_ref)
    for m in range(micro):
        gain_ref[bins[m]] += rows[m : m + 1]
        shift_ref[bins[m]] += rows[micro + m : micro + m + 1]


def spread_kernel(outer, part, *refs):
    chunk_refs = refs[-3 - outer : -3]
    out_ref, held, sems = refs[-3:]
    chunk = chunk_refs[0].shape[0]
    mine = lax.axis_index("bulk") // 2
    pairs = []
    for k in range(outer):
        held[k] = chunk_refs[k][...].astype(F32)
        start = pl.multiple_of(((mine ^ k) * PARTS + part) * chunk, 8)
        pairs.append((held.at[k], out_ref.at[pl.ds(start, chunk), :]))
    for copy in copies(pairs, sems):
        copy.wait()


def written(chunks, outer, part, before, rows):
    chunk, channels = chunks[0].shape
    hbm = pl.BlockSpec(memory_space=pltpu.HBM)
    return pl.pallas_call(
        functools.partial(spread_kernel, outer, part),
        in_specs=[hbm] * len(before) + [pl.BlockSpec(memory_space=pltpu.VMEM)] * outer,
        out_specs=hbm,
        out_shape=shape_of((rows, channels), F32),
        scratch_shapes=[
            pltpu.VMEM((outer, chunk, channels), F32),
            pltpu.SemaphoreType.DMA((outer,)),
        ],
        input_output_aliases={0: 0} if before else {},
        compiler_params=pltpu.CompilerParams(vmem_limit_bytes=4 << 20),
        cost_estimate=cost(1, 1 << 20),
        name="spread",
    )(*before, *chunks)


def shape_of(shape, dtype):
    return jax.ShapeDtypeStruct(shape, dtype)


def call(kernel, outs, args, scalars=(), remote=(), scratch=(), flops=1, limit=4):
    vmem = pl.BlockSpec(memory_space=pltpu.VMEM)
    smem = pl.BlockSpec(memory_space=pltpu.SMEM)
    kept = pl.BlockSpec(memory_space=pltpu.HBM)
    several = isinstance(outs, (list, tuple))
    return pl.pallas_call(
        kernel,
        in_specs=[smem] * len(scalars) + [kept] * len(remote) + [vmem] * len(args),
        out_specs=[vmem] * len(outs) if several else vmem,
        out_shape=outs,
        scratch_shapes=scratch,
        compiler_params=pltpu.CompilerParams(vmem_limit_bytes=limit << 20),
        cost_estimate=cost(flops, 1 << 20),
    )(*scalars, *[pltpu.with_memory_space_constraint(v, pltpu.HBM) for v in remote], *args)


def step(activations, weights, film_gain, film_shift, doa_bins, cotangent):
    sections = lax.axis_size("section")
    bulk_count = lax.axis_size("bulk")
    outer = bulk_count // 2
    x = activations[0]
    w_set = weights[0]
    micro, rows, channels = x.shape
    bins_count = film_gain.shape[1]
    gain_table = film_gain.reshape(bins_count, 1, channels)
    shift_table = film_shift.reshape(bins_count, 1, channels)
    pad = 16 * -(-(sections + 1) // 16)
    wide = rows + 2 * pad

    count = micro // 2
    edges = shape_of((micro + count, pad, channels), BF16)
    picked = shape_of((micro, 1, channels), F32)
    near, far, x, cot, w_set, gain_rows, shift_rows = call(
        load_kernel,
        [edges, edges, shape_of(x.shape, BF16), shape_of((count, rows, channels), BF16)]
        + [shape_of(w_set.shape, BF16), picked, picked],
        [],
        remote=[doa_bins, x, cotangent, w_set, gain_table, shift_table],
        scratch=[
            pltpu.SMEM(doa_bins.shape, jnp.int32),
            pltpu.VMEM(gain_table.shape, F32),
            pltpu.VMEM(shift_table.shape, F32),
            pltpu.SemaphoreType.DMA((6,)),
        ],
        limit=8,
    )
    opposite = [(i, (i + 1 if i % 2 else i - 1) % bulk_count) for i in range(bulk_count)]
    far = lax.ppermute(far, "bulk", opposite)
    near = lax.ppermute(near, "bulk", [(i, i ^ 1) for i in range(bulk_count)])

    matmul = 2 * 3 * micro * wide * channels * channels
    picked = shape_of((micro, 1, channels), F32)
    count = micro // 2
    half_main = shape_of((count, rows, channels), F32)
    half_main = shape_of((count, rows, channels), F32)
    send, keep, pre = call(
        forward_kernel,
        [half_main, half_main, shape_of(x.shape, F32)],
        [x, w_set, gain_rows, shift_rows],
        flops=matmul,
        limit=8,
    )

    def to_other(value):
        return lax.ppermute(value, "section", [(i, i ^ 1) for i in range(sections)])

    other_w = to_other(w_set)
    other = to_other(send)
    half_rim = shape_of((count, 2, 2 * pad, channels), F32)
    keep_rim, send_rim, pre_rim, g_rim = call(
        rim_kernel,
        [half_rim, half_rim]
        + [shape_of((micro, 2, 2 * pad, channels), F32), shape_of((count, 2, pad, channels), BF16)],
        [near, far, x, w_set, gain_rows, shift_rows],
        scratch=[pltpu.VMEM((2, *edges.shape), BF16)],
        flops=matmul // 4,
        limit=8,
    )
    other_rim = to_other(send_rim)
    tables = [keep, keep_rim, w_set, other, other_rim, other_w]

    half_wide = shape_of((count, wide, channels), BF16)
    hops = sections // 2 - 1
    cut = 8 * -(-sections // 8)
    inner_shape = shape_of((count, rows - 2 * cut, channels), BF16)
    outer_shape = shape_of((count, 2, 2 * cut, channels), BF16)

    def down(value, pair):
        pairs = [(2 * pair + c, 2 * pair - 2 + c) for c in range(2)]
        return lax.ppermute(value, "section", pairs + [(low, high) for high, low in pairs])

    sources = []
    for hop in range(hops):
        pair = hops - hop
        if hop:
            inner, outer_rows = call(
                functools.partial(relay_kernel, pair),
                [inner_shape, outer_shape],
                tables + sources[-2:],
                flops=matmul,
                limit=8,
            )
            sources += [down(inner, pair), down(outer_rows, pair)]
            continue
        inner = call(
            functools.partial(inner_kernel, pair),
            inner_shape,
            [keep, w_set, other, other_w, cot],
            flops=matmul,
            limit=8,
        )
        inner = down(inner, pair)
        outer_rows = call(
            functools.partial(outer_kernel, pair),
            outer_shape,
            [keep_rim, w_set, other_rim, other_w, cot, g_rim],
            flops=matmul // 2,
            limit=8,
        )
        outer_rows = down(outer_rows, pair)
        sources += [inner, outer_rows]
    grad_own, d_own, away = call(
        functools.partial(chain_kernel, hops),
        [
            half_wide,
            shape_of((count, rows, channels), BF16),
            shape_of((count, wide + rows, channels), BF16),
        ],
        tables + [cot, g_rim] + sources,
        scratch=[pltpu.VMEM(half_wide.shape, F32)],
        flops=matmul,
        limit=12,
    )
    got_away = to_other(away)
    shared = [x, pre, pre_rim, gain_rows]
    total_own, sums_own = call(
        own_kernel,
        [shape_of((3 * channels, channels), F32), shape_of((2 * micro, channels), F32)],
        shared + [grad_own],
        flops=matmul // 2,
        limit=8,
    )

    chunk = 3 * channels // outer // PARTS
    extra = 4 * micro
    messages = [shape_of((chunk + (0 if part else extra), channels), BF16) for part in range(PARTS)]
    made = call(
        functools.partial(last_kernel, outer),
        [shape_of(x.shape, BF16)]
        + [shape_of((chunk, channels), F32)] * PARTS
        + [messages[part] for part in range(PARTS) for _ in range(outer - 1)],
        shared + [total_own, sums_own, d_own, got_away],
        scratch=[
            pltpu.VMEM((3 * channels, channels), F32),
            pltpu.VMEM((2 * micro, channels), F32),
        ],
        flops=matmul,
        limit=16,
    )
    d_local = made[0]
    owns = made[1 : 1 + PARTS]

    def across(value, k):
        pairs = [(i, i ^ (2 * k)) for i in range(bulk_count)]
        return lax.ppermute(value, "bulk", pairs)

    swap = [(i, i ^ 1) for i in range(bulk_count)]
    order = [k for k in range(2, outer)] + [1]
    scattered = []
    for part in range(PARTS):
        sends = made[1 + PARTS + part * (outer - 1) :][: outer - 1]
        got = {k: across(sends[k - 1], k) for k in order}
        scattered.append((sends[0], got))
    summed = []
    for part in range(PARTS):
        first, got = scattered[part]
        partial_sum = call(
            functools.partial(gather_kernel, outer),
            messages[part],
            [owns[part], first] + [got[k] for k in range(1, outer)],
            scratch=[pltpu.VMEM((outer, 2 * micro, channels), F32)],
        )
        summed.append((partial_sum, lax.ppermute(partial_sum, "bulk", swap)))
    spread = []
    for part in range(PARTS):
        done = call(
            pair_kernel, shape_of((chunk, channels), BF16), list(summed[part]) + spread[-outer:][:1]
        )
        got = {k: across(done, k) for k in order}
        spread += [done] + [got[k] for k in range(1, outer)]
    table = shape_of((bins_count, 1, channels), F32)
    d_gain, d_shift = call(
        functools.partial(bins_kernel, micro), [table, table], list(summed[0]), scalars=[doa_bins]
    )
    before = []
    for part in range(PARTS):
        chunks = spread[part * outer : (part + 1) * outer]
        before = [written(chunks, outer, part, before, 3 * channels)]
    d_weights = before[0]
    return (
        d_local[None],
        d_weights.reshape(1, 3, channels, channels),
        d_gain.reshape(1, bins_count, channels),
        d_shift.reshape(1, bins_count, channels),
    )


def solution(mesh):
    return jax.shard_map(
        step,
        mesh=mesh,
        in_specs=(
            P("section", None, "bulk", None),
            P("section", None, None, None),
            P("section", None, None),
            P("section", None, None),
            P(),
            P(None, "bulk", None),
        ),
        out_specs=(
            P("section", None, "bulk", None),
            P("section", None, None, None),
            P("section", None, None),
            P("section", None, None),
        ),
        check_vma=False,
    )
```

```python
import functools

import jax
import jax.numpy as jnp
from jax import lax
from jax.experimental import pallas as pl
from jax.experimental.pallas import tpu as pltpu
from jax.sharding import PartitionSpec as P


F32 = jnp.float32
BF16 = jnp.bfloat16
PARTS = 2


def cost(flops, moved, trans=0):
    return pl.CostEstimate(flops=flops, bytes_accessed=moved, transcendentals=trans)


def shifted(value, amount):
    rows = value.shape[0]
    return pltpu.roll(value, amount % rows, 0)


def copies(pairs, sems):
    started = []
    for index, (source, target) in enumerate(pairs):
        copy = pltpu.make_async_copy(source, target, sems.at[index])
        copy.start()
        started.append(copy)
    return started


def load_kernel(bins_in, x_in, cot_in, w_in, gain_in, shift_in, *refs):
    near_ref, far_ref, x_ref, cot_ref, w_ref, gain_ref, shift_ref = refs[:7]
    bins, gains, shifts, sems = refs[7:]
    micro, rows = x_ref.shape[:2]
    count = micro // 2
    pad = near_ref.shape[1]
    odd = lax.axis_index("bulk") % 2
    mine = cot_in.at[pl.ds(lax.axis_index("section") % 2 * count, count)]
    pairs = [(x_in, x_ref), (mine, cot_ref), (bins_in, bins), (gain_in, gains)]
    started = copies(pairs + [(shift_in, shifts), (w_in, w_ref)], sems)
    for copy in started[:2]:
        copy.wait()
    near = pl.multiple_of((1 - odd) * (rows - pad), pad)
    far = pl.multiple_of(odd * (rows - pad), pad)
    for out, start in ((near_ref, near), (far_ref, far)):
        out[:micro] = x_ref[:, pl.ds(start, pad), :]
        out[micro:] = cot_ref[:, pl.ds(start, pad), :]
    for copy in started[2:]:
        copy.wait()
    for m in range(micro):
        gain_ref[m] = gains[bins[m]]
        shift_ref[m] = shifts[bins[m]]


def slopes(filmed):
    sig = 0.5 * jnp.tanh(0.5 * filmed) + 0.5
    return sig * (1.0 + filmed * (1.0 - sig))


def taps(value, w_ref):
    wide = value.astype(F32)
    pre = jnp.dot(shifted(wide, 1).astype(BF16), w_ref[0], preferred_element_type=F32)
    pre = pre + jnp.dot(value, w_ref[1], preferred_element_type=F32)
    return pre + jnp.dot(shifted(wide, -1).astype(BF16), w_ref[2], preferred_element_type=F32)


def turn(half, micro, place):
    start = half if place == 0 else 1 - half
    return [start * (micro // 2) + j for j in range(micro // 2)]


def forward_kernel(x_ref, w_ref, gain_ref, shift_ref, send_ref, keep_ref, pre_ref):
    micro = x_ref.shape[0]
    half = lax.axis_index("section") % 2
    for place, out in ((1, send_ref), (0, keep_ref)):
        for j, m in enumerate(turn(half, micro, place)):
            pre = taps(x_ref[m], w_ref)
            out[j] = slopes(pre * gain_ref[m] + shift_ref[m]) * gain_ref[m]
            pre_ref[m] = pre


def rim_kernel(near_ref, far_ref, x_ref, w_ref, gain_ref, shift_ref, *refs):
    keep_ref, send_ref, pre_ref, g_ref, halo = refs
    micro, rows = x_ref.shape[:2]
    pad = near_ref.shape[1]
    odd = lax.axis_index("bulk") % 2
    half = lax.axis_index("section") % 2

    @pl.when(odd == 1)
    def _():
        halo[0] = near_ref[...]
        halo[1] = far_ref[...]

    @pl.when(odd == 0)
    def _():
        halo[0] = far_ref[...]
        halo[1] = near_ref[...]

    parts = []
    order = turn(half, micro, 0) + turn(half, micro, 1)
    for m in order:
        parts += [halo[0, m], x_ref[m, :pad], x_ref[m, rows - pad :], halo[1, m]]
    for j in range(micro // 2):
        g_ref[j, 0] = halo[0, micro + j]
        g_ref[j, 1] = halo[1, micro + j]
    pre = taps(jnp.concatenate(parts, axis=0), w_ref)
    for index, m in enumerate(order):
        out = (keep_ref, send_ref)[index // (micro // 2)]
        for side in range(2):
            start = (2 * index + side) * 2 * pad
            here = pre[start : start + 2 * pad]
            pre_ref[m, side] = here
            filmed = here * gain_ref[m] + shift_ref[m]
            out[index % (micro // 2), side] = slopes(filmed) * gain_ref[m]


def with_rim(main, rim, m):
    pad = rim.shape[2] // 2
    rows = main.shape[1]
    parts = [rim[m, 0, : pad + 8], main[m, 8 : rows - 8], rim[m, 1, pad - 8 :]]
    return jnp.concatenate(parts, axis=0)


def times_trans(left, right):
    return lax.dot_general(left, right, (((1,), (1,)), ((), ())), preferred_element_type=F32)


def trans_times(left, right):
    return lax.dot_general(left, right, (((0,), (0,)), ((), ())), preferred_element_type=F32)


def both_sides(grad_pre):
    wide = grad_pre.astype(F32)
    return shifted(wide, -1).astype(BF16), shifted(wide, 1).astype(BF16)


def backward(g, slope, w_ref):
    grad_pre = (g * slope).astype(BF16)
    later, earlier = both_sides(grad_pre)
    d_in = g + times_trans(later, w_ref[0]) + times_trans(grad_pre, w_ref[1])
    d_in = d_in + times_trans(earlier, w_ref[2])
    return grad_pre, d_in.astype(BF16), d_in


def top_gradient(cot_ref, rim_ref, m):
    return jnp.concatenate([rim_ref[m, 0], cot_ref[m], rim_ref[m, 1]], axis=0)


def factors(refs, j):
    main, rim, w_ref = refs
    return with_rim(main, rim, j), w_ref


def by_half(pair, own, other, run):
    section_id = lax.axis_index("section")
    for half in range(2):
        upper, lower = (own, other) if half else (other, own)
        here = section_id % 2 == half if pair is None else section_id == 2 * pair + half

        @pl.when(here)
        def _(upper=upper, lower=lower, half=half):
            run(upper, lower, half)


def inner_kernel(pair, *refs):
    own, other, cot_ref, d_ref = refs[:2], refs[2:4], refs[4], refs[5]
    rows = cot_ref.shape[1]
    cut = (rows - d_ref.shape[1]) // 2

    def run(upper, lower, half):
        for j in range(d_ref.shape[0]):
            g = cot_ref[j].astype(F32)
            middle = backward(g, upper[0][j], upper[1])[1].astype(F32)
            d_ref[j] = backward(middle, lower[0][j], lower[1])[2][cut : rows - cut].astype(BF16)

    by_half(pair, own, other, run)


def outer_kernel(pair, *refs):
    own, other, cot_ref, rim_ref, d_ref = refs[:2], refs[2:4], refs[4], refs[5], refs[6]
    count, rows = cot_ref.shape[:2]
    pad = rim_ref.shape[2]
    cut = d_ref.shape[2] // 2

    def stacked(ref):
        return jnp.concatenate([ref[j, side] for j in range(count) for side in range(2)], axis=0)

    def run(upper, lower, half):
        parts = []
        for j in range(count):
            parts += [rim_ref[j, 0], cot_ref[j, :pad], cot_ref[j, rows - pad :], rim_ref[j, 1]]
        g = jnp.concatenate(parts, axis=0).astype(F32)
        middle = backward(g, stacked(upper[0]), upper[1])[1].astype(F32)
        d_in = backward(middle, stacked(lower[0]), lower[1])[2]
        for j in range(count):
            for side in range(2):
                start = (2 * j + side) * 2 * pad + pad - cut
                d_ref[j, side] = d_in[start : start + 2 * cut].astype(BF16)

    by_half(pair, own, other, run)


def arrived(inner_ref, outer_ref, j, wide):
    rest = wide - inner_ref.shape[1] - 2 * outer_ref.shape[2]
    fill = jnp.zeros((rest // 2, inner_ref.shape[2]), F32)
    parts = [outer_ref[j, 0], inner_ref[j], outer_ref[j, 1]]
    return jnp.concatenate([fill] + [part.astype(F32) for part in parts] + [fill], axis=0)


def relay_kernel(pair, *refs):
    own, other, got_refs = refs[:3], refs[3:6], refs[6:8]
    inner_ref, outer_ref = refs[8:]
    cut = outer_ref.shape[2] // 2
    size = inner_ref.shape[1]
    wide = own[0].shape[1] + own[1].shape[2]

    def run(upper, lower, half):
        for j in range(inner_ref.shape[0]):
            g = arrived(*got_refs, j, wide)
            middle = backward(g, *factors(upper, j))[1].astype(F32)
            d_in = backward(middle, *factors(lower, j))[2]
            start = (wide - size) // 2
            inner_ref[j] = d_in[start : start + size].astype(BF16)
            outer_ref[j, 0] = d_in[start - 2 * cut : start].astype(BF16)
            outer_ref[j, 1] = d_in[start + size : start + size + 2 * cut].astype(BF16)

    by_half(pair, own, other, run)


def chain_kernel(hops, *refs):
    own, other, top_refs = refs[:3], refs[3:6], refs[6:8]
    got_refs = refs[8 : 8 + 2 * hops]
    grad_ref, d_ref, send_ref, g_now = refs[8 + 2 * hops :]
    rows, wide = d_ref.shape[1], grad_ref.shape[1]
    pad = (wide - rows) // 2
    inner = slice(pad, pad + rows)
    section_id = lax.axis_index("section")

    @pl.when(section_id // 2 == hops)
    def _():
        for j in range(d_ref.shape[0]):
            g_now[j] = top_gradient(*top_refs, j).astype(F32)

    for index in range(hops):

        @pl.when(section_id // 2 == hops - 1 - index)
        def _(index=index):
            for j in range(d_ref.shape[0]):
                g_now[j] = arrived(*got_refs[2 * index : 2 * index + 2], j, wide)

    def run(upper, lower, half):
        for j in range(d_ref.shape[0]):
            first = backward(g_now[j], *factors(upper, j))
            second = backward(first[1].astype(F32), *factors(lower, j))
            mine, away = (first, second) if half else (second, first)
            grad_ref[j] = mine[0]
            d_ref[j] = mine[1][inner]
            send_ref[j, :wide] = away[0]
            send_ref[j, wide:] = away[1][inner]

    by_half(None, own, other, run)


def split_rows(rows):
    high = rows.astype(BF16).astype(F32)
    low = (rows - high).astype(BF16).astype(F32)
    return jnp.concatenate([high, low], axis=0).astype(BF16)


def joined_rows(pair):
    wide = pair.astype(F32)
    half = wide.shape[0] // 2
    return wide[:half] + wide[half:]


def add_terms(place, source, wide, x_ref, pre_ref, pre_rim, gain_ref, total, sums, start=None):
    micro, rows, channels = x_ref.shape
    pad = (wide - rows) // 2
    inner = slice(pad, pad + rows)
    half = lax.axis_index("section") % 2
    for j, m in enumerate(turn(half, micro, place)):
        grad_pre = source[j, :wide]
        later, earlier = both_sides(grad_pre)
        for tap, side in enumerate((later, grad_pre, earlier)):
            where = slice(tap * channels, (tap + 1) * channels)
            term = trans_times(x_ref[m], side[inner])
            if j:
                term = total[where] + term
            elif start is not None:
                term = start[where] + term
            total[where] = term
        film = grad_pre[inner].astype(F32)
        pre = with_rim(pre_ref, pre_rim, m)[inner]
        scale = 1.0 / gain_ref[m]
        sums[pl.ds(m, 1)] = scale * jnp.sum(film * pre, axis=0, keepdims=True)
        sums[pl.ds(micro + m, 1)] = scale * jnp.sum(film, axis=0, keepdims=True)


def own_kernel(x_ref, pre_ref, pre_rim, gain_ref, grad_ref, total, sums):
    sums[...] = jnp.zeros_like(sums)
    wide = grad_ref.shape[1]
    add_terms(0, grad_ref, wide, x_ref, pre_ref, pre_rim, gain_ref, total, sums)


def last_kernel(outer, *refs):
    x_ref, pre_ref, pre_rim, gain_ref, total_in, sums_in, got_ref = refs[:7]
    own_refs = refs[7 : 7 + PARTS]
    send_refs = refs[7 + PARTS : -2]
    total, sums = refs[-2:]
    _, rows, _ = x_ref.shape
    wide = got_ref.shape[1] - rows
    mine = lax.axis_index("bulk") // 2
    sums[...] = sums_in[...]
    add_terms(1, got_ref, wide, x_ref, pre_ref, pre_rim, gain_ref, total, sums, total_in)
    rows_out = split_rows(sums[...])
    extra = rows_out.shape[0]
    chunk = own_refs[0].shape[0]
    parts_count = len(own_refs)
    for part in range(parts_count):
        for k in range(outer):
            start = pl.multiple_of(((mine ^ k) * parts_count + part) * chunk, 8)
            term = total[pl.ds(start, chunk), :]
            if k == 0:
                own_refs[part][...] = term
            else:
                ref = send_refs[part * (outer - 1) + k - 1]
                ref[ref.shape[0] - chunk :] = term.astype(BF16)
                if part == 0:
                    ref[:extra] = rows_out


def gather_kernel(outer, own_ref, mine_ref, *refs):
    got_refs = refs[: outer - 1]
    out_ref, held = refs[outer - 1 :]
    mine = lax.axis_index("bulk") // 2
    chunk = own_ref.shape[0]
    extra = out_ref.shape[0] - chunk
    acc = own_ref[...]
    for k in range(1, outer):
        acc = acc + got_refs[k - 1][extra:].astype(F32)
    out_ref[extra:] = acc.astype(BF16)
    if extra:
        held[mine] = joined_rows(mine_ref[:extra])
        for k in range(1, outer):
            held[mine ^ k] = joined_rows(got_refs[k - 1][:extra])
        rows = held[0]
        for index in range(1, outer):
            rows = rows + held[index]
        out_ref[:extra] = split_rows(rows)


def pair_kernel(a_ref, b_ref, *refs):
    out_ref = refs[-1]
    extra = a_ref.shape[0] - out_ref.shape[0]
    out_ref[...] = (a_ref[extra:].astype(F32) + b_ref[extra:].astype(F32)).astype(BF16)


def result_kernel(d_mine, got_ref, out_ref, sems):
    count, rows = d_mine.shape[:2]
    half = lax.axis_index("section") % 2
    away = got_ref.at[:, pl.ds(got_ref.shape[1] - rows, rows), :]
    pairs = [(d_mine, out_ref.at[pl.ds(half * count, count)])]
    pairs.append((away, out_ref.at[pl.ds((1 - half) * count, count)]))
    for copy in copies(pairs, sems):
        copy.wait()


def bins_kernel(micro, bins, a_ref, b_ref, gain_ref, shift_ref):
    extra = 4 * micro
    rows = joined_rows(a_ref[:extra]) + joined_rows(b_ref[:extra])
    gain_ref[...] = jnp.zeros_like(gain_ref)
    shift_ref[...] = jnp.zeros_like(shift_ref)
    for m in range(micro):
        gain_ref[bins[m]] += rows[m : m + 1]
        shift_ref[bins[m]] += rows[micro + m : micro + m + 1]


def spread_kernel(outer, part, *refs):
    chunk_refs = refs[-3 - outer : -3]
    out_ref, held, sems = refs[-3:]
    chunk = chunk_refs[0].shape[0]
    mine = lax.axis_index("bulk") // 2
    pairs = []
    for k in range(outer):
        held[k] = chunk_refs[k][...].astype(F32)
        start = pl.multiple_of(((mine ^ k) * PARTS + part) * chunk, 8)
        pairs.append((held.at[k], out_ref.at[pl.ds(start, chunk), :]))
    for copy in copies(pairs, sems):
        copy.wait()


def written(chunks, outer, part, before, rows):
    chunk, channels = chunks[0].shape
    hbm = pl.BlockSpec(memory_space=pltpu.HBM)
    return pl.pallas_call(
        functools.partial(spread_kernel, outer, part),
        in_specs=[hbm] * len(before) + [pl.BlockSpec(memory_space=pltpu.VMEM)] * outer,
        out_specs=hbm,
        out_shape=shape_of((rows, channels), F32),
        scratch_shapes=[
            pltpu.VMEM((outer, chunk, channels), F32),
            pltpu.SemaphoreType.DMA((outer,)),
        ],
        input_output_aliases={0: 0} if before else {},
        compiler_params=pltpu.CompilerParams(vmem_limit_bytes=4 << 20),
        cost_estimate=cost(1, 1 << 20),
        name="spread",
    )(*before, *chunks)


def shape_of(shape, dtype):
    return jax.ShapeDtypeStruct(shape, dtype)


def call(kernel, outs, args, scalars=(), remote=(), scratch=(), flops=1, limit=4):
    vmem = pl.BlockSpec(memory_space=pltpu.VMEM)
    smem = pl.BlockSpec(memory_space=pltpu.SMEM)
    kept = pl.BlockSpec(memory_space=pltpu.HBM)
    several = isinstance(outs, (list, tuple))
    return pl.pallas_call(
        kernel,
        in_specs=[smem] * len(scalars) + [kept] * len(remote) + [vmem] * len(args),
        out_specs=[vmem] * len(outs) if several else vmem,
        out_shape=outs,
        scratch_shapes=scratch,
        compiler_params=pltpu.CompilerParams(vmem_limit_bytes=limit << 20),
        cost_estimate=cost(flops, 1 << 20),
    )(*scalars, *[pltpu.with_memory_space_constraint(v, pltpu.HBM) for v in remote], *args)


def step(activations, weights, film_gain, film_shift, doa_bins, cotangent):
    sections = lax.axis_size("section")
    bulk_count = lax.axis_size("bulk")
    outer = bulk_count // 2
    x = activations[0]
    w_set = weights[0]
    micro, rows, channels = x.shape
    bins_count = film_gain.shape[1]
    gain_table = film_gain.reshape(bins_count, 1, channels)
    shift_table = film_shift.reshape(bins_count, 1, channels)
    pad = 16 * -(-(sections + 1) // 16)
    wide = rows + 2 * pad

    count = micro // 2
    edges = shape_of((micro + count, pad, channels), BF16)
    picked = shape_of((micro, 1, channels), F32)
    near, far, x, cot, w_set, gain_rows, shift_rows = call(
        load_kernel,
        [edges, edges, shape_of(x.shape, BF16), shape_of((count, rows, channels), BF16)]
        + [shape_of(w_set.shape, BF16), picked, picked],
        [],
        remote=[doa_bins, x, cotangent, w_set, gain_table, shift_table],
        scratch=[
            pltpu.SMEM(doa_bins.shape, jnp.int32),
            pltpu.VMEM(gain_table.shape, F32),
            pltpu.VMEM(shift_table.shape, F32),
            pltpu.SemaphoreType.DMA((6,)),
        ],
        limit=8,
    )
    opposite = [(i, (i + 1 if i % 2 else i - 1) % bulk_count) for i in range(bulk_count)]
    far = lax.ppermute(far, "bulk", opposite)
    near = lax.ppermute(near, "bulk", [(i, i ^ 1) for i in range(bulk_count)])

    matmul = 2 * 3 * micro * wide * channels * channels
    picked = shape_of((micro, 1, channels), F32)
    count = micro // 2
    half_main = shape_of((count, rows, channels), F32)
    half_main = shape_of((count, rows, channels), F32)
    send, keep, pre = call(
        forward_kernel,
        [half_main, half_main, shape_of(x.shape, F32)],
        [x, w_set, gain_rows, shift_rows],
        flops=matmul,
        limit=8,
    )

    def to_other(value):
        return lax.ppermute(value, "section", [(i, i ^ 1) for i in range(sections)])

    other_w = to_other(w_set)
    other = to_other(send)
    half_rim = shape_of((count, 2, 2 * pad, channels), F32)
    keep_rim, send_rim, pre_rim, g_rim = call(
        rim_kernel,
        [half_rim, half_rim]
        + [shape_of((micro, 2, 2 * pad, channels), F32), shape_of((count, 2, pad, channels), BF16)],
        [near, far, x, w_set, gain_rows, shift_rows],
        scratch=[pltpu.VMEM((2, *edges.shape), BF16)],
        flops=matmul // 4,
        limit=8,
    )
    other_rim = to_other(send_rim)
    tables = [keep, keep_rim, w_set, other, other_rim, other_w]

    half_wide = shape_of((count, wide, channels), BF16)
    hops = sections // 2 - 1
    cut = 8 * -(-sections // 8)
    inner_shape = shape_of((count, rows - 2 * cut, channels), BF16)
    outer_shape = shape_of((count, 2, 2 * cut, channels), BF16)

    def down(value, pair):
        pairs = [(2 * pair + c, 2 * pair - 2 + c) for c in range(2)]
        return lax.ppermute(value, "section", pairs + [(low, high) for high, low in pairs])

    sources = []
    for hop in range(hops):
        pair = hops - hop
        if hop:
            inner, outer_rows = call(
                functools.partial(relay_kernel, pair),
                [inner_shape, outer_shape],
                tables + sources[-2:],
                flops=matmul,
                limit=8,
            )
            sources += [down(inner, pair), down(outer_rows, pair)]
            continue
        inner = call(
            functools.partial(inner_kernel, pair),
            inner_shape,
            [keep, w_set, other, other_w, cot],
            flops=matmul,
            limit=8,
        )
        inner = down(inner, pair)
        outer_rows = call(
            functools.partial(outer_kernel, pair),
            outer_shape,
            [keep_rim, w_set, other_rim, other_w, cot, g_rim],
            flops=matmul // 2,
            limit=8,
        )
        outer_rows = down(outer_rows, pair)
        sources += [inner, outer_rows]
    grad_own, d_own, away = call(
        functools.partial(chain_kernel, hops),
        [
            half_wide,
            shape_of((count, rows, channels), BF16),
            shape_of((count, wide + rows, channels), BF16),
        ],
        tables + [cot, g_rim] + sources,
        scratch=[pltpu.VMEM(half_wide.shape, F32)],
        flops=matmul,
        limit=12,
    )
    got_away = to_other(away)
    shared = [x, pre, pre_rim, gain_rows]
    total_own, sums_own = call(
        own_kernel,
        [shape_of((3 * channels, channels), F32), shape_of((2 * micro, channels), F32)],
        shared + [grad_own],
        flops=matmul // 2,
        limit=8,
    )

    chunk = 3 * channels // outer // PARTS
    extra = 4 * micro
    messages = [shape_of((chunk + (0 if part else extra), channels), BF16) for part in range(PARTS)]
    made = call(
        functools.partial(last_kernel, outer),
        [shape_of((chunk, channels), F32)] * PARTS
        + [messages[part] for part in range(PARTS) for _ in range(outer - 1)],
        shared + [total_own, sums_own, got_away],
        scratch=[
            pltpu.VMEM((3 * channels, channels), F32),
            pltpu.VMEM((2 * micro, channels), F32),
        ],
        flops=matmul,
        limit=16,
    )
    owns = made[:PARTS]
    d_local = pl.pallas_call(
        result_kernel,
        in_specs=[pl.BlockSpec(memory_space=pltpu.VMEM)] * 2,
        out_specs=pl.BlockSpec(memory_space=pltpu.HBM),
        out_shape=shape_of(x.shape, BF16),
        scratch_shapes=[pltpu.SemaphoreType.DMA((2,))],
        compiler_params=pltpu.CompilerParams(vmem_limit_bytes=4 << 20),
        cost_estimate=cost(1, 1 << 20),
        name="results",
    )(d_own, got_away)

    def across(value, k):
        pairs = [(i, i ^ (2 * k)) for i in range(bulk_count)]
        return lax.ppermute(value, "bulk", pairs)

    swap = [(i, i ^ 1) for i in range(bulk_count)]
    order = [k for k in range(2, outer)] + [1]
    scattered = []
    for part in range(PARTS):
        sends = made[PARTS + part * (outer - 1) :][: outer - 1]
        got = {k: across(sends[k - 1], k) for k in order}
        scattered.append((sends[0], got))
    summed = []
    for part in range(PARTS):
        first, got = scattered[part]
        partial_sum = call(
            functools.partial(gather_kernel, outer),
            messages[part],
            [owns[part], first] + [got[k] for k in range(1, outer)],
            scratch=[pltpu.VMEM((outer, 2 * micro, channels), F32)],
        )
        summed.append((partial_sum, lax.ppermute(partial_sum, "bulk", swap)))
    spread = []
    for part in range(PARTS):
        done = call(
            pair_kernel, shape_of((chunk, channels), BF16), list(summed[part]) + spread[-outer:][:1]
        )
        got = {k: across(done, k) for k in order}
        spread += [done] + [got[k] for k in range(1, outer)]
    table = shape_of((bins_count, 1, channels), F32)
    d_gain, d_shift = call(
        functools.partial(bins_kernel, micro), [table, table], list(summed[0]), scalars=[doa_bins]
    )
    before = []
    for part in range(PARTS):
        chunks = spread[part * outer : (part + 1) * outer]
        before = [written(chunks, outer, part, before, 3 * channels)]
    d_weights = before[0]
    return (
        d_local[None],
        d_weights.reshape(1, 3, channels, channels),
        d_gain.reshape(1, bins_count, channels),
        d_shift.reshape(1, bins_count, channels),
    )


def solution(mesh):
    return jax.shard_map(
        step,
        mesh=mesh,
        in_specs=(
            P("section", None, "bulk", None),
            P("section", None, None, None),
            P("section", None, None),
            P("section", None, None),
            P(),
            P(None, "bulk", None),
        ),
        out_specs=(
            P("section", None, "bulk", None),
            P("section", None, None, None),
            P("section", None, None),
            P("section", None, None),
        ),
        check_vma=False,
    )
```

```python
import functools

import jax
import jax.numpy as jnp
from jax import lax
from jax.experimental import pallas as pl
from jax.experimental.pallas import tpu as pltpu
from jax.sharding import PartitionSpec as P


F32 = jnp.float32
BF16 = jnp.bfloat16
PARTS = 2


def cost(flops, moved, trans=0):
    return pl.CostEstimate(flops=flops, bytes_accessed=moved, transcendentals=trans)


def shifted(value, amount):
    rows = value.shape[0]
    return pltpu.roll(value, amount % rows, 0)


def copies(pairs, sems):
    started = []
    for index, (source, target) in enumerate(pairs):
        copy = pltpu.make_async_copy(source, target, sems.at[index])
        copy.start()
        started.append(copy)
    return started


def load_kernel(bins_in, x_in, cot_in, w_in, gain_in, shift_in, *refs):
    near_ref, far_ref, x_ref, cot_ref, w_ref, gain_ref, shift_ref = refs[:7]
    bins, gains, shifts, sems = refs[7:]
    micro, rows = x_ref.shape[:2]
    count = micro // 2
    pad = near_ref.shape[1]
    odd = lax.axis_index("bulk") % 2
    mine = cot_in.at[pl.ds(lax.axis_index("section") % 2 * count, count)]
    pairs = [(x_in, x_ref), (mine, cot_ref), (bins_in, bins), (gain_in, gains)]
    started = copies(pairs + [(shift_in, shifts), (w_in, w_ref)], sems)
    for copy in started[:2]:
        copy.wait()
    near = pl.multiple_of((1 - odd) * (rows - pad), pad)
    far = pl.multiple_of(odd * (rows - pad), pad)
    for out, start in ((near_ref, near), (far_ref, far)):
        out[:micro] = x_ref[:, pl.ds(start, pad), :]
        out[micro:] = cot_ref[:, pl.ds(start, pad), :]
    for copy in started[2:]:
        copy.wait()
    for m in range(micro):
        gain_ref[m] = gains[bins[m]]
        shift_ref[m] = shifts[bins[m]]


def slopes(filmed):
    sig = 0.5 * jnp.tanh(0.5 * filmed) + 0.5
    return sig * (1.0 + filmed * (1.0 - sig))


def taps(value, w_ref):
    wide = value.astype(F32)
    pre = jnp.dot(shifted(wide, 1).astype(BF16), w_ref[0], preferred_element_type=F32)
    pre = pre + jnp.dot(value, w_ref[1], preferred_element_type=F32)
    return pre + jnp.dot(shifted(wide, -1).astype(BF16), w_ref[2], preferred_element_type=F32)


def turn(half, micro, place):
    start = half if place == 0 else 1 - half
    return [start * (micro // 2) + j for j in range(micro // 2)]


def forward_kernel(x_ref, w_ref, gain_ref, shift_ref, send_ref, keep_ref, pre_ref):
    micro = x_ref.shape[0]
    half = lax.axis_index("section") % 2
    for place, out in ((1, send_ref), (0, keep_ref)):
        for j, m in enumerate(turn(half, micro, place)):
            pre = taps(x_ref[m], w_ref)
            out[j] = slopes(pre * gain_ref[m] + shift_ref[m]) * gain_ref[m]
            pre_ref[m] = pre


def rim_kernel(near_ref, far_ref, x_ref, w_ref, gain_ref, shift_ref, *refs):
    keep_ref, send_ref, pre_ref, g_ref, halo = refs
    micro, rows = x_ref.shape[:2]
    pad = near_ref.shape[1]
    odd = lax.axis_index("bulk") % 2
    half = lax.axis_index("section") % 2

    @pl.when(odd == 1)
    def _():
        halo[0] = near_ref[...]
        halo[1] = far_ref[...]

    @pl.when(odd == 0)
    def _():
        halo[0] = far_ref[...]
        halo[1] = near_ref[...]

    parts = []
    order = turn(half, micro, 0) + turn(half, micro, 1)
    for m in order:
        parts += [halo[0, m], x_ref[m, :pad], x_ref[m, rows - pad :], halo[1, m]]
    for j in range(micro // 2):
        g_ref[j, 0] = halo[0, micro + j]
        g_ref[j, 1] = halo[1, micro + j]
    pre = taps(jnp.concatenate(parts, axis=0), w_ref)
    for index, m in enumerate(order):
        out = (keep_ref, send_ref)[index // (micro // 2)]
        for side in range(2):
            start = (2 * index + side) * 2 * pad
            here = pre[start : start + 2 * pad]
            pre_ref[m, side] = here
            filmed = here * gain_ref[m] + shift_ref[m]
            out[index % (micro // 2), side] = slopes(filmed) * gain_ref[m]


def with_rim(main, rim, m):
    pad = rim.shape[2] // 2
    rows = main.shape[1]
    parts = [rim[m, 0, : pad + 8], main[m, 8 : rows - 8], rim[m, 1, pad - 8 :]]
    return jnp.concatenate(parts, axis=0)


def times_trans(left, right):
    return lax.dot_general(left, right, (((1,), (1,)), ((), ())), preferred_element_type=F32)


def trans_times(left, right):
    return lax.dot_general(left, right, (((0,), (0,)), ((), ())), preferred_element_type=F32)


def both_sides(grad_pre):
    wide = grad_pre.astype(F32)
    return shifted(wide, -1).astype(BF16), shifted(wide, 1).astype(BF16)


def backward(g, slope, w_ref):
    grad_pre = (g * slope).astype(BF16)
    later, earlier = both_sides(grad_pre)
    d_in = g + times_trans(later, w_ref[0]) + times_trans(grad_pre, w_ref[1])
    d_in = d_in + times_trans(earlier, w_ref[2])
    return grad_pre, d_in.astype(BF16), d_in


def top_gradient(cot_ref, rim_ref, m):
    return jnp.concatenate([rim_ref[m, 0], cot_ref[m], rim_ref[m, 1]], axis=0)


def factors(refs, j):
    main, rim, w_ref = refs
    return with_rim(main, rim, j), w_ref


def by_half(pair, own, other, run):
    section_id = lax.axis_index("section")
    for half in range(2):
        upper, lower = (own, other) if half else (other, own)
        here = section_id % 2 == half if pair is None else section_id == 2 * pair + half

        @pl.when(here)
        def _(upper=upper, lower=lower, half=half):
            run(upper, lower, half)


def inner_kernel(pair, *refs):
    own, other, cot_ref, d_ref = refs[:2], refs[2:4], refs[4], refs[5]
    rows = cot_ref.shape[1]
    cut = (rows - d_ref.shape[1]) // 2

    def run(upper, lower, half):
        for j in range(d_ref.shape[0]):
            g = cot_ref[j].astype(F32)
            middle = backward(g, upper[0][j], upper[1])[1].astype(F32)
            d_ref[j] = backward(middle, lower[0][j], lower[1])[2][cut : rows - cut].astype(BF16)

    by_half(pair, own, other, run)


def outer_kernel(pair, *refs):
    own, other, cot_ref, rim_ref, d_ref = refs[:2], refs[2:4], refs[4], refs[5], refs[6]
    count, rows = cot_ref.shape[:2]
    pad = rim_ref.shape[2]
    cut = d_ref.shape[2] // 2

    def stacked(ref):
        return jnp.concatenate([ref[j, side] for j in range(count) for side in range(2)], axis=0)

    def run(upper, lower, half):
        parts = []
        for j in range(count):
            parts += [rim_ref[j, 0], cot_ref[j, :pad], cot_ref[j, rows - pad :], rim_ref[j, 1]]
        g = jnp.concatenate(parts, axis=0).astype(F32)
        middle = backward(g, stacked(upper[0]), upper[1])[1].astype(F32)
        d_in = backward(middle, stacked(lower[0]), lower[1])[2]
        for j in range(count):
            for side in range(2):
                start = (2 * j + side) * 2 * pad + pad - cut
                d_ref[j, side] = d_in[start : start + 2 * cut].astype(BF16)

    by_half(pair, own, other, run)


def arrived(inner_ref, outer_ref, j, wide):
    rest = wide - inner_ref.shape[1] - 2 * outer_ref.shape[2]
    fill = jnp.zeros((rest // 2, inner_ref.shape[2]), F32)
    parts = [outer_ref[j, 0], inner_ref[j], outer_ref[j, 1]]
    return jnp.concatenate([fill] + [part.astype(F32) for part in parts] + [fill], axis=0)


def relay_kernel(pair, *refs):
    own, other, got_refs = refs[:3], refs[3:6], refs[6:8]
    inner_ref, outer_ref = refs[8:]
    cut = outer_ref.shape[2] // 2
    size = inner_ref.shape[1]
    wide = own[0].shape[1] + own[1].shape[2]

    def run(upper, lower, half):
        for j in range(inner_ref.shape[0]):
            g = arrived(*got_refs, j, wide)
            middle = backward(g, *factors(upper, j))[1].astype(F32)
            d_in = backward(middle, *factors(lower, j))[2]
            start = (wide - size) // 2
            inner_ref[j] = d_in[start : start + size].astype(BF16)
            outer_ref[j, 0] = d_in[start - 2 * cut : start].astype(BF16)
            outer_ref[j, 1] = d_in[start + size : start + size + 2 * cut].astype(BF16)

    by_half(pair, own, other, run)


def chain_kernel(hops, *refs):
    own, other, top_refs = refs[:3], refs[3:6], refs[6:8]
    got_refs = refs[8 : 8 + 2 * hops]
    grad_ref, d_ref, send_ref, send_d, g_now = refs[8 + 2 * hops :]
    rows, wide = d_ref.shape[1], grad_ref.shape[1]
    pad = (wide - rows) // 2
    inner = slice(pad, pad + rows)
    section_id = lax.axis_index("section")

    @pl.when(section_id // 2 == hops)
    def _():
        for j in range(d_ref.shape[0]):
            g_now[j] = top_gradient(*top_refs, j).astype(F32)

    for index in range(hops):

        @pl.when(section_id // 2 == hops - 1 - index)
        def _(index=index):
            for j in range(d_ref.shape[0]):
                g_now[j] = arrived(*got_refs[2 * index : 2 * index + 2], j, wide)

    def run(upper, lower, half):
        for j in range(d_ref.shape[0]):
            first = backward(g_now[j], *factors(upper, j))
            second = backward(first[1].astype(F32), *factors(lower, j))
            mine, away = (first, second) if half else (second, first)
            grad_ref[j] = mine[0]
            d_ref[j] = mine[1][inner]
            send_ref[j] = away[0]
            send_d[j] = away[1][inner]

    by_half(None, own, other, run)


def split_rows(rows):
    high = rows.astype(BF16).astype(F32)
    low = (rows - high).astype(BF16).astype(F32)
    return jnp.concatenate([high, low], axis=0).astype(BF16)


def joined_rows(pair):
    wide = pair.astype(F32)
    half = wide.shape[0] // 2
    return wide[:half] + wide[half:]


def add_terms(place, source, wide, x_ref, pre_ref, pre_rim, gain_ref, total, sums, start=None):
    micro, rows, channels = x_ref.shape
    pad = (wide - rows) // 2
    inner = slice(pad, pad + rows)
    half = lax.axis_index("section") % 2
    for j, m in enumerate(turn(half, micro, place)):
        grad_pre = source[j, :wide]
        later, earlier = both_sides(grad_pre)
        for tap, side in enumerate((later, grad_pre, earlier)):
            where = slice(tap * channels, (tap + 1) * channels)
            term = trans_times(x_ref[m], side[inner])
            if j:
                term = total[where] + term
            elif start is not None:
                term = start[where] + term
            total[where] = term
        film = grad_pre[inner].astype(F32)
        pre = with_rim(pre_ref, pre_rim, m)[inner]
        scale = 1.0 / gain_ref[m]
        sums[pl.ds(m, 1)] = scale * jnp.sum(film * pre, axis=0, keepdims=True)
        sums[pl.ds(micro + m, 1)] = scale * jnp.sum(film, axis=0, keepdims=True)


def own_kernel(x_ref, pre_ref, pre_rim, gain_ref, grad_ref, total, sums):
    sums[...] = jnp.zeros_like(sums)
    wide = grad_ref.shape[1]
    add_terms(0, grad_ref, wide, x_ref, pre_ref, pre_rim, gain_ref, total, sums)


def last_kernel(outer, *refs):
    x_ref, pre_ref, pre_rim, gain_ref, total_in, sums_in, got_ref = refs[:7]
    own_refs = refs[7 : 7 + PARTS]
    send_refs = refs[7 + PARTS : -2]
    total, sums = refs[-2:]
    wide = got_ref.shape[1]
    mine = lax.axis_index("bulk") // 2
    sums[...] = sums_in[...]
    add_terms(1, got_ref, wide, x_ref, pre_ref, pre_rim, gain_ref, total, sums, total_in)
    rows_out = split_rows(sums[...])
    extra = rows_out.shape[0]
    chunk = own_refs[0].shape[0]
    parts_count = len(own_refs)
    for part in range(parts_count):
        for k in range(outer):
            start = pl.multiple_of(((mine ^ k) * parts_count + part) * chunk, 8)
            term = total[pl.ds(start, chunk), :]
            if k == 0:
                own_refs[part][...] = term
            else:
                ref = send_refs[part * (outer - 1) + k - 1]
                ref[ref.shape[0] - chunk :] = term.astype(BF16)
                if part == 0:
                    ref[:extra] = rows_out


def gather_kernel(outer, own_ref, mine_ref, *refs):
    got_refs = refs[: outer - 1]
    out_ref, held = refs[outer - 1 :]
    mine = lax.axis_index("bulk") // 2
    chunk = own_ref.shape[0]
    extra = out_ref.shape[0] - chunk
    acc = own_ref[...]
    for k in range(1, outer):
        acc = acc + got_refs[k - 1][extra:].astype(F32)
    out_ref[extra:] = acc.astype(BF16)
    if extra:
        held[mine] = joined_rows(mine_ref[:extra])
        for k in range(1, outer):
            held[mine ^ k] = joined_rows(got_refs[k - 1][:extra])
        rows = held[0]
        for index in range(1, outer):
            rows = rows + held[index]
        out_ref[:extra] = split_rows(rows)


def pair_kernel(a_ref, b_ref, *refs):
    out_ref = refs[-1]
    extra = a_ref.shape[0] - out_ref.shape[0]
    out_ref[...] = (a_ref[extra:].astype(F32) + b_ref[extra:].astype(F32)).astype(BF16)


def result_kernel(d_mine, got_ref, out_ref, sems):
    count = d_mine.shape[0]
    half = lax.axis_index("section") % 2
    pairs = [(d_mine, out_ref.at[pl.ds(half * count, count)])]
    pairs.append((got_ref, out_ref.at[pl.ds((1 - half) * count, count)]))
    for copy in copies(pairs, sems):
        copy.wait()


def bins_kernel(micro, bins, a_ref, b_ref, gain_ref, shift_ref):
    extra = 4 * micro
    rows = joined_rows(a_ref[:extra]) + joined_rows(b_ref[:extra])
    gain_ref[...] = jnp.zeros_like(gain_ref)
    shift_ref[...] = jnp.zeros_like(shift_ref)
    for m in range(micro):
        gain_ref[bins[m]] += rows[m : m + 1]
        shift_ref[bins[m]] += rows[micro + m : micro + m + 1]


def spread_kernel(outer, part, *refs):
    chunk_refs = refs[-3 - outer : -3]
    out_ref, held, sems = refs[-3:]
    chunk = chunk_refs[0].shape[0]
    mine = lax.axis_index("bulk") // 2
    pairs = []
    for k in range(outer):
        held[k] = chunk_refs[k][...].astype(F32)
        start = pl.multiple_of(((mine ^ k) * PARTS + part) * chunk, 8)
        pairs.append((held.at[k], out_ref.at[pl.ds(start, chunk), :]))
    for copy in copies(pairs, sems):
        copy.wait()


def written(chunks, outer, part, before, rows):
    chunk, channels = chunks[0].shape
    hbm = pl.BlockSpec(memory_space=pltpu.HBM)
    return pl.pallas_call(
        functools.partial(spread_kernel, outer, part),
        in_specs=[hbm] * len(before) + [pl.BlockSpec(memory_space=pltpu.VMEM)] * outer,
        out_specs=hbm,
        out_shape=shape_of((rows, channels), F32),
        scratch_shapes=[
            pltpu.VMEM((outer, chunk, channels), F32),
            pltpu.SemaphoreType.DMA((outer,)),
        ],
        input_output_aliases={0: 0} if before else {},
        compiler_params=pltpu.CompilerParams(vmem_limit_bytes=4 << 20),
        cost_estimate=cost(1, 1 << 20),
        name="spread",
    )(*before, *chunks)


def shape_of(shape, dtype):
    return jax.ShapeDtypeStruct(shape, dtype)


def call(kernel, outs, args, scalars=(), remote=(), scratch=(), flops=1, limit=4):
    vmem = pl.BlockSpec(memory_space=pltpu.VMEM)
    smem = pl.BlockSpec(memory_space=pltpu.SMEM)
    kept = pl.BlockSpec(memory_space=pltpu.HBM)
    several = isinstance(outs, (list, tuple))
    return pl.pallas_call(
        kernel,
        in_specs=[smem] * len(scalars) + [kept] * len(remote) + [vmem] * len(args),
        out_specs=[vmem] * len(outs) if several else vmem,
        out_shape=outs,
        scratch_shapes=scratch,
        compiler_params=pltpu.CompilerParams(vmem_limit_bytes=limit << 20),
        cost_estimate=cost(flops, 1 << 20),
    )(*scalars, *[pltpu.with_memory_space_constraint(v, pltpu.HBM) for v in remote], *args)


def step(activations, weights, film_gain, film_shift, doa_bins, cotangent):
    sections = lax.axis_size("section")
    bulk_count = lax.axis_size("bulk")
    outer = bulk_count // 2
    x = activations[0]
    w_set = weights[0]
    micro, rows, channels = x.shape
    bins_count = film_gain.shape[1]
    gain_table = film_gain.reshape(bins_count, 1, channels)
    shift_table = film_shift.reshape(bins_count, 1, channels)
    pad = 16 * -(-(sections + 1) // 16)
    wide = rows + 2 * pad

    count = micro // 2
    edges = shape_of((micro + count, pad, channels), BF16)
    picked = shape_of((micro, 1, channels), F32)
    near, far, x, cot, w_set, gain_rows, shift_rows = call(
        load_kernel,
        [edges, edges, shape_of(x.shape, BF16), shape_of((count, rows, channels), BF16)]
        + [shape_of(w_set.shape, BF16), picked, picked],
        [],
        remote=[doa_bins, x, cotangent, w_set, gain_table, shift_table],
        scratch=[
            pltpu.SMEM(doa_bins.shape, jnp.int32),
            pltpu.VMEM(gain_table.shape, F32),
            pltpu.VMEM(shift_table.shape, F32),
            pltpu.SemaphoreType.DMA((6,)),
        ],
        limit=8,
    )
    opposite = [(i, (i + 1 if i % 2 else i - 1) % bulk_count) for i in range(bulk_count)]
    far = lax.ppermute(far, "bulk", opposite)
    near = lax.ppermute(near, "bulk", [(i, i ^ 1) for i in range(bulk_count)])

    matmul = 2 * 3 * micro * wide * channels * channels
    picked = shape_of((micro, 1, channels), F32)
    count = micro // 2
    half_main = shape_of((count, rows, channels), F32)
    half_main = shape_of((count, rows, channels), F32)
    send, keep, pre = call(
        forward_kernel,
        [half_main, half_main, shape_of(x.shape, F32)],
        [x, w_set, gain_rows, shift_rows],
        flops=matmul,
        limit=8,
    )

    def to_other(value):
        return lax.ppermute(value, "section", [(i, i ^ 1) for i in range(sections)])

    other_w = to_other(w_set)
    other = to_other(send)
    half_rim = shape_of((count, 2, 2 * pad, channels), F32)
    keep_rim, send_rim, pre_rim, g_rim = call(
        rim_kernel,
        [half_rim, half_rim]
        + [shape_of((micro, 2, 2 * pad, channels), F32), shape_of((count, 2, pad, channels), BF16)],
        [near, far, x, w_set, gain_rows, shift_rows],
        scratch=[pltpu.VMEM((2, *edges.shape), BF16)],
        flops=matmul // 4,
        limit=8,
    )
    other_rim = to_other(send_rim)
    tables = [keep, keep_rim, w_set, other, other_rim, other_w]

    half_wide = shape_of((count, wide, channels), BF16)
    hops = sections // 2 - 1
    cut = 8 * -(-sections // 8)
    inner_shape = shape_of((count, rows - 2 * cut, channels), BF16)
    outer_shape = shape_of((count, 2, 2 * cut, channels), BF16)

    def down(value, pair):
        pairs = [(2 * pair + c, 2 * pair - 2 + c) for c in range(2)]
        return lax.ppermute(value, "section", pairs + [(low, high) for high, low in pairs])

    sources = []
    for hop in range(hops):
        pair = hops - hop
        if hop:
            inner, outer_rows = call(
                functools.partial(relay_kernel, pair),
                [inner_shape, outer_shape],
                tables + sources[-2:],
                flops=matmul,
                limit=8,
            )
            sources += [down(inner, pair), down(outer_rows, pair)]
            continue
        inner = call(
            functools.partial(inner_kernel, pair),
            inner_shape,
            [keep, w_set, other, other_w, cot],
            flops=matmul,
            limit=8,
        )
        inner = down(inner, pair)
        outer_rows = call(
            functools.partial(outer_kernel, pair),
            outer_shape,
            [keep_rim, w_set, other_rim, other_w, cot, g_rim],
            flops=matmul // 2,
            limit=8,
        )
        outer_rows = down(outer_rows, pair)
        sources += [inner, outer_rows]
    grad_own, d_own, away, away_d = call(
        functools.partial(chain_kernel, hops),
        [
            half_wide,
            shape_of((count, rows, channels), BF16),
            half_wide,
            shape_of((count, rows, channels), BF16),
        ],
        tables + [cot, g_rim] + sources,
        scratch=[pltpu.VMEM(half_wide.shape, F32)],
        flops=matmul,
        limit=12,
    )
    got_away = to_other(away)
    got_d = to_other(away_d)
    shared = [x, pre, pre_rim, gain_rows]
    total_own, sums_own = call(
        own_kernel,
        [shape_of((3 * channels, channels), F32), shape_of((2 * micro, channels), F32)],
        shared + [grad_own],
        flops=matmul // 2,
        limit=8,
    )

    chunk = 3 * channels // outer // PARTS
    extra = 4 * micro
    messages = [shape_of((chunk + (0 if part else extra), channels), BF16) for part in range(PARTS)]
    made = call(
        functools.partial(last_kernel, outer),
        [shape_of((chunk, channels), F32)] * PARTS
        + [messages[part] for part in range(PARTS) for _ in range(outer - 1)],
        shared + [total_own, sums_own, got_away],
        scratch=[
            pltpu.VMEM((3 * channels, channels), F32),
            pltpu.VMEM((2 * micro, channels), F32),
        ],
        flops=matmul,
        limit=16,
    )
    owns = made[:PARTS]
    d_local = pl.pallas_call(
        result_kernel,
        in_specs=[pl.BlockSpec(memory_space=pltpu.VMEM)] * 2,
        out_specs=pl.BlockSpec(memory_space=pltpu.HBM),
        out_shape=shape_of(x.shape, BF16),
        scratch_shapes=[pltpu.SemaphoreType.DMA((2,))],
        compiler_params=pltpu.CompilerParams(vmem_limit_bytes=4 << 20),
        cost_estimate=cost(1, 1 << 20),
        name="results",
    )(d_own, got_d)

    def across(value, k):
        pairs = [(i, i ^ (2 * k)) for i in range(bulk_count)]
        return lax.ppermute(value, "bulk", pairs)

    swap = [(i, i ^ 1) for i in range(bulk_count)]
    order = [k for k in range(2, outer)] + [1]
    scattered = []
    for part in range(PARTS):
        sends = made[PARTS + part * (outer - 1) :][: outer - 1]
        got = {k: across(sends[k - 1], k) for k in order}
        scattered.append((sends[0], got))
    summed = []
    for part in range(PARTS):
        first, got = scattered[part]
        partial_sum = call(
            functools.partial(gather_kernel, outer),
            messages[part],
            [owns[part], first] + [got[k] for k in range(1, outer)],
            scratch=[pltpu.VMEM((outer, 2 * micro, channels), F32)],
        )
        summed.append((partial_sum, lax.ppermute(partial_sum, "bulk", swap)))
    spread = []
    for part in range(PARTS):
        done = call(
            pair_kernel, shape_of((chunk, channels), BF16), list(summed[part]) + spread[-outer:][:1]
        )
        got = {k: across(done, k) for k in order}
        spread += [done] + [got[k] for k in range(1, outer)]
    table = shape_of((bins_count, 1, channels), F32)
    d_gain, d_shift = call(
        functools.partial(bins_kernel, micro), [table, table], list(summed[0]), scalars=[doa_bins]
    )
    before = []
    for part in range(PARTS):
        chunks = spread[part * outer : (part + 1) * outer]
        before = [written(chunks, outer, part, before, 3 * channels)]
    d_weights = before[0]
    return (
        d_local[None],
        d_weights.reshape(1, 3, channels, channels),
        d_gain.reshape(1, bins_count, channels),
        d_shift.reshape(1, bins_count, channels),
    )


def solution(mesh):
    return jax.shard_map(
        step,
        mesh=mesh,
        in_specs=(
            P("section", None, "bulk", None),
            P("section", None, None, None),
            P("section", None, None),
            P("section", None, None),
            P(),
            P(None, "bulk", None),
        ),
        out_specs=(
            P("section", None, "bulk", None),
            P("section", None, None, None),
            P("section", None, None),
            P("section", None, None),
        ),
        check_vma=False,
    )
```
